32 devices in a mesh: ha: 4 (over y, x), ba: 8 (over z, core).
Axes of the slice: x: 2, y: 2, z: 4, core: 2. Of those that a mesh axis runs over, the one named last changes fastest.
Arguments:
- images_in: bfloat16 [64, 32, 32, 1024], P('ba', 'ha'), may hold values from -6 to 6
- reduce_w: bfloat16 [1024, 1024], replicated, may hold values from -0.1875 to 0.1875
- gain_one: float32 [1024], replicated, may hold values from 0.1 to 1.9
- shift_one: float32 [1024], replicated, may hold values from -2 to 2
- group_w: bfloat16 [3, 3, 32, 1024], replicated, may hold values from -0.375 to 0.375
- gain_two: float32 [1024], replicated, may hold values from 0.1 to 1.9
- shift_two: float32 [1024], replicated, may hold values from -2 to 2
- expand_w: bfloat16 [1024, 2048], replicated, may hold values from -0.1875 to 0.1875
- gain_three: float32 [2048], replicated, may hold values from 0.1 to 1.9
- shift_three: float32 [2048], replicated, may hold values from -2 to 2
- proj_w: bfloat16 [1024, 2048], replicated, may hold values from -0.1875 to 0.1875
- gain_proj: float32 [2048], replicated, may hold values from 0.1 to 1.9
- shift_proj: float32 [2048], replicated, may hold values from -2 to 2
- valid_mask: int32 [64], P('ba'), may hold values from 0 to 1, as said below
- cotangent: bfloat16 [64, 16, 16, 2048], P('ba', 'ha'), may hold values from -6 to 6
Outputs:
- output: bfloat16 [64, 16, 16, 2048], P('ba', 'ha')
- grad_images: bfloat16 [64, 32, 32, 1024], P('ba', 'ha')
- grad_reduce: float32 [1024, 1024], replicated
- grad_gain_one: float32 [1024], replicated
- grad_shift_one: float32 [1024], replicated
- grad_group: float32 [3, 3, 32, 1024], replicated
- grad_gain_two: float32 [1024], replicated
- grad_shift_two: float32 [1024], replicated
- grad_expand: float32 [1024, 2048], replicated
- grad_gain_three: float32 [2048], replicated
- grad_shift_three: float32 [2048], replicated
- grad_proj: float32 [1024, 2048], replicated
- grad_gain_proj: float32 [2048], replicated
- grad_shift_proj: float32 [2048], replicated
The draws below stay inside these ranges and needn't reach their ends.
Inputs may be any that keep to these rules, and one draw needn't show every extreme that they name: `valid_mask`: in each aligned block of 8 images (the images of one index of ba) the valid images come first; a block holds 8, 4, 2 or 1 valid images, and at least one block holds 8.
All inputs are finite; a program needn't handle non-finite values.
Results may differ from the reference program's by a relative error of at most 0.0087.
Values may be sent and summed in bfloat16 or wider, within the bound.
No kernel may reach another device: no remote copies, remote signals or barrier semaphores. Data moves between devices by JAX's collectives and lax.ppermute only.
A program may use at most 256 MiB of HBM per device.

```python
import jax
import jax.numpy as jnp
from jax import lax

CIN = 1024
GROUPS = 32
GW = 32
COUT = 2048
MID = 1024
B_DEV = 8
WO = 16
IMAGES = 64
HO = 16
HI = 32
WI = 32


def draw_valid_mask(key, part):
    blocks = IMAGES // B_DEV
    levels = jax.random.randint(jax.random.fold_in(key, 11), (blocks,), 0, 4)
    chosen = jax.random.randint(jax.random.fold_in(key, 12), (), 0, blocks)
    levels = jnp.where(jnp.arange(blocks) == chosen, 0, levels)
    counts = jnp.maximum(jnp.right_shift(jnp.full((blocks,), B_DEV, jnp.int32), levels), 1)
    slots = jnp.arange(B_DEV, dtype=jnp.int32)
    return (slots[None, :] < counts[:, None]).astype(jnp.int32).reshape(-1)


def block_scale(own_key, shape, cuts, least, high):
    factor_of = 1.0
    for axis_at, shards_of in cuts:
        heights = jax.random.uniform(jax.random.fold_in(jax.random.fold_in(own_key, 6), axis_at), (shards_of,), jnp.float32, least / len(cuts), high / len(cuts))
        factor_of = factor_of * jnp.repeat(jnp.exp(heights), shape[axis_at] // shards_of).reshape((-1,) + (1,) * (len(shape) - 1 - axis_at))
    return factor_of


def scatter_about(stream_key, shape, scale, reach, split=(), kind=jnp.bfloat16):
    array = jax.random.normal(stream_key, shape, jnp.float32) * scale
    if len(split) > 0:
        array = block_scale(stream_key, shape, split, -0.22, 0.18) * array
    return jnp.clip(array, min=-reach, max=reach).astype(kind)


def setup_inputs(seed: int = 0) -> dict:
    streams_of = jax.random.split(jax.random.key(seed), 16)
    return {
        "images_in": scatter_about(streams_of[0], (IMAGES, HI, WI, CIN), 1.0, 6.0, ((0, 8), (1, 4))),
        "reduce_w": scatter_about(streams_of[1], (CIN, MID), CIN ** -0.5, 0.1875),
        "gain_one": jnp.clip(1.0 + 0.18 * jax.random.normal(streams_of[2], (MID,), jnp.float32), 0.1, 1.9),
        "shift_one": scatter_about(streams_of[3], (MID,), 0.3, 2.0, (), jnp.float32),
        "group_w": scatter_about(streams_of[4], (3, 3, GW, MID), (9 * GW) ** -0.5, 0.375),
        "gain_two": jnp.clip(1.0 + 0.18 * jax.random.normal(streams_of[5], (MID,), jnp.float32), 0.1, 1.9),
        "shift_two": scatter_about(streams_of[6], (MID,), 0.3, 2.0, (), jnp.float32),
        "expand_w": scatter_about(streams_of[7], (MID, COUT), MID ** -0.5, 0.1875),
        "gain_three": jnp.clip(1.0 + 0.18 * jax.random.normal(streams_of[8], (COUT,), jnp.float32), 0.1, 1.9),
        "shift_three": scatter_about(streams_of[9], (COUT,), 0.3, 2.0, (), jnp.float32),
        "proj_w": scatter_about(streams_of[10], (CIN, COUT), CIN ** -0.5, 0.1875),
        "gain_proj": jnp.clip(1.0 + 0.18 * jax.random.normal(streams_of[11], (COUT,), jnp.float32), 0.1, 1.9),
        "shift_proj": scatter_about(streams_of[12], (COUT,), 0.3, 2.0, (), jnp.float32),
        "valid_mask": draw_valid_mask(jax.random.fold_in(streams_of[15], 71), 0),
        "cotangent": scatter_about(streams_of[14], (IMAGES, HO, WO, COUT), 1.0, 6.0, ((0, 8), (1, 4))),
    }


EPS = 1e-05

@jax.custom_vjp
def low(v):
    return lax.optimization_barrier(v.astype(jnp.bfloat16)).astype(jnp.float32)

@jax.custom_vjp
def low_back(v):
    return v

def low_keep(v):
    return (low(v), None)

def low_pass(kept, grad):
    return (grad,)

def back_keep(v):
    return (v, None)

def back_low(kept, grad):
    return (low(grad),)
low.defvjp(low_keep, low_pass)
low_back.defvjp(back_keep, back_low)

def normalize(activation, weight, count_of, gain_vec, shift_vec):
    mean_of = lax.optimization_barrier(jnp.sum(activation * weight, axis=(0, 1, 2))) / count_of
    centred = activation - mean_of
    variance = lax.optimization_barrier(jnp.sum(centred * centred * weight, axis=(0, 1, 2))) / count_of
    return centred * lax.rsqrt(variance + EPS) * gain_vec + shift_vec

def forward(images_in, reduce_w, gain_one, shift_one, group_w, gain_two, shift_two, expand_w, gain_three, shift_three, proj_w, gain_proj, shift_proj, weight):
    highest = lax.Precision.HIGHEST
    count_in = jnp.sum(weight) * (HI * WI)
    count_out = jnp.sum(weight) * (HO * WO)
    reduced = low_back(jnp.einsum('nhwc,cd->nhwd', images_in, reduce_w, precision=highest))
    hidden_one = low(jax.nn.silu(normalize(reduced, weight, count_in, gain_one, shift_one)))
    grouped = low_back(lax.conv_general_dilated(hidden_one, group_w, (2, 2), ((1, 1), (1, 1)), dimension_numbers=('NHWC', 'HWIO', 'NHWC'), feature_group_count=GROUPS, precision=highest))
    hidden_two = low(jax.nn.silu(normalize(grouped, weight, count_out, gain_two, shift_two)))
    expanded = low_back(jnp.einsum('nhwc,cd->nhwd', hidden_two, expand_w, precision=highest))
    sampled = images_in[:, ::2, ::2]
    projected = low_back(jnp.einsum('nhwc,cd->nhwd', sampled, proj_w, precision=highest))
    summed = normalize(expanded, weight, count_out, gain_three, shift_three) + normalize(projected, weight, count_out, gain_proj, shift_proj)
    return jax.nn.silu(summed) * weight

def reference(images_in, reduce_w, gain_one, shift_one, group_w, gain_two, shift_two, expand_w, gain_three, shift_three, proj_w, gain_proj, shift_proj, valid_mask, cotangent):
    weight = valid_mask.astype(jnp.float32)[:, None, None, None]
    primals = (images_in.astype(jnp.float32), reduce_w.astype(jnp.float32), gain_one, shift_one, group_w.astype(jnp.float32), gain_two, shift_two, expand_w.astype(jnp.float32), gain_three, shift_three, proj_w.astype(jnp.float32), gain_proj, shift_proj)

    def closed(*params):
        return forward(*params, weight)
    result, pullback = jax.vjp(closed, *primals)
    gradients = pullback(cotangent.astype(jnp.float32))
    return (result.astype(jnp.bfloat16), gradients[0].astype(jnp.bfloat16), gradients[1], gradients[2], gradients[3], gradients[4], gradients[5], gradients[6], gradients[7], gradients[8], gradients[9], gradients[10], gradients[11], gradients[12])
```

```python
import jax
import jax.numpy as jnp
from jax import lax
from jax.experimental import pallas as pl
from jax.experimental.pallas import tpu as pltpu
from jax.sharding import PartitionSpec as P

GROUPS = 32
GW = 32


EPS = 1e-05


def shifted(value, axis, by):
    peers = lax.axis_size(axis)
    pairs = [(i, i + by) for i in range(peers) if 0 <= i + by < peers]
    return lax.ppermute(value, axis, pairs)


def silu_slope(values):
    logistic = jax.nn.sigmoid(values)
    return logistic * (1.0 + values * (1.0 - logistic))


def channel_sums(values):
    return jnp.sum(values, axis=(0, 1, 2))


def split_like(vector, extents):
    pieces = []
    offset = 0
    for extent in extents:
        pieces.append(vector[offset : offset + extent])
        offset += extent
    return pieces


def exchange(value, axis, mask):
    peers = lax.axis_size(axis)
    return lax.ppermute(value, axis, [(i, i ^ mask) for i in range(peers)])


def sum_plan():
    rounds = []
    for axis in ("ba", "ha"):
        bits = [1 << b for b in range(lax.axis_size(axis).bit_length() - 1)]
        if axis == "ba" and bits:
            rounds.append((axis, bits[:1]))
            bits = bits[1:]
        while bits:
            rounds.append((axis, bits[:2]))
            bits = bits[2:]
    return rounds


def meet(value, axis, masks):
    offsets = [0]
    for mask in masks:
        offsets = offsets + [o ^ mask for o in offsets]
    return [value] + [exchange(value, axis, o) for o in offsets[1:]]


def mesh_sum(value):
    for axis, masks in sum_plan():
        parts = meet(value, axis, masks)
        while len(parts) > 1:
            parts = [parts[i] + parts[i + 1] for i in range(0, len(parts), 2)]
        value = parts[0]
    return value


def merge(one, two):
    count = one[0] + two[0]
    gap = two[1] - one[1]
    mean = (one[0] * one[1] + two[0] * two[1]) / count
    return (count, mean, one[2] + two[2] + gap * gap * (one[0] * two[0] / count))


def mesh_moments(count, mean, spread):
    width = mean.shape[0]
    state = (count, mean, spread)
    for axis, masks in sum_plan():
        packed = jnp.stack([jnp.broadcast_to(state[0], (width,)), state[1], state[2]])
        parts = [state] + [(p[0], p[1], p[2]) for p in meet(packed, axis, masks)[1:]]
        while len(parts) > 1:
            parts = [merge(parts[i], parts[i + 1]) for i in range(0, len(parts), 2)]
        state = parts[0]
    return state


CUTS = (("ba", 1), ("ha", 1), ("ha", 2), ("ba", 2), ("ba", 4))
PARTS = 32


def own_part(cuts):
    index = jnp.int32(0)
    for axis, mask in cuts:
        bit = jnp.bitwise_and(lax.axis_index(axis), mask) // mask
        index = index * 2 + bit.astype(jnp.int32)
    return index


def pack_kernel(own_ref, value_ref, out_ref):
    out_ref[...] = value_ref[...].astype(out_ref.dtype)


def relabel(value, own, dtype):
    parts, rows, cols = value.shape
    spec = pltpu.PrefetchScalarGridSpec(
        num_scalar_prefetch=1,
        grid=(parts,),
        in_specs=[pl.BlockSpec((None, rows, cols), lambda j, own: (jnp.bitwise_xor(j, own[0]), 0, 0))],
        out_specs=pl.BlockSpec((None, rows, cols), lambda j, own: (j, 0, 0)),
    )
    return pl.pallas_call(
        pack_kernel,
        grid_spec=spec,
        out_shape=jax.ShapeDtypeStruct(value.shape, dtype),
    )(own.reshape(1), value)


def add_low(one, two):
    return (one.astype(jnp.float32) + two.astype(jnp.float32)).astype(jnp.bfloat16)


def scatter_sum(blocks, cuts):
    for axis, mask in cuts:
        half = blocks.shape[0] // 2
        got = exchange(blocks[half:], axis, mask)
        blocks = add_low(blocks[:half], got)
    spare = 8
    while spare < lax.axis_size("ba"):
        blocks = add_low(blocks, exchange(blocks, "ba", spare))
        spare *= 2
    return blocks


def gather_all(part, cuts):
    blocks = part
    for axis, mask in reversed(cuts):
        blocks = jnp.concatenate([blocks, exchange(blocks, axis, mask)], axis=0)
    return blocks


def total_gradient(value, cuts):
    own = own_part(cuts)
    part = scatter_sum(relabel(value, own, jnp.bfloat16), cuts)
    return relabel(gather_all(part, cuts), own, jnp.float32)


def moments(activations, weight, local_count):
    extents = [member.shape[-1] for member in activations]
    means = [channel_sums(member * weight) / local_count for member in activations]
    spreads = [
        channel_sums((member - mean) * (member - mean) * weight)
        for member, mean in zip(activations, means)
    ]
    count, mean, spread = mesh_moments(local_count, jnp.concatenate(means), jnp.concatenate(spreads))
    if jnp.ndim(count):
        count = count[0]
    inv_std = split_like(lax.rsqrt(spread / count + EPS), extents)
    centred = [member - m for member, m in zip(activations, split_like(mean, extents))]
    normed = [member * scale for member, scale in zip(centred, inv_std)]
    return (normed, inv_std, count)


def norm_back(upstreams, normed, inv_std, gain_list, weight, count_of):
    extents = [member.shape[-1] for member in upstreams]
    sums = mesh_sum(
        jnp.stack(
            [
                jnp.concatenate([channel_sums(member) for member in upstreams]),
                jnp.concatenate(
                    [channel_sums(member * other) for member, other in zip(upstreams, normed)]
                ),
            ]
        )
    )
    shift_grads = split_like(sums[0], extents)
    gain_grads = split_like(sums[1], extents)
    results = []
    for position in range(len(upstreams)):
        adjusted = (
            upstreams[position]
            - weight * (shift_grads[position] + normed[position] * gain_grads[position]) / count_of
        )
        results.append((gain_list[position] * inv_std[position] * adjusted).astype(jnp.bfloat16))
    return (results, gain_grads, shift_grads)


def window_at(padded, row_tap, col_tap, rows_out, cols_out):
    return padded[:, row_tap : row_tap + 2 * rows_out : 2, col_tap : col_tap + 2 * cols_out : 2]


def by_group(values):
    return values.reshape(values.shape[:3] + (GROUPS, GW))


def pad_along(values, axis, before, after):
    widths = [(0, 0)] * values.ndim
    widths[axis] = (before, after)
    return jnp.pad(values, widths)


def weave(even_part, odd_part, axis):
    extent = odd_part.shape[axis]
    head = lax.slice_in_dim(even_part, 0, extent, axis=axis)
    tail = lax.slice_in_dim(even_part, extent, extent + 1, axis=axis)
    paired = jnp.stack([head, odd_part], axis=axis + 1)
    shape_of = list(odd_part.shape)
    shape_of[axis] = 2 * extent
    return jnp.concatenate([paired.reshape(shape_of), tail], axis=axis)


def per_device(
    images_in,
    reduce_w,
    gain_one,
    shift_one,
    group_w,
    gain_two,
    shift_two,
    expand_w,
    gain_three,
    shift_three,
    proj_w,
    gain_proj,
    shift_proj,
    valid_mask,
    cotangent,
):
    weight = valid_mask.astype(jnp.float32)[:, None, None, None]
    n_images, rows_in, cols_in, chans_in = images_in.shape
    rows_out = rows_in // 2
    cols_out = cols_in // 2
    mid_width = reduce_w.shape[1]
    reduced = jnp.einsum("nhwc,cd->nhwd", images_in, reduce_w, preferred_element_type=jnp.float32)
    normed_one, inv_one, count_in = moments(
        [reduced], weight, jnp.sum(weight) * float(rows_in * cols_in)
    )
    pre_one = normed_one[0] * gain_one + shift_one
    hidden_one = jax.nn.silu(pre_one).astype(jnp.bfloat16)
    from_above = shifted(hidden_one[:, -1:], "ha", 1)
    padded = jnp.pad(
        jnp.concatenate([from_above, hidden_one], axis=1), ((0, 0), (0, 0), (1, 0), (0, 0))
    )
    grouped = jnp.zeros((n_images, rows_out, cols_out, GROUPS, GW), jnp.float32)
    for row_tap in range(3):
        for col_tap in range(3):
            kernel = group_w[row_tap, col_tap].reshape(GW, GROUPS, GW)
            grouped = grouped + jnp.einsum(
                "nhwgc,cgj->nhwgj",
                by_group(window_at(padded, row_tap, col_tap, rows_out, cols_out)),
                kernel,
                preferred_element_type=jnp.float32,
            )
    grouped = grouped.reshape(n_images, rows_out, cols_out, mid_width)
    normed_two, inv_two, count_out = moments(
        [grouped], weight, jnp.sum(weight) * float(rows_out * cols_out)
    )
    pre_two = normed_two[0] * gain_two + shift_two
    hidden_two = jax.nn.silu(pre_two).astype(jnp.bfloat16)
    expanded = jnp.einsum("nhwc,cd->nhwd", hidden_two, expand_w, preferred_element_type=jnp.float32)
    sampled = images_in[:, ::2, ::2]
    projected = jnp.einsum("nhwc,cd->nhwd", sampled, proj_w, preferred_element_type=jnp.float32)
    normed_out, inv_out, count_out = moments(
        [expanded, projected], weight, jnp.sum(weight) * float(rows_out * cols_out)
    )
    summed = normed_out[0] * gain_three + shift_three + normed_out[1] * gain_proj + shift_proj
    output = (jax.nn.silu(summed) * weight).astype(jnp.bfloat16)
    upstream = cotangent.astype(jnp.float32) * weight * silu_slope(summed)
    grads_out, gains_out, shifts_out = norm_back(
        [upstream, upstream], normed_out, inv_out, [gain_three, gain_proj], weight, count_out
    )
    d_expanded, d_projected = (grads_out[0], grads_out[1])
    grad_expand = jnp.einsum(
        "nhwc,nhwd->cd", hidden_two, d_expanded, preferred_element_type=jnp.float32
    )
    grad_proj = jnp.einsum(
        "nhwc,nhwd->cd", sampled, d_projected, preferred_element_type=jnp.float32
    )
    back_two = jnp.einsum("nhwd,cd->nhwc", d_expanded, expand_w, preferred_element_type=jnp.float32)
    back_side = jnp.einsum("nhwd,cd->nhwc", d_projected, proj_w, preferred_element_type=jnp.float32)
    grads_two, gains_two, shifts_two = norm_back(
        [back_two * silu_slope(pre_two)], normed_two, inv_two, [gain_two], weight, count_out
    )
    d_grouped = by_group(grads_two[0])
    kernel_grads = []
    row_lines = []
    for row_tap in range(3):
        tap_pieces = []
        for col_tap in range(3):
            kernel = group_w[row_tap, col_tap].reshape(GW, GROUPS, GW)
            window = by_group(window_at(padded, row_tap, col_tap, rows_out, cols_out))
            kernel_grads.append(
                jnp.einsum(
                    "nhwgc,nhwgj->cgj", window, d_grouped, preferred_element_type=jnp.float32
                ).reshape(GW, mid_width)
            )
            tap_pieces.append(
                jnp.einsum(
                    "nhwgj,cgj->nhwgc", d_grouped, kernel, preferred_element_type=jnp.float32
                ).reshape(n_images, rows_out, cols_out, mid_width)
            )
        col_even = pad_along(tap_pieces[0], 2, 0, 1) + pad_along(tap_pieces[2], 2, 1, 0)
        row_lines.append(weave(col_even, tap_pieces[1], 2))
    row_even = pad_along(row_lines[0], 1, 0, 1) + pad_along(row_lines[2], 1, 1, 0)
    back_pad = weave(row_even, row_lines[1], 1)
    grad_group = jnp.stack(kernel_grads).reshape(3, 3, GW, mid_width)
    from_below = shifted(back_pad[:, 0:1, 1:].astype(jnp.bfloat16), "ha", -1).astype(jnp.float32)
    back_one = back_pad[:, 1:, 1:]
    back_one = jnp.concatenate([back_one[:, :-1], back_one[:, -1:] + from_below], axis=1)
    grads_one, gains_one, shifts_one = norm_back(
        [back_one * silu_slope(pre_one)], normed_one, inv_one, [gain_one], weight, count_in
    )
    d_reduced = grads_one[0]
    grad_reduce = jnp.einsum(
        "nhwc,nhwd->cd", images_in, d_reduced, preferred_element_type=jnp.float32
    )
    back_in = jnp.einsum("nhwd,cd->nhwc", d_reduced, reduce_w, preferred_element_type=jnp.float32)
    zeros_side = jnp.zeros_like(back_side)
    side_row = weave(pad_along(back_side, 2, 0, 1), zeros_side, 2)[:, :, :cols_in]
    side_full = weave(pad_along(side_row, 1, 0, 1), jnp.zeros_like(side_row), 1)[:, :rows_in]
    grad_images = (back_in + side_full).astype(jnp.bfloat16)
    swapped = (CUTS[0], CUTS[2], CUTS[1], CUTS[3], CUTS[4])
    mid = grad_reduce.shape[1]
    wide = grad_expand.shape[1]
    grad_expand = total_gradient(grad_expand.reshape(PARTS, -1, wide), CUTS).reshape(grad_expand.shape)
    grad_proj = total_gradient(grad_proj.reshape(PARTS, -1, wide), swapped).reshape(grad_proj.shape)
    taps = jnp.transpose(grad_group.reshape(9, GW, mid), (1, 0, 2))
    taps = total_gradient(taps, swapped)
    grad_group = jnp.transpose(taps, (1, 0, 2)).reshape(grad_group.shape)
    grad_reduce = total_gradient(grad_reduce.reshape(PARTS, -1, mid), CUTS).reshape(grad_reduce.shape)
    return (
        output,
        grad_images,
        grad_reduce,
        gains_one[0],
        shifts_one[0],
        grad_group,
        gains_two[0],
        shifts_two[0],
        grad_expand,
        gains_out[0],
        shifts_out[0],
        grad_proj,
        gains_out[1],
        shifts_out[1],
    )


def solution(mesh):
    return jax.shard_map(
        per_device,
        mesh=mesh,
        in_specs=(
            P("ba", "ha", None, None),
            P(),
            P(),
            P(),
            P(),
            P(),
            P(),
            P(),
            P(),
            P(),
            P(),
            P(),
            P(),
            P("ba"),
            P("ba", "ha", None, None),
        ),
        out_specs=(
            P("ba", "ha", None, None),
            P("ba", "ha", None, None),
            P(),
            P(),
            P(),
            P(),
            P(),
            P(),
            P(),
            P(),
            P(),
            P(),
            P(),
            P(),
        ),
        check_vma=False,
    )
```

```python
import functools

import jax
import jax.numpy as jnp
from jax import lax
from jax.experimental import pallas as pl
from jax.experimental.pallas import tpu as pltpu
from jax.sharding import PartitionSpec as P

GW = 32
EPS = 1e-05


def shifted(value, axis, by):
    peers = lax.axis_size(axis)
    pairs = [(i, i + by) for i in range(peers) if 0 <= i + by < peers]
    return lax.ppermute(value, axis, pairs)


def exchange(value, axis, mask):
    peers = lax.axis_size(axis)
    return lax.ppermute(value, axis, [(i, i ^ mask) for i in range(peers)])


def sum_plan():
    rounds = []
    for axis in ("ba", "ha"):
        bits = [1 << b for b in range(lax.axis_size(axis).bit_length() - 1)]
        if axis == "ba" and bits:
            rounds.append((axis, bits[:1]))
            bits = bits[1:]
        while bits:
            rounds.append((axis, bits[:2]))
            bits = bits[2:]
    return rounds


def meet(value, axis, masks):
    offsets = [0]
    for mask in masks:
        offsets = offsets + [o ^ mask for o in offsets]
    return [value] + [exchange(value, axis, o) for o in offsets[1:]]


def mesh_sum(value):
    for axis, masks in sum_plan():
        parts = meet(value, axis, masks)
        while len(parts) > 1:
            parts = [parts[i] + parts[i + 1] for i in range(0, len(parts), 2)]
        value = parts[0]
    return value


def merge(one, two, one_count, two_count):
    count = one_count + two_count
    gap = two[0] - one[0]
    mean = (one_count * one[0] + two_count * two[0]) / count
    return jnp.stack([mean, one[1] + two[1] + gap * gap * (one_count * two_count / count)])


def merge_parts(parts, counts):
    parts, counts = list(parts), list(counts)
    while len(parts) > 1:
        pairs = range(0, len(parts), 2)
        parts = [merge(parts[i], parts[i + 1], counts[i], counts[i + 1]) for i in pairs]
        counts = [counts[i] + counts[i + 1] for i in pairs]
    return parts[0], counts[0]


def first_moments(packed):
    rounds = []
    state = packed
    for axis, masks in sum_plan():
        parts = meet(state, axis, masks)
        counts = [part[0, 0] for part in parts]
        rounds.append(counts)
        merged, count = merge_parts([part[1:] for part in parts], counts)
        state = jnp.concatenate([jnp.full((1, merged.shape[1]), count), merged])
    return state[1:], state[0, 0], rounds


def mesh_moments(packed, rounds):
    for (axis, masks), counts in zip(sum_plan(), rounds):
        packed, _ = merge_parts(meet(packed, axis, masks), counts)
    return packed


CUTS = (("ba", 1), ("ha", 1), ("ha", 2), ("ba", 2), ("ba", 4))
PARTS = 32


def own_part(cuts):
    index = jnp.int32(0)
    for axis, mask in cuts:
        bit = jnp.bitwise_and(lax.axis_index(axis), mask) // mask
        index = index * 2 + bit.astype(jnp.int32)
    return index


def pack_kernel(own_ref, value_ref, out_ref):
    out_ref[...] = value_ref[...].astype(out_ref.dtype)


def relabel(value, own, dtype):
    parts, rows, cols = value.shape
    spec = pltpu.PrefetchScalarGridSpec(
        num_scalar_prefetch=1,
        grid=(parts,),
        in_specs=[pl.BlockSpec((None, rows, cols), lambda j, own: (jnp.bitwise_xor(j, own[0]), 0, 0))],
        out_specs=pl.BlockSpec((None, rows, cols), lambda j, own: (j, 0, 0)),
    )
    return pl.pallas_call(
        pack_kernel,
        grid_spec=spec,
        out_shape=jax.ShapeDtypeStruct(value.shape, dtype),
    )(own.reshape(1), value)


def add_low(one, two):
    return (one.astype(jnp.float32) + two.astype(jnp.float32)).astype(jnp.bfloat16)


def scatter_sum(blocks, cuts):
    for axis, mask in cuts:
        half = blocks.shape[0] // 2
        got = exchange(blocks[half:], axis, mask)
        blocks = add_low(blocks[:half], got)
    spare = 8
    while spare < lax.axis_size("ba"):
        blocks = add_low(blocks, exchange(blocks, "ba", spare))
        spare *= 2
    return blocks


def gather_all(part, cuts):
    blocks = part
    for axis, mask in reversed(cuts):
        blocks = jnp.concatenate([blocks, exchange(blocks, axis, mask)], axis=0)
    return blocks


def total_gradient(blocks, cuts, own):
    return relabel(gather_all(scatter_sum(blocks, cuts), cuts), own, jnp.float32)


LOW = jnp.bfloat16
WIDE = jnp.float32
TAPS = 3
SMEM = pltpu.SMEM


def dot(one, two):
    return jnp.dot(one, two, preferred_element_type=WIDE)


def dot_nt(one, two):
    return lax.dot_general(one, two, (((1,), (1,)), ((), ())), preferred_element_type=WIDE)


def dot_tn(one, two):
    return lax.dot_general(one, two, (((0,), (0,)), ((), ())), preferred_element_type=WIDE)


def iota(shape, axis):
    return lax.broadcasted_iota(jnp.int32, shape, axis)


def logistic(values):
    return 0.5 * jnp.tanh(0.5 * values) + 0.5


def fold(values):
    rows, width = values.shape
    return jnp.sum(values.reshape(rows // 8, 8, width), axis=0)


def close(partial):
    return jnp.sum(partial, axis=0, keepdims=True)


def spans(rows, size):
    return [slice(at, at + size) for at in range(0, rows, size)]


def widen(mask, width):
    return jnp.concatenate([mask] * (width // mask.shape[1]), axis=1)


def parity_order(image_rows, cols, axis=0):
    pixels = image_rows * cols
    quarter = pixels // 4
    half_cols = cols // 2
    place = iota((pixels, pixels), axis)
    source = iota((pixels, pixels), 1 - axis)
    plane = place // quarter
    inside = place % quarter
    row = 2 * (inside // half_cols) + plane // 2
    col = 2 * (inside % half_cols) + plane % 2
    return (source == row * cols + col).astype(WIDE).astype(LOW)


def halo_order(images, cols):
    count = images * cols
    half_cols = cols // 2
    place = iota((count, count), 0)
    source = iota((count, count), 1)
    parity = place // (count // 2)
    inside = place % (count // 2)
    image = inside // half_cols
    col = 2 * (inside % half_cols) + parity
    return (source == image * cols + col).astype(WIDE).astype(LOW)


def local_moments(ref, mask_ref, planes, plane_rows, count, size):
    width = ref.shape[1]
    total = jnp.zeros((8, width), WIDE)
    for plane in range(planes):
        for span in spans(plane_rows, size):
            at = slice(plane * plane_rows + span.start, plane * plane_rows + span.stop)
            total += fold(ref[at, :] * widen(mask_ref[span, :], width))
    mean = close(total) / count
    total = jnp.zeros((8, width), WIDE)
    for plane in range(planes):
        for span in spans(plane_rows, size):
            at = slice(plane * plane_rows + span.start, plane * plane_rows + span.stop)
            gap = ref[at, :] - mean
            total += fold(gap * gap * widen(mask_ref[span, :], width))
    return mean, close(total)


def reduce_kernel(dims, count_ref, x_ref, w_ref, mask_ref, planes_ref, reduced_ref, stats_ref):
    images, image_rows, cols = dims
    pixels = image_rows * cols
    quarter = pixels // 4
    plane_rows = images * quarter

    @pl.when(pl.program_id(0) == 0)
    def _():
        order = parity_order(image_rows, cols)
        for image in range(images):
            moved = dot(order, x_ref[image * pixels : (image + 1) * pixels, :]).astype(LOW)
            for plane in range(4):
                at = plane * plane_rows + image * quarter
                planes_ref[at : at + quarter, :] = moved[plane * quarter : (plane + 1) * quarter, :]

    for plane in range(4):
        at = slice(plane * plane_rows, (plane + 1) * plane_rows)
        reduced_ref[at, :] = dot(planes_ref[at, :], w_ref[...])
    count = count_ref[0] * float(pixels)
    mean, spread = local_moments(reduced_ref, mask_ref, 4, plane_rows, count, quarter)
    stats_ref[0:1, :] = jnp.full(mean.shape, count, WIDE)
    stats_ref[1:2, :] = mean
    stats_ref[2:3, :] = spread


def project_kernel(quarter, count_ref, x_ref, w_ref, mask_ref, out_ref, stats_ref):
    out_ref[...] = dot(x_ref[...], w_ref[...])
    count = count_ref[0] * float(quarter)
    mean, spread = local_moments(out_ref, mask_ref, 1, out_ref.shape[0], count, quarter)
    stats_ref[0:1, :] = mean
    stats_ref[1:2, :] = spread


def group_mask(width):
    return (iota((width, width), 0) // GW == iota((width, width), 1) // GW).astype(WIDE).astype(LOW)


def block_weights(w_ref, mask, tap):
    width = w_ref.shape[1]
    part = w_ref[tap * GW : (tap + 1) * GW, :]
    return jnp.concatenate([part] * (width // GW), axis=0) * mask


def shift_columns(values, cols, by):
    rows, width = values.shape
    moved = pltpu.roll(values, by % rows, 0)
    edge = 0 if by > 0 else cols - 1
    return jnp.where(iota((rows, width), 0) % cols == edge, 0.0, moved)


def activate(values, mean, scale, shift):
    normal = (values - mean) * scale + shift
    return normal * logistic(normal)


def windows(planes, odd, halves):
    even_even, even_odd, even_moved = planes
    images, deep, half_cols, width = odd[0].shape
    tall = deep - 1

    def part(ref, at):
        return ref[:, at : at + tall, :, :].reshape(images * tall * half_cols, width)

    result = []
    for row_tap in range(TAPS):
        if row_tap == 1:
            result += [even_moved[...], even_even[...], even_odd[...]]
        else:
            at = 0 if row_tap == 0 else 1
            result += [part(odd[2], at), part(odd[0], at), part(odd[1], at)]
    return result


def store_hidden(dims, get, halo, even, odd):
    images, tall, half_cols = dims
    quarter = tall * half_cols
    for image in range(images):
        at = slice(image * quarter, (image + 1) * quarter)
        even[0][at, :] = get(0, image).astype(LOW)
        values = get(1, image)
        even[1][at, :] = values.astype(LOW)
        even[2][at, :] = shift_columns(values, half_cols, 1).astype(LOW)
        values = get(2, image)
        width = values.shape[1]
        odd[0][image, 1:, :, :] = values.astype(LOW).reshape(tall, half_cols, width)
        values = get(3, image)
        odd[1][image, 1:, :, :] = values.astype(LOW).reshape(tall, half_cols, width)
        odd[2][image, 1:, :, :] = shift_columns(values, half_cols, 1).astype(LOW).reshape(tall, half_cols, width)
    width = halo[0].shape[1]
    odd[0][:, 0, :, :] = halo[0].astype(LOW).reshape(images, half_cols, width)
    odd[1][:, 0, :, :] = halo[1].astype(LOW).reshape(images, half_cols, width)
    odd[2][:, 0, :, :] = shift_columns(halo[1], half_cols, 1).astype(LOW).reshape(images, half_cols, width)


def window_scratch(images, tall, half_cols, width):
    flat = pltpu.VMEM((images * tall * half_cols, width), LOW)
    deep = pltpu.VMEM((images, tall + 1, half_cols, width), LOW)
    return [flat, flat, flat, deep, deep, deep]


def conv_kernel(
    dims,
    scalar_ref,
    reduced_ref,
    moments_ref,
    affine_ref,
    halo_ref,
    reduce_ref,
    group_ref,
    mask_ref,
    grouped_ref,
    stats_ref,
    edge_ref,
    moved_ref,
    *buffers,
):
    images, tall, half_cols = dims
    quarter = tall * half_cols
    plane_rows = images * quarter
    width = reduced_ref.shape[1]

    @pl.when(pl.program_id(0) == 0)
    def _():
        moved_ref[...] = dot(halo_order(images, 2 * half_cols), halo_ref[...]).astype(LOW)

    mean = moments_ref[0:1, :]
    scale = affine_ref[0:1, :] * lax.rsqrt(moments_ref[1:2, :] / scalar_ref[1] + EPS)
    shift = affine_ref[1:2, :]
    edge = activate(dot(moved_ref[...], reduce_ref[...]), mean, scale, shift) * scalar_ref[3]
    edge_ref[...] = edge.astype(LOW)
    half = edge.shape[0] // 2

    def get(plane, image):
        at = plane * plane_rows + image * quarter
        return activate(reduced_ref[at : at + quarter, :], mean, scale, shift)

    even, odd = buffers[:3], buffers[3:]
    store_hidden(dims, get, (edge[:half], edge[half:]), even, odd)
    mask = group_mask(width)
    total = None
    for tap, window in enumerate(windows(even, odd, half_cols)):
        term = dot(window, block_weights(group_ref, mask, tap))
        total = term if total is None else total + term
    grouped_ref[...] = total
    count = scalar_ref[0] * float(quarter)
    mean, spread = local_moments(grouped_ref, mask_ref, 1, plane_rows, count, quarter)
    stats_ref[0:1, :] = mean
    stats_ref[1:2, :] = spread


def expand_kernel(
    quarter, scalar_ref, grouped_ref, moments_ref, affine_ref, w_ref, mask_ref, hidden_ref, out_ref, stats_ref
):
    @pl.when(pl.program_id(0) == 0)
    def _():
        mean = moments_ref[0:1, :]
        scale = affine_ref[0:1, :] * lax.rsqrt(moments_ref[1:2, :] / scalar_ref[2] + EPS)
        for span in spans(grouped_ref.shape[0], 16):
            hidden_ref[span, :] = activate(grouped_ref[span, :], mean, scale, affine_ref[1:2, :]).astype(LOW)

    out_ref[...] = dot(hidden_ref[...], w_ref[...])
    count = scalar_ref[0] * float(quarter)
    mean, spread = local_moments(out_ref, mask_ref, 1, out_ref.shape[0], count, quarter)
    stats_ref[0:1, :] = mean
    stats_ref[1:2, :] = spread


def slope(values, gate):
    return gate * (1.0 + values * (1.0 - gate))


def tail_values(one, two, stats, affine, count):
    first = (one - stats[0:1, :]) * lax.rsqrt(stats[1:2, :] / count + EPS)
    second = (two - stats[2:3, :]) * lax.rsqrt(stats[3:4, :] / count + EPS)
    summed = first * affine[0:1, :] + affine[1:2, :] + second * affine[2:3, :] + affine[3:4, :]
    return first, second, summed


def output_kernel(
    size, scalar_ref, expanded_ref, projected_ref, stats_ref, affine_ref, cot_ref, mask_ref, out_ref, sums_ref
):
    rows, width = out_ref.shape
    totals = [jnp.zeros((8, width), WIDE) for _ in range(3)]
    stats = stats_ref[...]
    affine = affine_ref[...]
    for span in spans(rows, size):
        first, second, summed = tail_values(
            expanded_ref[span, :], projected_ref[span, :], stats, affine, scalar_ref[2]
        )
        valid = widen(mask_ref[span, :], width)
        gate = logistic(summed)
        out_ref[span, :] = (valid * (summed * gate)).astype(LOW)
        upstream = cot_ref[span, :].astype(WIDE) * valid * slope(summed, gate)
        totals[0] += fold(upstream)
        totals[1] += fold(upstream * first)
        totals[2] += fold(upstream * second)
    for at in range(3):
        sums_ref[at : at + 1, :] = close(totals[at])


def weights_kernel(
    size,
    scalar_ref,
    own_ref,
    expanded_ref,
    projected_ref,
    stats_ref,
    affine_ref,
    sums_ref,
    cot_ref,
    mask_ref,
    hidden_ref,
    sampled_ref,
    d_expanded_ref,
    d_projected_ref,
    grad_expand_ref,
    grad_proj_ref,
):
    rows, width = d_expanded_ref.shape
    stats = stats_ref[...]
    affine = affine_ref[...]
    count = scalar_ref[2]
    gain_one = affine[0:1, :] * lax.rsqrt(stats[1:2, :] / count + EPS)
    gain_two = affine[2:3, :] * lax.rsqrt(stats[3:4, :] / count + EPS)
    sums = sums_ref[...] / count
    for span in spans(rows, size):
        first, second, summed = tail_values(expanded_ref[span, :], projected_ref[span, :], stats, affine, count)
        valid = widen(mask_ref[span, :], width)
        upstream = cot_ref[span, :].astype(WIDE) * slope(summed, logistic(summed)) - sums[0:1, :]
        d_expanded_ref[span, :] = (valid * gain_one * (upstream - first * sums[1:2, :])).astype(LOW)
        d_projected_ref[span, :] = (valid * gain_two * (upstream - second * sums[2:3, :])).astype(LOW)
    relabel_store(dot_tn(sampled_ref[...], d_projected_ref[...]), grad_proj_ref, own_ref[1])
    relabel_store(dot_tn(hidden_ref[...], d_expanded_ref[...]), grad_expand_ref, own_ref[0])


def relabel_store(value, ref, own):
    parts, rows, _ = ref.shape
    for part in range(parts):
        ref[jnp.bitwise_xor(own, part)] = value[part * rows : (part + 1) * rows, :].astype(ref.dtype)


def back_two_kernel(size, scalar_ref, d_ref, w_ref, grouped_ref, moments_ref, affine_ref, out_ref, sums_ref):
    rows, width = out_ref.shape
    mean = moments_ref[0:1, :]
    inv = lax.rsqrt(moments_ref[1:2, :] / scalar_ref[2] + EPS)
    out_ref[...] = dot_nt(d_ref[...], w_ref[...])
    totals = [jnp.zeros((8, width), WIDE) for _ in range(2)]
    for span in spans(rows, size):
        normed = (grouped_ref[span, :] - mean) * inv
        before = normed * affine_ref[0:1, :] + affine_ref[1:2, :]
        grad = out_ref[span, :] * slope(before, logistic(before))
        out_ref[span, :] = grad
        totals[0] += fold(grad)
        totals[1] += fold(grad * normed)
    for at in range(2):
        sums_ref[at : at + 1, :] = close(totals[at])


def norm_back_values(grad, values, mean, inv, gain, sums):
    return gain * inv * (grad - (sums[0:1, :] + (values - mean) * inv * sums[1:2, :]))


def conv_back_kernel(
    dims,
    scalar_ref,
    own_ref,
    grad_ref,
    grouped_ref,
    below_grad_ref,
    below_grouped_ref,
    moments_two_ref,
    affine_two_ref,
    sums_two_ref,
    reduced_ref,
    edge_ref,
    moments_one_ref,
    affine_one_ref,
    group_ref,
    mask_ref,
    out_ref,
    sums_ref,
    grad_group_ref,
    *buffers,
):
    images, tall, half_cols = dims
    quarter = tall * half_cols
    plane_rows = images * quarter
    width = reduced_ref.shape[1]
    even, odd, below = buffers[:3], buffers[3:6], buffers[6:8]
    count_in, count_out = scalar_ref[1], scalar_ref[2]

    mean = moments_two_ref[0:1, :]
    inv = lax.rsqrt(moments_two_ref[1:2, :] / count_out + EPS)
    gain = affine_two_ref[0:1, :]
    sums = sums_two_ref[...] / count_out
    for image in range(images):
        at = slice(image * quarter, (image + 1) * quarter)
        values = norm_back_values(grad_ref[at, :], grouped_ref[at, :], mean, inv, gain, sums)
        values = values * widen(mask_ref[at, :], width)
        below[0][image, :tall, :, :] = values.astype(LOW).reshape(tall, half_cols, width)
        below[1][image, :tall, :, :] = (
            shift_columns(values, half_cols, -1).astype(LOW).reshape(tall, half_cols, width)
        )
        at = slice(image * half_cols, (image + 1) * half_cols)
        values = norm_back_values(
            below_grad_ref[at, :].astype(WIDE), below_grouped_ref[at, :].astype(WIDE), mean, inv, gain, sums
        )
        valid = mask_ref[image * quarter : image * quarter + half_cols, :]
        values = values * widen(valid, width) * scalar_ref[4]
        below[0][image, tall, :, :] = values.astype(LOW)
        below[1][image, tall, :, :] = shift_columns(values, half_cols, -1).astype(LOW)

    def part(ref, at):
        return ref[:, at : at + tall, :, :].reshape(plane_rows, width)

    mask = group_mask(width)
    weights = [block_weights(group_ref, mask, tap) for tap in range(TAPS * TAPS)]
    here, left = part(below[0], 0), part(below[1], 0)
    next_here, next_left = part(below[0], 1), part(below[1], 1)
    out_ref[0:plane_rows, :] = dot_nt(here, weights[4])
    out_ref[plane_rows : 2 * plane_rows, :] = dot_nt(here, weights[5]) + dot_nt(left, weights[3])
    out_ref[2 * plane_rows : 3 * plane_rows, :] = dot_nt(here, weights[7]) + dot_nt(next_here, weights[1])
    out_ref[3 * plane_rows : 4 * plane_rows, :] = (
        dot_nt(here, weights[8])
        + dot_nt(left, weights[6])
        + dot_nt(next_here, weights[2])
        + dot_nt(next_left, weights[0])
    )

    mean_one = moments_one_ref[0:1, :]
    inv_one = lax.rsqrt(moments_one_ref[1:2, :] / count_in + EPS)
    totals = [jnp.zeros((8, width), WIDE) for _ in range(2)]

    def get(plane, image):
        start = plane * plane_rows + image * quarter
        at = slice(start, start + quarter)
        normed = (reduced_ref[at, :] - mean_one) * inv_one
        before = normed * affine_one_ref[0:1, :] + affine_one_ref[1:2, :]
        gate = logistic(before)
        grad = out_ref[at, :] * slope(before, gate)
        out_ref[at, :] = grad
        totals[0] += fold(grad)
        totals[1] += fold(grad * normed)
        return before * gate

    half = edge_ref.shape[0] // 2
    edge = edge_ref[...].astype(WIDE)
    store_hidden(dims, get, (edge[:half], edge[half:]), even, odd)
    for at in range(2):
        sums_ref[at : at + 1, :] = close(totals[at])
    wide_mask = mask.astype(WIDE)
    pieces = []
    for window in windows(even, odd, half_cols):
        full = dot_tn(window, here) * wide_mask
        pieces.append(jnp.sum(full.reshape(width // GW, GW, width), axis=0))
    relabel_store(jnp.concatenate(pieces, axis=0), grad_group_ref, own_ref[1])


def reduced_back_kernel(
    size,
    scalar_ref,
    own_ref,
    grad_ref,
    reduced_ref,
    moments_ref,
    affine_ref,
    sums_ref,
    mask_ref,
    planes_ref,
    d_ref,
    grad_reduce_ref,
):
    rows, width = d_ref.shape
    plane_rows = mask_ref.shape[0]
    mean = moments_ref[0:1, :]
    inv = lax.rsqrt(moments_ref[1:2, :] / scalar_ref[1] + EPS)
    sums = sums_ref[...] / scalar_ref[1]
    for span in spans(rows, size):
        values = norm_back_values(grad_ref[span, :], reduced_ref[span, :], mean, inv, affine_ref[0:1, :], sums)
        at = span.start % plane_rows
        d_ref[span, :] = (values * widen(mask_ref[at : at + size, :], width)).astype(LOW)
    relabel_store(dot_tn(planes_ref[...], d_ref[...]), grad_reduce_ref, own_ref[0])


def images_back_kernel(dims, d_ref, w_ref, side_ref, proj_ref, out_ref, side_out, order_ref):
    image_rows, cols = dims
    pixels = image_rows * cols
    quarter = pixels // 4

    @pl.when(pl.program_id(0) == 0)
    def _():
        side_out[...] = dot_nt(side_ref[...], proj_ref[...])
        order_ref[...] = parity_order(image_rows, cols, 1)

    image = pl.program_id(0)
    values = dot_nt(d_ref[...].reshape(pixels, d_ref.shape[-1]), w_ref[...])
    first = values[:quarter] + side_out[pl.ds(pl.multiple_of(image * quarter, quarter), quarter), :]
    planes = jnp.concatenate([first, values[quarter:]], axis=0).astype(LOW)
    out_ref[...] = dot(order_ref[...], planes).astype(LOW)


def whole(shape):
    return pl.BlockSpec(shape, lambda i: (0,) * len(shape))


def wide_cols(rows, width):
    return pl.BlockSpec((rows, width), lambda i: (0, i))


SCALARS = pl.BlockSpec(memory_space=pltpu.SMEM)


def call(kernel, grid, in_specs, out_specs, out_shapes, cost, scratch=()):
    flops, moved = cost
    return pl.pallas_call(
        kernel,
        grid=(grid,),
        in_specs=in_specs,
        out_specs=out_specs,
        out_shape=[jax.ShapeDtypeStruct(shape, kind) for shape, kind in out_shapes],
        scratch_shapes=list(scratch),
        compiler_params=pltpu.CompilerParams(vmem_limit_bytes=56 * 1024 * 1024),
        cost_estimate=pl.CostEstimate(flops=flops, bytes_accessed=moved, transcendentals=0),
    )


def per_device(
    images_in,
    reduce_w,
    gain_one,
    shift_one,
    group_w,
    gain_two,
    shift_two,
    expand_w,
    gain_three,
    shift_three,
    proj_w,
    gain_proj,
    shift_proj,
    valid_mask,
    cotangent,
):
    images, image_rows, cols, chans = images_in.shape
    mid = reduce_w.shape[1]
    wide = expand_w.shape[1]
    tall, half_cols = image_rows // 2, cols // 2
    quarter = tall * half_cols
    rows = images * quarter
    pixels = images * image_rows * cols
    block = 256
    steps = mid // block
    strip = 512
    strips = wide // strip

    weight = valid_mask.astype(WIDE)
    local = jnp.sum(weight)
    local_one = local.reshape(1)
    mask = jnp.broadcast_to(weight[:, None, None], (images, quarter, 128)).reshape(rows, 128)
    row_index = lax.axis_index("ha")
    has_upper = (row_index > 0).astype(WIDE)
    has_lower = (row_index < lax.axis_size("ha") - 1).astype(WIDE)
    swapped = (CUTS[0], CUTS[2], CUTS[1], CUTS[3], CUTS[4])
    own_plain, own_swapped = own_part(CUTS), own_part(swapped)
    own = jnp.stack([own_plain, own_swapped])
    affine_one = jnp.stack([gain_one, shift_one])
    affine_two = jnp.stack([gain_two, shift_two])
    affine_out = jnp.stack([gain_three, shift_three, gain_proj, shift_proj])
    group_flat = group_w.reshape(TAPS * TAPS * GW, mid)

    halo_images = shifted(images_in[:, -1], "ha", 1).reshape(images * cols, chans)
    planes, reduced, stats = call(
        functools.partial(reduce_kernel, (images, image_rows, cols)),
        steps,
        [SCALARS, whole((pixels, chans)), wide_cols(chans, block), whole((rows, 128))],
        [whole((pixels, chans)), wide_cols(pixels, block), wide_cols(3, block)],
        [((pixels, chans), LOW), ((pixels, mid), WIDE), ((3, mid), WIDE)],
        (2 * pixels * chans * (mid + 256), 20 << 20),
    )(local_one, images_in.reshape(pixels, chans), reduce_w, mask)
    moments_one, count_in, rounds = first_moments(stats)
    projected, stats_proj = call(
        functools.partial(project_kernel, quarter),
        strips,
        [SCALARS, whole((rows, chans)), wide_cols(chans, strip), whole((rows, 128))],
        [wide_cols(rows, strip), wide_cols(2, strip)],
        [((rows, wide), WIDE), ((2, wide), WIDE)],
        (2 * rows * chans * wide, 10 << 20),
    )(local_one, planes, proj_w, mask)
    count_out = count_in / 4.0
    rounds = [[count / 4.0 for count in counts] for counts in rounds]
    scalars = jnp.stack([local, count_in, count_out, has_upper, has_lower])

    grouped, stats, edge = call(
        functools.partial(conv_kernel, (images, tall, half_cols)),
        steps,
        [
            SCALARS,
            wide_cols(pixels, block),
            wide_cols(2, block),
            wide_cols(2, block),
            whole((images * cols, chans)),
            wide_cols(chans, block),
            wide_cols(TAPS * TAPS * GW, block),
            whole((rows, 128)),
        ],
        [wide_cols(rows, block), wide_cols(2, block), wide_cols(images * cols, block)],
        [((rows, mid), WIDE), ((2, mid), WIDE), ((images * cols, mid), LOW)],
        (2 * rows * mid * 9 * 256, 14 << 20),
        [pltpu.VMEM((images * cols, chans), LOW)] + window_scratch(images, tall, half_cols, block),
    )(scalars, reduced, moments_one, affine_one, halo_images, reduce_w, group_flat, mask)
    below_grouped = shifted(
        grouped.reshape(images, tall, half_cols, mid)[:, 0].astype(LOW), "ha", -1
    ).reshape(images * half_cols, mid)
    merged = mesh_moments(jnp.concatenate([stats, stats_proj], axis=1), rounds)
    moments_two, moments_proj = merged[:, :mid], merged[:, mid:]

    hidden_two, expanded, stats = call(
        functools.partial(expand_kernel, quarter),
        strips,
        [
            SCALARS,
            whole((rows, mid)),
            whole((2, mid)),
            whole((2, mid)),
            wide_cols(mid, strip),
            whole((rows, 128)),
        ],
        [whole((rows, mid)), wide_cols(rows, strip), wide_cols(2, strip)],
        [((rows, mid), LOW), ((rows, wide), WIDE), ((2, wide), WIDE)],
        (2 * rows * mid * wide, 12 << 20),
    )(scalars, grouped, moments_two, affine_two, expand_w, mask)
    moments_out = jnp.concatenate([mesh_moments(stats, rounds), moments_proj])

    cot = cotangent.reshape(rows, wide)
    output, sums = call(
        functools.partial(output_kernel, 16),
        strips,
        [
            SCALARS,
            wide_cols(rows, strip),
            wide_cols(rows, strip),
            wide_cols(4, strip),
            wide_cols(4, strip),
            wide_cols(rows, strip),
            whole((rows, 128)),
        ],
        [wide_cols(rows, strip), wide_cols(3, strip)],
        [((rows, wide), LOW), ((3, wide), WIDE)],
        (20 * rows * wide, 12 << 20),
    )(scalars, expanded, projected, moments_out, affine_out, cot, mask)
    sums_out = mesh_sum(sums)

    parts_spec = pl.BlockSpec((PARTS, mid // PARTS, strip), lambda i: (0, 0, i))
    d_expanded, d_projected, parts_expand, parts_proj = call(
        functools.partial(weights_kernel, 16),
        strips,
        [
            SCALARS,
            SCALARS,
            wide_cols(rows, strip),
            wide_cols(rows, strip),
            wide_cols(4, strip),
            wide_cols(4, strip),
            wide_cols(3, strip),
            wide_cols(rows, strip),
            whole((rows, 128)),
            whole((rows, mid)),
            whole((rows, chans)),
        ],
        [wide_cols(rows, strip), wide_cols(rows, strip), parts_spec, parts_spec],
        [
            ((rows, wide), LOW),
            ((rows, wide), LOW),
            ((PARTS, mid // PARTS, wide), LOW),
            ((PARTS, chans // PARTS, wide), LOW),
        ],
        (4 * rows * mid * wide, 24 << 20),
    )(scalars, own, expanded, projected, moments_out, affine_out, sums_out, cot, mask, hidden_two, planes)

    grad_two, sums = call(
        functools.partial(back_two_kernel, 16),
        steps,
        [
            SCALARS,
            whole((rows, wide)),
            pl.BlockSpec((block, wide), lambda i: (i, 0)),
            wide_cols(rows, block),
            wide_cols(2, block),
            wide_cols(2, block),
        ],
        [wide_cols(rows, block), wide_cols(2, block)],
        [((rows, mid), WIDE), ((2, mid), WIDE)],
        (2 * rows * mid * wide, 10 << 20),
    )(scalars, d_expanded, expand_w, grouped, moments_two, affine_two)
    below_grad = shifted(
        grad_two.reshape(images, tall, half_cols, mid)[:, 0].astype(LOW), "ha", -1
    ).reshape(images * half_cols, mid)
    sums_two = mesh_sum(sums)

    deep = pltpu.VMEM((images, tall + 1, half_cols, block), LOW)
    grad_one, sums, parts_group = call(
        functools.partial(conv_back_kernel, (images, tall, half_cols)),
        steps,
        [
            SCALARS,
            SCALARS,
            wide_cols(rows, block),
            wide_cols(rows, block),
            wide_cols(images * half_cols, block),
            wide_cols(images * half_cols, block),
            wide_cols(2, block),
            wide_cols(2, block),
            wide_cols(2, block),
            wide_cols(pixels, block),
            wide_cols(images * cols, block),
            wide_cols(2, block),
            wide_cols(2, block),
            wide_cols(TAPS * TAPS * GW, block),
            whole((rows, 128)),
        ],
        [
            wide_cols(pixels, block),
            wide_cols(2, block),
            pl.BlockSpec((PARTS, TAPS * TAPS * GW // PARTS, block), lambda i: (0, 0, i)),
        ],
        [
            ((pixels, mid), WIDE),
            ((2, mid), WIDE),
            ((PARTS, TAPS * TAPS * GW // PARTS, mid), LOW),
        ],
        (4 * rows * mid * 9 * 256, 24 << 20),
        window_scratch(images, tall, half_cols, block) + [deep, deep],
    )(
        scalars,
        own,
        grad_two,
        grouped,
        below_grad,
        below_grouped,
        moments_two,
        affine_two,
        sums_two,
        reduced,
        edge,
        moments_one,
        affine_one,
        group_flat,
        mask,
    )
    sums_one = mesh_sum(sums)

    d_reduced, parts_reduce = call(
        functools.partial(reduced_back_kernel, 16),
        steps,
        [
            SCALARS,
            SCALARS,
            wide_cols(pixels, block),
            wide_cols(pixels, block),
            wide_cols(2, block),
            wide_cols(2, block),
            wide_cols(2, block),
            whole((rows, 128)),
            whole((pixels, chans)),
        ],
        [
            wide_cols(pixels, block),
            pl.BlockSpec((PARTS, chans // PARTS, block), lambda i: (0, 0, i)),
        ],
        [((pixels, mid), LOW), ((PARTS, chans // PARTS, mid), LOW)],
        (2 * pixels * mid * chans, 26 << 20),
    )(scalars, own, grad_one, reduced, moments_one, affine_one, sums_one, mask, planes)

    grad_images = call(
        functools.partial(images_back_kernel, (image_rows, cols)),
        images,
        [
            pl.BlockSpec((4, None, quarter, mid), lambda i: (0, i, 0, 0)),
            whole((chans, mid)),
            whole((rows, wide)),
            whole((chans, wide)),
        ],
        [pl.BlockSpec((None, image_rows * cols, chans), lambda i: (i, 0, 0))],
        [((images, image_rows * cols, chans), LOW)],
        (2 * pixels * mid * chans + 2 * rows * wide * chans, 16 << 20),
        [pltpu.VMEM((rows, chans), WIDE), pltpu.VMEM((image_rows * cols, image_rows * cols), LOW)],
    )(d_reduced.reshape(4, images, quarter, mid), reduce_w, d_projected, proj_w)[0]

    grad_expand = total_gradient(parts_expand, CUTS, own_plain)
    grad_proj = total_gradient(parts_proj, swapped, own_swapped)
    grad_group = total_gradient(parts_group, swapped, own_swapped)
    grad_reduce = total_gradient(parts_reduce, CUTS, own_plain)
    return (
        output.reshape(cotangent.shape),
        grad_images.reshape(images_in.shape),
        grad_reduce.reshape(reduce_w.shape),
        sums_one[1],
        sums_one[0],
        grad_group.reshape(group_w.shape),
        sums_two[1],
        sums_two[0],
        grad_expand.reshape(expand_w.shape),
        sums_out[1],
        sums_out[0],
        grad_proj.reshape(proj_w.shape),
        sums_out[2],
        sums_out[0],
    )


def solution(mesh):
    split = P("ba", "ha", None, None)
    rest = (P(),) * 12
    return jax.shard_map(
        per_device,
        mesh=mesh,
        in_specs=(split,) + rest + (P("ba"), split),
        out_specs=(split, split) + rest,
        check_vma=False,
    )
```

```python
import functools
import math

import jax
import jax.numpy as jnp
from jax import lax
from jax.experimental import pallas as pl
from jax.experimental.pallas import tpu as pltpu
from jax.sharding import PartitionSpec as P

GW = 32
EPS = 1e-05
VMEM_LIMIT = 40 * 1024 * 1024


def shifted(value, axis, by):
    peers = lax.axis_size(axis)
    pairs = [(i, i + by) for i in range(peers) if 0 <= i + by < peers]
    return lax.ppermute(value, axis, pairs)


def exchange(value, axis, mask):
    peers = lax.axis_size(axis)
    return lax.ppermute(value, axis, [(i, i ^ mask) for i in range(peers)])


def sum_plan(axes):
    rounds = []
    for axis in axes:
        bits = [1 << b for b in range(lax.axis_size(axis).bit_length() - 1)]
        if axis == "ba" and bits:
            rounds.append((axis, bits[:1]))
            bits = bits[1:]
        while bits:
            rounds.append((axis, bits[:2]))
            bits = bits[2:]
    return rounds


def meet(value, axis, masks):
    offsets = [0]
    for mask in masks:
        offsets = offsets + [o ^ mask for o in offsets]
    return [value] + [exchange(value, axis, o) for o in offsets[1:]]


def add_round(value, axis, masks):
    parts = meet(value, axis, masks)
    while len(parts) > 1:
        parts = [parts[i] + parts[i + 1] for i in range(0, len(parts), 2)]
    return parts[0]


def mesh_sum(value, rounds):
    for axis, masks in rounds:
        value = add_round(value, axis, masks)
    return value


def merge(one, two):
    count = one[0] + two[0]
    gap = two[1] - one[1]
    return (
        count,
        (one[0] * one[1] + two[0] * two[1]) / count,
        one[2] + two[2] + gap * gap * (one[0] * two[0] / count),
        (one[0] * one[3] + two[0] * two[3]) / count,
    )


def mesh_moments(packed, rounds):
    for axis, masks in rounds:
        parts = [tuple(part) for part in meet(packed, axis, masks)]
        while len(parts) > 1:
            parts = [merge(parts[i], parts[i + 1]) for i in range(0, len(parts), 2)]
        packed = jnp.stack(parts[0])
    return packed


CUTS = (("ba", 1), ("ha", 1), ("ha", 2), ("ba", 2), ("ba", 4))
PARTS = 32


def own_part(cuts):
    index = jnp.int32(0)
    for axis, mask in cuts:
        bit = jnp.bitwise_and(lax.axis_index(axis), mask) // mask
        index = index * 2 + bit.astype(jnp.int32)
    return index


def spread_kernel(own_ref, low_ref, high_ref, *out_refs):
    half = low_ref.shape[0]
    rows = out_refs[0].shape[1]
    for part in range(2 * half):
        at = jnp.bitwise_xor(own_ref[0], part)
        ref = low_ref if part < half else high_ref
        out_refs[0][at] = ref[part % half, :rows, :].astype(jnp.float32)
        if len(out_refs) > 1:
            more = out_refs[1].shape[0]
            extra = ref[part % half, rows : rows + more, :].astype(jnp.float32)
            for row in range(more):
                out_refs[1][row, pl.ds(at, 1), :] = extra[row : row + 1, :]


def plain_order(low, high, own, rows, more):
    half, deep, cols = low.shape
    width = 512
    shapes = [(2 * half, rows)] + ([(more, 2 * half)] if more else [])
    block = pl.BlockSpec((half, deep, width), lambda i: (0, 0, i))
    return pl.pallas_call(
        spread_kernel,
        grid=(cols // width,),
        in_specs=[pl.BlockSpec(memory_space=pltpu.SMEM), block, block],
        out_specs=[pl.BlockSpec(shape + (width,), lambda i: (0, 0, i)) for shape in shapes],
        out_shape=[jax.ShapeDtypeStruct(shape + (cols,), jnp.float32) for shape in shapes],
        compiler_params=pltpu.CompilerParams(vmem_limit_bytes=VMEM_LIMIT),
        cost_estimate=pl.CostEstimate(flops=0, bytes_accessed=12 * low.size, transcendentals=0),
    )(own.reshape(1), low, high)


def add_low(one, two):
    return (one.astype(jnp.float32) + two.astype(jnp.float32)).astype(jnp.bfloat16)


def tie(*values):
    return lax.optimization_barrier(values)


class Gradient:
    def __init__(self, low, high, cuts, own):
        self.low, self.high, self.cuts, self.own = low, high, cuts, own
        self.blocks = None
        self.at = 0
        self.got = None

    def send(self):
        count = len(self.cuts)
        if self.at < count:
            self.got = exchange(self.high, *self.cuts[self.at])
        else:
            self.got = exchange(self.blocks, *self.cuts[2 * count - 1 - self.at])

    def take(self):
        count = len(self.cuts)
        if self.at < count:
            blocks = add_low(self.low, self.got)
            half = blocks.shape[0] // 2
            if half:
                self.low, self.high = blocks[:half], blocks[half:]
            else:
                spare = 8
                while spare < lax.axis_size("ba"):
                    blocks = add_low(blocks, exchange(blocks, "ba", spare))
                    spare *= 2
                self.blocks = blocks
        else:
            if self.at == 2 * count - 1:
                self.low, self.high = self.blocks, self.got
            else:
                self.blocks = jnp.concatenate([self.blocks, self.got], axis=0)
        self.got = None
        self.at += 1

    def step(self):
        self.take()
        if self.at < 2 * len(self.cuts):
            self.send()

    def finish(self, rows, more=0):
        return plain_order(self.low, self.high, self.own, rows, more)


def arrive(grads, *values):
    held = tie(*values, *[grad.got for grad in grads])
    for grad, got in zip(grads, held[len(values) :]):
        grad.got = got
    return held[: len(values)]


LOW = jnp.bfloat16
WIDE = jnp.float32
TAPS = 3
SMEM = pltpu.SMEM


def dot(one, two):
    return jnp.dot(one, two, preferred_element_type=WIDE)


def dot_nt(one, two):
    return lax.dot_general(one, two, (((1,), (1,)), ((), ())), preferred_element_type=WIDE)


def dot_tn(one, two):
    return lax.dot_general(one, two, (((0,), (0,)), ((), ())), preferred_element_type=WIDE)


def iota(shape, axis):
    return lax.broadcasted_iota(jnp.int32, shape, axis)


def logistic(values):
    return 0.5 * jnp.tanh(0.5 * values) + 0.5


def fold(values):
    rows, width = values.shape
    return jnp.sum(values.reshape(rows // 8, 8, width), axis=0)


def close(partial):
    return jnp.sum(partial, axis=0, keepdims=True)


def spans(rows, size):
    return [slice(at, at + size) for at in range(0, rows, size)]


def parity_order(image_rows, cols, axis=0):
    pixels = image_rows * cols
    quarter = pixels // 4
    half_cols = cols // 2
    place = iota((pixels, pixels), axis)
    source = iota((pixels, pixels), 1 - axis)
    plane = place // quarter
    inside = place % quarter
    row = 2 * (inside // half_cols) + plane // 2
    col = 2 * (inside % half_cols) + plane % 2
    return (source == row * cols + col).astype(WIDE).astype(LOW)


def halo_order(images, cols):
    count = images * cols
    half_cols = cols // 2
    place = iota((count, count), 0)
    source = iota((count, count), 1)
    parity = place // (count // 2)
    inside = place % (count // 2)
    image = inside // half_cols
    col = 2 * (inside % half_cols) + parity
    return (source == image * cols + col).astype(WIDE).astype(LOW)


def shifted_sums(ref, valid_ref, base, planes, images, quarter):
    width = ref.shape[1]
    total = jnp.zeros((8, width), WIDE)
    square = jnp.zeros((8, width), WIDE)
    for image in range(images):
        first = jnp.zeros((8, width), WIDE)
        second = jnp.zeros((8, width), WIDE)
        for plane in range(planes):
            at = (plane * images + image) * quarter
            gap = ref[at : at + quarter, :] - base
            first += fold(gap)
            second += fold(gap * gap)
        total += first * valid_ref[image]
        square += second * valid_ref[image]
    return close(total), close(square)


def moments_of(sums, base, count):
    offset = sums[0:1, :] / count
    variance = jnp.maximum(sums[1:2, :] / count - offset * offset, 0.0)
    return base + offset, lax.rsqrt(variance + EPS)


def row_of(values, w):
    return dot(jnp.broadcast_to(values, (16, values.shape[1])).astype(LOW), w)[0:1, :]


def reduce_kernel(dims, valid_ref, x_ref, w_ref, planes_ref, reduced_ref, stats_ref, sampled_ref):
    images, image_rows, cols = dims
    pixels = image_rows * cols
    quarter = pixels // 4
    plane_rows = images * quarter
    valid = valid_ref[0]
    for image in range(1, images):
        valid = valid + valid_ref[image]

    @pl.when(pl.program_id(0) == 0)
    def _():
        order = parity_order(image_rows, cols)
        total = jnp.zeros((8, x_ref.shape[1]), WIDE)
        for image in range(images):
            moved = dot(order, x_ref[image * pixels : (image + 1) * pixels, :])
            total += fold(moved[:quarter, :]) * valid_ref[image]
            moved = moved.astype(LOW)
            for plane in range(4):
                at = plane * plane_rows + image * quarter
                planes_ref[at : at + quarter, :] = moved[plane * quarter : (plane + 1) * quarter, :]
        sampled_ref[...] = close(total) / (valid * float(quarter))

    for plane in range(4):
        at = slice(plane * plane_rows, (plane + 1) * plane_rows)
        reduced_ref[at, :] = dot(planes_ref[at, :], w_ref[...])
    count = valid * float(pixels)
    base = reduced_ref[0:1, :]
    total, square = shifted_sums(reduced_ref, valid_ref, base, 4, images, quarter)
    stats_ref[0:1, :] = jnp.full(base.shape, count, WIDE)
    stats_ref[1:2, :] = base + total / count
    stats_ref[2:3, :] = jnp.maximum(square - total * (total / count), 0.0)


def turn_kernel(own_ref, value_ref, out_ref):
    parts, rows, _ = out_ref.shape
    turned = value_ref[...].T
    for part in range(parts):
        out_ref[jnp.bitwise_xor(own_ref[0], part)] = turned[part * rows : (part + 1) * rows, :]


def project_kernel(quarter, valid_ref, x_ref, w_ref, sampled_ref, out_ref, sums_ref):
    out_ref[...] = dot(x_ref[...], w_ref[...])
    base = row_of(sampled_ref[...], w_ref[...])
    images = out_ref.shape[0] // quarter
    total, square = shifted_sums(out_ref, valid_ref, base, 1, images, quarter)
    sums_ref[0:1, :] = total
    sums_ref[1:2, :] = square
    sums_ref[2:3, :] = base


def group_mask(width):
    return (iota((width, width), 0) // GW == iota((width, width), 1) // GW).astype(WIDE).astype(LOW)


def block_weights(w_ref, mask, tap):
    width = w_ref.shape[1]
    part = w_ref[tap * GW : (tap + 1) * GW, :]
    return jnp.concatenate([part] * (width // GW), axis=0) * mask


def shift_columns(values, cols, by):
    rows, width = values.shape
    moved = pltpu.roll(values, by % rows, 0)
    edge = 0 if by > 0 else cols - 1
    return jnp.where(iota((rows, width), 0) % cols == edge, 0.0, moved)


def activate(values, mean, scale, shift):
    normal = (values - mean) * scale + shift
    return normal * logistic(normal)


def windows(planes, odd, halves):
    even_even, even_odd, even_moved = planes
    images, deep, half_cols, width = odd[0].shape
    tall = deep - 1

    def part(ref, at):
        return ref[:, at : at + tall, :, :].reshape(images * tall * half_cols, width)

    result = []
    for row_tap in range(TAPS):
        if row_tap == 1:
            result += [even_moved[...], even_even[...], even_odd[...]]
        else:
            at = 0 if row_tap == 0 else 1
            result += [part(odd[2], at), part(odd[0], at), part(odd[1], at)]
    return result


def store_hidden(dims, get, halo, even, odd):
    images, tall, half_cols = dims
    quarter = tall * half_cols
    for image in range(images):
        at = slice(image * quarter, (image + 1) * quarter)
        even[0][at, :] = get(0, image).astype(LOW)
        values = get(1, image)
        even[1][at, :] = values.astype(LOW)
        even[2][at, :] = shift_columns(values, half_cols, 1).astype(LOW)
        values = get(2, image)
        width = values.shape[1]
        odd[0][image, 1:, :, :] = values.astype(LOW).reshape(tall, half_cols, width)
        values = get(3, image)
        odd[1][image, 1:, :, :] = values.astype(LOW).reshape(tall, half_cols, width)
        odd[2][image, 1:, :, :] = shift_columns(values, half_cols, 1).astype(LOW).reshape(tall, half_cols, width)
    width = halo[0].shape[1]
    odd[0][:, 0, :, :] = halo[0].astype(LOW).reshape(images, half_cols, width)
    odd[1][:, 0, :, :] = halo[1].astype(LOW).reshape(images, half_cols, width)
    odd[2][:, 0, :, :] = shift_columns(halo[1], half_cols, 1).astype(LOW).reshape(images, half_cols, width)


def window_scratch(images, tall, half_cols, width):
    flat = pltpu.VMEM((images * tall * half_cols, width), LOW)
    deep = pltpu.VMEM((images, tall + 1, half_cols, width), LOW)
    return [flat, flat, flat, deep, deep, deep]


def conv_kernel(
    dims,
    scalar_ref,
    valid_ref,
    reduced_ref,
    moments_ref,
    affine_ref,
    halo_ref,
    reduce_ref,
    group_ref,
    grouped_ref,
    sums_ref,
    base_ref,
    first_ref,
    edge_ref,
    moved_ref,
    *buffers,
):
    images, tall, half_cols = dims
    quarter = tall * half_cols
    plane_rows = images * quarter
    width = reduced_ref.shape[1]

    @pl.when(pl.program_id(0) == 0)
    def _():
        moved_ref[...] = dot(halo_order(images, 2 * half_cols), halo_ref[...]).astype(LOW)

    mean = moments_ref[0:1, :]
    scale = affine_ref[0:1, :] * lax.rsqrt(moments_ref[1:2, :] / scalar_ref[0] + EPS)
    shift = affine_ref[1:2, :]
    edge = activate(dot(moved_ref[...], reduce_ref[...]), mean, scale, shift) * scalar_ref[2]
    edge_ref[...] = edge.astype(LOW)
    half = edge.shape[0] // 2

    def get(plane, image):
        at = plane * plane_rows + image * quarter
        return activate(reduced_ref[at : at + quarter, :], mean, scale, shift)

    even, odd = buffers[:3], buffers[3:]
    store_hidden(dims, get, (edge[:half], edge[half:]), even, odd)
    mask = group_mask(width)
    total = None
    for tap, window in enumerate(windows(even, odd, half_cols)):
        term = dot(window, block_weights(group_ref, mask, tap))
        total = term if total is None else total + term
    grouped_ref[...] = total
    kernel = group_ref[0:GW, :].astype(WIDE)
    for tap in range(1, TAPS * TAPS):
        kernel = kernel + group_ref[tap * GW : (tap + 1) * GW, :].astype(WIDE)
    kernel = jnp.concatenate([kernel.astype(LOW)] * (width // GW), axis=0) * mask
    base = row_of(shift * logistic(shift), kernel)
    total, square = shifted_sums(grouped_ref, valid_ref, base, 1, images, quarter)
    sums_ref[0:1, :] = total
    sums_ref[1:2, :] = square
    base_ref[...] = base
    for image in range(images):
        at = image * quarter
        first_ref[image * half_cols : (image + 1) * half_cols, :] = grouped_ref[at : at + half_cols, :].astype(LOW)


def expand_kernel(
    quarter,
    scalar_ref,
    valid_ref,
    grouped_ref,
    sums_two_ref,
    base_two_ref,
    affine_ref,
    w_ref,
    side_ref,
    hidden_ref,
    out_ref,
    sums_ref,
    base_ref,
):
    shift = affine_ref[1:2, :]

    @pl.when(pl.program_id(0) == 0)
    def _():
        mean, inv = moments_of(sums_two_ref[...], base_two_ref[...], scalar_ref[1])
        scale = affine_ref[0:1, :] * inv
        for span in spans(grouped_ref.shape[0], 16):
            hidden_ref[span, :] = activate(grouped_ref[span, :], mean, scale, shift).astype(LOW)

    out_ref[...] = dot(hidden_ref[...], w_ref[...])
    base = row_of(shift * logistic(shift), w_ref[...])
    images = out_ref.shape[0] // quarter
    total, square = shifted_sums(out_ref, valid_ref, base, 1, images, quarter)
    sums_ref[0:1, :] = total
    sums_ref[1:2, :] = square
    sums_ref[2:4, :] = side_ref[0:2, :]
    base_ref[0:1, :] = base
    base_ref[1:2, :] = side_ref[2:3, :]


def slope(values, gate):
    return gate * (1.0 + values * (1.0 - gate))


def tail_moments(sums_ref, base_ref, count):
    return (
        *moments_of(sums_ref[0:2, :], base_ref[0:1, :], count),
        *moments_of(sums_ref[2:4, :], base_ref[1:2, :], count),
    )


def tail_values(one, two, moments, affine):
    first = (one - moments[0]) * moments[1]
    second = (two - moments[2]) * moments[3]
    summed = first * affine[0:1, :] + affine[1:2, :] + second * affine[2:3, :] + affine[3:4, :]
    return first, second, summed


def output_kernel(
    size,
    scalar_ref,
    valid_ref,
    expanded_ref,
    projected_ref,
    stats_ref,
    base_ref,
    affine_ref,
    cot_ref,
    out_ref,
    sums_ref,
):
    rows, width = out_ref.shape
    quarter = rows // valid_ref.shape[0]
    totals = [jnp.zeros((8, width), WIDE) for _ in range(3)]
    moments = tail_moments(stats_ref, base_ref, scalar_ref[1])
    affine = affine_ref[...]
    for span in spans(rows, size):
        first, second, summed = tail_values(expanded_ref[span, :], projected_ref[span, :], moments, affine)
        valid = valid_ref[span.start // quarter]
        gate = logistic(summed)
        out_ref[span, :] = (valid * (summed * gate)).astype(LOW)
        upstream = (cot_ref[span, :].astype(WIDE) * valid) * slope(summed, gate)
        totals[0] += fold(upstream)
        totals[1] += fold(upstream * first)
        totals[2] += fold(upstream * second)
    for at in range(3):
        sums_ref[at : at + 1, :] = close(totals[at])


def weights_kernel(
    size,
    scalar_ref,
    valid_ref,
    expanded_ref,
    projected_ref,
    stats_ref,
    base_ref,
    affine_ref,
    sums_ref,
    cot_ref,
    hidden_ref,
    sampled_ref,
    d_expanded_ref,
    d_projected_ref,
    expand_low_ref,
    expand_high_ref,
    proj_low_ref,
    proj_high_ref,
):
    rows, width = d_expanded_ref.shape
    quarter = rows // valid_ref.shape[0]
    count = scalar_ref[1]
    moments = tail_moments(stats_ref, base_ref, count)
    affine = affine_ref[...]
    gain_one = affine[0:1, :] * moments[1]
    gain_two = affine[2:3, :] * moments[3]
    sums = sums_ref[...] / count
    for span in spans(rows, size):
        first, second, summed = tail_values(expanded_ref[span, :], projected_ref[span, :], moments, affine)
        valid = valid_ref[span.start // quarter]
        upstream = cot_ref[span, :].astype(WIDE) * slope(summed, logistic(summed)) - sums[0:1, :]
        d_expanded_ref[span, :] = ((valid * gain_one) * (upstream - first * sums[1:2, :])).astype(LOW)
        d_projected_ref[span, :] = ((valid * gain_two) * (upstream - second * sums[2:3, :])).astype(LOW)
    store_halves(sampled_ref[...], d_projected_ref[...], proj_low_ref, proj_high_ref)
    store_halves(hidden_ref[...], d_expanded_ref[...], expand_low_ref, expand_high_ref)


def store_halves(turned, grads, low_ref, high_ref):
    half = low_ref.shape[0]
    for at, ref in ((0, low_ref), (half, high_ref)):
        left = turned[at : at + half].reshape(half * turned.shape[1], turned.shape[2])
        ref[...] = dot(left, grads).astype(LOW).reshape(ref.shape)


def back_two_kernel(
    size, dims, scalar_ref, d_ref, w_ref, grouped_ref, sums_two_ref, base_two_ref, affine_ref, out_ref, sums_ref, first_ref
):
    rows, width = out_ref.shape
    images, tall, half_cols = dims
    mean, inv = moments_of(sums_two_ref[...], base_two_ref[...], scalar_ref[1])
    out_ref[...] = dot_nt(d_ref[...], w_ref[...])
    totals = [jnp.zeros((8, width), WIDE) for _ in range(2)]
    for span in spans(rows, size):
        normed = (grouped_ref[span, :] - mean) * inv
        before = normed * affine_ref[0:1, :] + affine_ref[1:2, :]
        grad = out_ref[span, :] * slope(before, logistic(before))
        out_ref[span, :] = grad
        totals[0] += fold(grad)
        totals[1] += fold(grad * normed)
    for at in range(2):
        sums_ref[at : at + 1, :] = close(totals[at])
    for image in range(images):
        at = image * tall * half_cols
        first_ref[image * half_cols : (image + 1) * half_cols, :] = out_ref[at : at + half_cols, :].astype(LOW)


def side_kernel(d_ref, w_ref, out_ref):
    out_ref[...] = dot_nt(d_ref[...], w_ref[...])


def norm_back_values(grad, values, mean, inv, gain, sums):
    return gain * inv * (grad - (sums[0:1, :] + (values - mean) * inv * sums[1:2, :]))


def conv_back_kernel(
    dims,
    scalar_ref,
    own_ref,
    valid_ref,
    grad_ref,
    grouped_ref,
    below_grad_ref,
    below_grouped_ref,
    sums_two_ref,
    base_two_ref,
    affine_two_ref,
    grads_two_ref,
    reduced_ref,
    edge_ref,
    moments_one_ref,
    affine_one_ref,
    group_ref,
    out_ref,
    sums_ref,
    grad_group_ref,
    *buffers,
):
    images, tall, half_cols = dims
    quarter = tall * half_cols
    plane_rows = images * quarter
    width = reduced_ref.shape[1]
    even, odd, below = buffers[:3], buffers[3:6], buffers[6:8]
    count_in, count_out = scalar_ref[0], scalar_ref[1]

    mean, inv = moments_of(sums_two_ref[...], base_two_ref[...], count_out)
    gain = affine_two_ref[0:1, :]
    sums = grads_two_ref[...] / count_out
    for image in range(images):
        at = slice(image * quarter, (image + 1) * quarter)
        values = norm_back_values(grad_ref[at, :], grouped_ref[at, :], mean, inv, gain, sums)
        values = values * valid_ref[image]
        below[0][image, :tall, :, :] = values.astype(LOW).reshape(tall, half_cols, width)
        below[1][image, :tall, :, :] = (
            shift_columns(values, half_cols, -1).astype(LOW).reshape(tall, half_cols, width)
        )
        at = slice(image * half_cols, (image + 1) * half_cols)
        values = norm_back_values(
            below_grad_ref[at, :].astype(WIDE), below_grouped_ref[at, :].astype(WIDE), mean, inv, gain, sums
        )
        values = values * (valid_ref[image] * scalar_ref[3])
        below[0][image, tall, :, :] = values.astype(LOW)
        below[1][image, tall, :, :] = shift_columns(values, half_cols, -1).astype(LOW)

    def part(ref, at):
        return ref[:, at : at + tall, :, :].reshape(plane_rows, width)

    mask = group_mask(width)
    weights = [block_weights(group_ref, mask, tap) for tap in range(TAPS * TAPS)]
    here, left = part(below[0], 0), part(below[1], 0)
    next_here, next_left = part(below[0], 1), part(below[1], 1)
    out_ref[0:plane_rows, :] = dot_nt(here, weights[4])
    out_ref[plane_rows : 2 * plane_rows, :] = dot_nt(here, weights[5]) + dot_nt(left, weights[3])
    out_ref[2 * plane_rows : 3 * plane_rows, :] = dot_nt(here, weights[7]) + dot_nt(next_here, weights[1])
    out_ref[3 * plane_rows : 4 * plane_rows, :] = (
        dot_nt(here, weights[8])
        + dot_nt(left, weights[6])
        + dot_nt(next_here, weights[2])
        + dot_nt(next_left, weights[0])
    )

    mean_one = moments_one_ref[0:1, :]
    inv_one = lax.rsqrt(moments_one_ref[1:2, :] / count_in + EPS)
    totals = [jnp.zeros((8, width), WIDE) for _ in range(2)]

    def get(plane, image):
        start = plane * plane_rows + image * quarter
        at = slice(start, start + quarter)
        normed = (reduced_ref[at, :] - mean_one) * inv_one
        before = normed * affine_one_ref[0:1, :] + affine_one_ref[1:2, :]
        gate = logistic(before)
        grad = out_ref[at, :] * slope(before, gate)
        out_ref[at, :] = grad
        totals[0] += fold(grad)
        totals[1] += fold(grad * normed)
        return before * gate

    half = edge_ref.shape[0] // 2
    edge = edge_ref[...].astype(WIDE)
    store_hidden(dims, get, (edge[:half], edge[half:]), even, odd)
    for at in range(2):
        sums_ref[at : at + 1, :] = close(totals[at])
    turned = here.T
    picked = jnp.bitwise_xor(iota((GW, width), 0), own_ref[0])
    one_hot = (iota((GW, width), 1) % GW == picked).astype(WIDE).astype(LOW)
    for tap, window in enumerate(windows(even, odd, half_cols)):
        full = dot(turned, window).astype(LOW) * mask
        grad_group_ref[tap] = dot_nt(one_hot, full).astype(LOW)


def reduced_back_kernel(
    size,
    scalar_ref,
    valid_ref,
    grad_ref,
    reduced_ref,
    moments_ref,
    affine_ref,
    sums_ref,
    *refs,
):
    planes_refs, (d_ref, low_ref, high_ref) = refs[:4], refs[4:]
    rows, width = d_ref.shape
    images = valid_ref.shape[0]
    quarter = rows // (4 * images)
    mean = moments_ref[0:1, :]
    inv = lax.rsqrt(moments_ref[1:2, :] / scalar_ref[0] + EPS)
    sums = sums_ref[...] / scalar_ref[0]
    for span in spans(rows, size):
        values = norm_back_values(grad_ref[span, :], reduced_ref[span, :], mean, inv, affine_ref[0:1, :], sums)
        d_ref[span, :] = (values * valid_ref[span.start // quarter % images]).astype(LOW)
    half = low_ref.shape[0]
    for at, ref in ((0, low_ref), (half, high_ref)):
        total = None
        for plane, planes_ref in enumerate(planes_refs):
            deep = planes_ref.shape[2]
            left = planes_ref[at : at + half].reshape(half * planes_ref.shape[1], deep)
            term = dot(left, d_ref[plane * deep : (plane + 1) * deep, :])
            total = term if total is None else total + term
        ref[...] = total.astype(LOW).reshape(ref.shape)


def images_back_kernel(dims, d_ref, w_ref, side_ref, out_ref, order_ref):
    image_rows, cols = dims
    pixels = image_rows * cols
    quarter = pixels // 4

    @pl.when(pl.program_id(0) == 0)
    def _():
        order_ref[...] = parity_order(image_rows, cols, 1)

    values = dot_nt(d_ref[...].reshape(pixels, d_ref.shape[-1]), w_ref[...])
    first = values[:quarter] + side_ref[...]
    planes = jnp.concatenate([first, values[quarter:]], axis=0).astype(LOW)
    out_ref[...] = dot(order_ref[...], planes).astype(LOW)


def whole(shape):
    return pl.BlockSpec(shape, lambda i: (0,) * len(shape))


def wide_cols(rows, width):
    return pl.BlockSpec((rows, width), lambda i: (0, i))


SCALARS = pl.BlockSpec(memory_space=pltpu.SMEM)


def place(shape, kind):
    if math.prod(shape) * jnp.dtype(kind).itemsize >= 4 << 20:
        return pltpu.HBM(shape, kind)
    return jax.ShapeDtypeStruct(shape, kind)


def call(kernel, grid, in_specs, out_specs, out_shapes, cost, scratch=()):
    flops, moved = cost
    return pl.pallas_call(
        kernel,
        grid=(grid,),
        in_specs=in_specs,
        out_specs=out_specs,
        out_shape=[place(shape, kind) for shape, kind in out_shapes],
        scratch_shapes=list(scratch),
        compiler_params=pltpu.CompilerParams(vmem_limit_bytes=VMEM_LIMIT),
        cost_estimate=pl.CostEstimate(flops=flops, bytes_accessed=moved, transcendentals=0),
    )


def per_device(
    images_in,
    reduce_w,
    gain_one,
    shift_one,
    group_w,
    gain_two,
    shift_two,
    expand_w,
    gain_three,
    shift_three,
    proj_w,
    gain_proj,
    shift_proj,
    valid_mask,
    cotangent,
):
    images, image_rows, cols, chans = images_in.shape
    mid = reduce_w.shape[1]
    wide = expand_w.shape[1]
    tall, half_cols = image_rows // 2, cols // 2
    quarter = tall * half_cols
    rows = images * quarter
    pixels = images * image_rows * cols
    block = 256
    steps = mid // block
    strip = 512
    strips = wide // strip

    valid = valid_mask.astype(WIDE)
    row_index = lax.axis_index("ha")
    has_upper = (row_index > 0).astype(WIDE)
    has_lower = (row_index < lax.axis_size("ha") - 1).astype(WIDE)
    swapped = (CUTS[0], CUTS[2], CUTS[1], CUTS[3], CUTS[4])
    own_plain, own_swapped = own_part(CUTS), own_part(swapped)
    own_one, own_two = own_plain.reshape(1), own_swapped.reshape(1)
    affine_one = jnp.stack([gain_one, shift_one])
    affine_two = jnp.stack([gain_two, shift_two])
    affine_out = jnp.stack([gain_three, shift_three, gain_proj, shift_proj])
    taps = TAPS * TAPS * GW
    group_flat = group_w.reshape(taps, mid)
    rounds = sum_plan(("ba", "ha"))
    back_rounds = sum_plan(("ha", "ba"))

    halo_images = shifted(images_in[:, -1], "ha", 1).reshape(images * cols, chans)
    planes, reduced, stats, sampled = call(
        functools.partial(reduce_kernel, (images, image_rows, cols)),
        steps,
        [SCALARS, whole((pixels, chans)), wide_cols(chans, block)],
        [whole((pixels, chans)), wide_cols(pixels, block), wide_cols(3, block), whole((1, chans))],
        [((pixels, chans), LOW), ((pixels, mid), WIDE), ((3, mid), WIDE), ((1, chans), WIDE)],
        (2 * pixels * chans * (mid + 256), 20 << 20),
    )(valid, images_in.reshape(pixels, chans), reduce_w)
    stats, halo_images = tie(jnp.concatenate([stats, sampled]), halo_images)
    stats = mesh_moments(stats, rounds)

    def turn(value, at, own):
        width = value.shape[1]
        return call(
            turn_kernel,
            1,
            [SCALARS, pl.BlockSpec((rows, width), lambda i: (at, 0))],
            [whole((PARTS, width // PARTS, rows))],
            [((PARTS, width // PARTS, rows), LOW)],
            (0, 2 << 20),
        )(own, value)[0]

    planes_turned = [turn(planes, plane, own_two) for plane in range(4)]
    stats, *planes_turned = tie(stats, *planes_turned)
    count_in, moments_one, sampled_mean = stats[0, 0], stats[1:3], stats[3:4]
    scalars = jnp.stack([count_in, count_in / 4.0, has_upper, has_lower])

    grouped, sums, base_two, first_row, edge = call(
        functools.partial(conv_kernel, (images, tall, half_cols)),
        steps,
        [
            SCALARS,
            SCALARS,
            wide_cols(pixels, block),
            wide_cols(2, block),
            wide_cols(2, block),
            whole((images * cols, chans)),
            wide_cols(chans, block),
            wide_cols(taps, block),
        ],
        [
            wide_cols(rows, block),
            wide_cols(2, block),
            wide_cols(1, block),
            wide_cols(images * half_cols, block),
            wide_cols(images * cols, block),
        ],
        [
            ((rows, mid), WIDE),
            ((2, mid), WIDE),
            ((1, mid), WIDE),
            ((images * half_cols, mid), LOW),
            ((images * cols, mid), LOW),
        ],
        (2 * rows * mid * 9 * 256, 14 << 20),
        [pltpu.VMEM((images * cols, chans), LOW)] + window_scratch(images, tall, half_cols, block),
    )(scalars, valid, reduced, moments_one, affine_one, halo_images, reduce_w, group_flat)
    sums_two = mesh_sum(sums, rounds)
    below_grouped = shifted(first_row, "ha", -1)
    sums_two, below_grouped = tie(sums_two, below_grouped)
    projected, side = call(
        functools.partial(project_kernel, quarter),
        strips,
        [SCALARS, whole((rows, chans)), wide_cols(chans, strip), whole((1, chans))],
        [wide_cols(rows, strip), wide_cols(3, strip)],
        [((rows, wide), WIDE), ((3, wide), WIDE)],
        (2 * rows * chans * wide, 10 << 20),
    )(valid, planes, proj_w, sampled_mean)

    hidden_two, expanded, sums, base_out = call(
        functools.partial(expand_kernel, quarter),
        strips,
        [
            SCALARS,
            SCALARS,
            whole((rows, mid)),
            whole((2, mid)),
            whole((1, mid)),
            whole((2, mid)),
            wide_cols(mid, strip),
            wide_cols(3, strip),
        ],
        [whole((rows, mid)), wide_cols(rows, strip), wide_cols(4, strip), wide_cols(2, strip)],
        [((rows, mid), LOW), ((rows, wide), WIDE), ((4, wide), WIDE), ((2, wide), WIDE)],
        (2 * rows * mid * wide, 12 << 20),
    )(scalars, valid, grouped, sums_two, base_two, affine_two, expand_w, side)
    stats_out = mesh_sum(sums, rounds)
    stats_out, hidden_turned = tie(stats_out, turn(hidden_two, 0, own_one))

    cot = cotangent.reshape(rows, wide)
    output, sums = call(
        functools.partial(output_kernel, 16),
        strips,
        [
            SCALARS,
            SCALARS,
            wide_cols(rows, strip),
            wide_cols(rows, strip),
            wide_cols(4, strip),
            wide_cols(2, strip),
            wide_cols(4, strip),
            wide_cols(rows, strip),
        ],
        [wide_cols(rows, strip), wide_cols(3, strip)],
        [((rows, wide), LOW), ((3, wide), WIDE)],
        (20 * rows * wide, 12 << 20),
    )(scalars, valid, expanded, projected, stats_out, base_out, affine_out, cot)
    sums_out = mesh_sum(sums, rounds)

    def halves_specs(height, width):
        return [pl.BlockSpec((PARTS // 2, height // PARTS, width), lambda i: (0, 0, i))] * 2

    def halves_shapes(height, width):
        return [((PARTS // 2, height // PARTS, width), LOW)] * 2

    d_expanded, d_projected, *halves = call(
        functools.partial(weights_kernel, 16),
        strips,
        [
            SCALARS,
            SCALARS,
            wide_cols(rows, strip),
            wide_cols(rows, strip),
            wide_cols(4, strip),
            wide_cols(2, strip),
            wide_cols(4, strip),
            wide_cols(3, strip),
            wide_cols(rows, strip),
            whole((PARTS, mid // PARTS, rows)),
            whole((PARTS, chans // PARTS, rows)),
        ],
        [wide_cols(rows, strip), wide_cols(rows, strip)] + halves_specs(mid, strip) + halves_specs(chans, strip),
        [((rows, wide), LOW), ((rows, wide), LOW)] + halves_shapes(mid, wide) + halves_shapes(chans, wide),
        (4 * rows * mid * wide, 24 << 20),
    )(
        scalars,
        valid,
        expanded,
        projected,
        stats_out,
        base_out,
        affine_out,
        sums_out,
        cot,
        hidden_turned,
        planes_turned[0],
    )
    expand_sum = Gradient(*halves[:2], CUTS, own_plain)
    proj_sum = Gradient(*halves[2:], swapped, own_swapped)
    pair = [expand_sum, proj_sum]
    for grad in pair:
        grad.send()

    grad_two, sums, first_row = call(
        functools.partial(back_two_kernel, 16, (images, tall, half_cols)),
        steps,
        [
            SCALARS,
            whole((rows, wide)),
            pl.BlockSpec((block, wide), lambda i: (i, 0)),
            wide_cols(rows, block),
            wide_cols(2, block),
            wide_cols(1, block),
            wide_cols(2, block),
        ],
        [wide_cols(rows, block), wide_cols(2, block), wide_cols(images * half_cols, block)],
        [((rows, mid), WIDE), ((2, mid), WIDE), ((images * half_cols, mid), LOW)],
        (2 * rows * mid * wide, 10 << 20),
    )(scalars, d_expanded, expand_w, grouped, sums_two, base_two, affine_two)
    below_grad = shifted(first_row, "ha", -1)
    sums = mesh_sum(sums, back_rounds[:1])
    sums, below_grad = arrive(pair, sums, below_grad)
    for grad in pair:
        grad.step()
    grads_two = mesh_sum(sums, back_rounds[1:])
    (d_projected,) = tie(d_projected)
    side_grad = call(
        side_kernel,
        1,
        [whole((rows, wide)), whole((chans, wide))],
        [whole((rows, chans))],
        [((rows, chans), WIDE)],
        (2 * rows * chans * wide, 8 << 20),
    )(d_projected, proj_w)[0]

    deep = pltpu.VMEM((images, tall + 1, half_cols, block), LOW)
    grads_two, side_grad = tie(grads_two, side_grad)
    grad_one, sums, parts_group = call(
        functools.partial(conv_back_kernel, (images, tall, half_cols)),
        steps,
        [
            SCALARS,
            SCALARS,
            SCALARS,
            wide_cols(rows, block),
            wide_cols(rows, block),
            wide_cols(images * half_cols, block),
            wide_cols(images * half_cols, block),
            wide_cols(2, block),
            wide_cols(1, block),
            wide_cols(2, block),
            wide_cols(2, block),
            wide_cols(pixels, block),
            wide_cols(images * cols, block),
            wide_cols(2, block),
            wide_cols(2, block),
            wide_cols(taps, block),
        ],
        [wide_cols(pixels, block), wide_cols(2, block), pl.BlockSpec((TAPS * TAPS, GW, block), lambda i: (0, 0, i))],
        [((pixels, mid), WIDE), ((2, mid), WIDE), ((TAPS * TAPS, GW, mid), LOW)],
        (4 * rows * mid * 9 * 256, 24 << 20),
        window_scratch(images, tall, half_cols, block) + [deep, deep],
    )(
        scalars,
        own_two,
        valid,
        grad_two,
        grouped,
        below_grad,
        below_grouped,
        sums_two,
        base_two,
        affine_two,
        grads_two,
        reduced,
        edge,
        moments_one,
        affine_one,
        group_flat,
    )
    parts_group = jnp.pad(jnp.transpose(parts_group, (1, 0, 2)), ((0, 0), (0, 16 - TAPS * TAPS), (0, 0)))
    (sums,) = arrive(pair, sums)
    sums = mesh_sum(sums, back_rounds[:1])
    (sums,) = tie(sums)
    for grad in pair:
        grad.step()
    grads_one = mesh_sum(sums, back_rounds[1:])
    grads_one, parts_group = arrive(pair, grads_one, parts_group)
    for grad in pair:
        grad.step()

    d_reduced, *halves = call(
        functools.partial(reduced_back_kernel, 16),
        steps,
        [
            SCALARS,
            SCALARS,
            wide_cols(pixels, block),
            wide_cols(pixels, block),
            wide_cols(2, block),
            wide_cols(2, block),
            wide_cols(2, block),
        ]
        + [whole((PARTS, chans // PARTS, rows))] * 4,
        [wide_cols(pixels, block)] + halves_specs(chans, block),
        [((pixels, mid), LOW)] + halves_shapes(chans, mid),
        (2 * pixels * mid * chans, 26 << 20),
    )(scalars, valid, grad_one, reduced, moments_one, affine_one, grads_one, *planes_turned)
    (d_reduced,) = arrive(pair, d_reduced)
    parts_group = [parts_group[: PARTS // 2], parts_group[PARTS // 2 :]]
    halves = [jnp.concatenate(both, axis=1) for both in zip(halves, parts_group)]
    reduce_sum = Gradient(*halves, swapped, own_swapped)
    reduce_sum.send()
    for grad in pair:
        grad.step()
    everyone = pair + [reduce_sum]

    def images_back(d_part, side_part):
        part = d_part.shape[1]
        return call(
            functools.partial(images_back_kernel, (image_rows, cols)),
            part,
            [
                pl.BlockSpec((4, None, quarter, mid), lambda i: (0, i, 0, 0)),
                whole((chans, mid)),
                pl.BlockSpec((quarter, chans), lambda i: (i, 0)),
            ],
            [pl.BlockSpec((None, image_rows * cols, chans), lambda i: (i, 0, 0))],
            [((part, image_rows * cols, chans), LOW)],
            (2 * pixels * mid * chans, 16 << 20),
            [pltpu.VMEM((image_rows * cols, image_rows * cols), LOW)],
        )(d_part, reduce_w, side_part)[0]

    grad_images = images_back(d_reduced.reshape(4, images, quarter, mid), side_grad)
    (grad_images,) = arrive(everyone, grad_images)
    for grad in everyone:
        grad.step()
    for beside in (0, 0, 1, 2):
        arrive(everyone)
        for grad in everyone:
            grad.step()
        for _ in range(beside):
            reduce_sum.step()
    arrive(pair)
    for grad in pair:
        grad.take()
    (grad_expand,), (grad_proj,) = [grad.finish(width // PARTS) for grad, width in zip(pair, (mid, chans))]
    while reduce_sum.at < 2 * len(CUTS):
        reduce_sum.step()
    grad_reduce, grad_group = reduce_sum.finish(chans // PARTS, TAPS * TAPS)
    return (
        output.reshape(cotangent.shape),
        grad_images.reshape(images_in.shape),
        grad_reduce.reshape(reduce_w.shape),
        grads_one[1],
        grads_one[0],
        grad_group.reshape(group_w.shape),
        grads_two[1],
        grads_two[0],
        grad_expand.reshape(expand_w.shape),
        sums_out[1],
        sums_out[0],
        grad_proj.reshape(proj_w.shape),
        sums_out[2],
        sums_out[0],
    )


def solution(mesh):
    split = P("ba", "ha", None, None)
    rest = (P(),) * 12
    return jax.shard_map(
        per_device,
        mesh=mesh,
        in_specs=(split,) + rest + (P("ba"), split),
        out_specs=(split, split) + rest,
        check_vma=False,
    )
```

```python
import functools
import math

import jax
import jax.numpy as jnp
from jax import lax
from jax.experimental import pallas as pl
from jax.experimental.pallas import tpu as pltpu
from jax.sharding import PartitionSpec as P

GW = 32
EPS = 1e-05
VMEM_LIMIT = 40 * 1024 * 1024


def shifted(value, axis, by):
    peers = lax.axis_size(axis)
    pairs = [(i, i + by) for i in range(peers) if 0 <= i + by < peers]
    return lax.ppermute(value, axis, pairs)


def exchange(value, axis, mask):
    peers = lax.axis_size(axis)
    return lax.ppermute(value, axis, [(i, i ^ mask) for i in range(peers)])


def sum_plan(axes):
    rounds = []
    for axis in axes:
        bits = [1 << b for b in range(lax.axis_size(axis).bit_length() - 1)]
        if axis == "ba" and bits:
            rounds.append((axis, bits[:1]))
            bits = bits[1:]
        while bits:
            rounds.append((axis, bits[:2]))
            bits = bits[2:]
    return rounds


def meet(value, axis, masks):
    offsets = [0]
    for mask in masks:
        offsets = offsets + [o ^ mask for o in offsets]
    return [value] + [exchange(value, axis, o) for o in offsets[1:]]


def add_round(value, axis, masks):
    parts = meet(value, axis, masks)
    while len(parts) > 1:
        parts = [parts[i] + parts[i + 1] for i in range(0, len(parts), 2)]
    return parts[0]


def mesh_sum(value, rounds):
    for axis, masks in rounds:
        value = add_round(value, axis, masks)
    return value


def merge(one, two):
    count = one[0] + two[0]
    gap = two[1] - one[1]
    return (
        count,
        (one[0] * one[1] + two[0] * two[1]) / count,
        one[2] + two[2] + gap * gap * (one[0] * two[0] / count),
        (one[0] * one[3] + two[0] * two[3]) / count,
    )


def mesh_moments(packed, rounds):
    for axis, masks in rounds:
        parts = [tuple(part) for part in meet(packed, axis, masks)]
        while len(parts) > 1:
            parts = [merge(parts[i], parts[i + 1]) for i in range(0, len(parts), 2)]
        packed = jnp.stack(parts[0])
    return packed


PARTS = 32
SPREAD = 8
CORE, SIDE_ONE, SIDE_TWO, DEEP_ONE, DEEP_TWO = ("ba", 1), ("ha", 1), ("ha", 2), ("ba", 2), ("ba", 4)


def own_part(rounds):
    index = jnp.int32(0)
    for axis, mask in [bit for bits in rounds for bit in bits]:
        bit = jnp.bitwise_and(lax.axis_index(axis), mask) // mask
        index = index * 2 + bit.astype(jnp.int32)
    return index


def partners(bits):
    masks = [0]
    for _, mask in bits:
        masks = [old ^ new for old in masks for new in (0, mask)]
    return [(bits[0][0], mask) for mask in masks[1:]]


def spread_kernel(own_ref, low_ref, high_ref, *out_refs):
    half = low_ref.shape[0]
    rows = out_refs[0].shape[1]
    for part in range(2 * half):
        at = jnp.bitwise_xor(own_ref[0], part)
        ref = low_ref if part < half else high_ref
        out_refs[0][at] = ref[part % half, :rows, :].astype(jnp.float32)
        if len(out_refs) > 1:
            more = out_refs[1].shape[0]
            extra = ref[part % half, rows : rows + more, :].astype(jnp.float32)
            for row in range(more):
                out_refs[1][row, pl.ds(at, 1), :] = extra[row : row + 1, :]


def plain_order(low, high, own, rows, more):
    half, deep, cols = low.shape
    width = 512
    shapes = [(2 * half, rows)] + ([(more, 2 * half)] if more else [])
    block = pl.BlockSpec((half, deep, width), lambda i: (0, 0, i))
    return pl.pallas_call(
        spread_kernel,
        grid=(cols // width,),
        in_specs=[pl.BlockSpec(memory_space=pltpu.SMEM), block, block],
        out_specs=[pl.BlockSpec(shape + (width,), lambda i: (0, 0, i)) for shape in shapes],
        out_shape=[jax.ShapeDtypeStruct(shape + (cols,), jnp.float32) for shape in shapes],
        compiler_params=pltpu.CompilerParams(vmem_limit_bytes=VMEM_LIMIT),
        cost_estimate=pl.CostEstimate(flops=0, bytes_accessed=12 * low.size, transcendentals=0),
    )(own.reshape(1), low, high)


def add_low(parts):
    total = parts[0].astype(jnp.float32)
    for part in parts[1:]:
        total = total + part.astype(jnp.float32)
    return total.astype(jnp.bfloat16)


def tie(*values):
    return lax.optimization_barrier(values)


class Gradient:
    def __init__(self, pieces, rounds, joins=None):
        self.pieces, self.rounds, self.own = list(pieces), rounds, own_part(rounds)
        self.joins = tuple(reversed(joins or rounds))
        self.at = 0
        self.got = None

    def left(self):
        return len(self.rounds) + len(self.joins) - self.at

    def send(self):
        count = len(self.rounds)
        if self.at < count:
            pairs = zip(self.pieces[1:], partners(self.rounds[self.at]))
        else:
            pairs = [(self.pieces[0], peer) for peer in partners(self.joins[self.at - count])]
        self.got = [exchange(piece, *peer) for piece, peer in pairs]

    def take(self):
        count = len(self.rounds)
        parts = [self.pieces[0]] + self.got
        self.got = None
        self.at += 1
        if self.at < count:
            blocks = add_low(parts)
            pieces = 1 << len(self.rounds[self.at])
            size = blocks.shape[0] // pieces
            self.pieces = [blocks[at * size : (at + 1) * size] for at in range(pieces)]
        elif self.at == count:
            part = add_low(parts)
            mask = SPREAD
            while mask < lax.axis_size("ba"):
                part = add_low([part, exchange(part, "ba", mask)])
                mask *= 2
            self.pieces = [part]
        elif self.left():
            self.pieces = [jnp.concatenate(parts, axis=0)]
        else:
            self.pieces = parts

    def step(self):
        self.take()
        if self.left():
            self.send()

    def finish(self, rows, more=0):
        return plain_order(*self.pieces, self.own, rows, more)


def join(grads):
    both = Gradient.__new__(Gradient)
    both.rounds, both.joins, both.at, both.got = grads[0].rounds, grads[0].joins, grads[0].at, None
    both.pieces = [jnp.concatenate(pieces, axis=1) for pieces in zip(*[grad.pieces for grad in grads])]
    return both


def part_again(both, grads):
    rows = both.pieces[0].shape[1] // len(grads)
    for at, grad in enumerate(grads):
        grad.at, grad.got = both.at, None
        grad.pieces = [piece[:, at * rows : (at + 1) * rows] for piece in both.pieces]


def arrive(grads, *values):
    flat = [got for grad in grads for got in grad.got]
    held = list(tie(*values, *flat))
    rest = held[len(values) :]
    for grad in grads:
        grad.got, rest = rest[: len(grad.got)], rest[len(grad.got) :]
    return held[: len(values)]


LOW = jnp.bfloat16
WIDE = jnp.float32
TAPS = 3
SMEM = pltpu.SMEM


def dot(one, two):
    return jnp.dot(one, two, preferred_element_type=WIDE)


def dot_nt(one, two):
    return lax.dot_general(one, two, (((1,), (1,)), ((), ())), preferred_element_type=WIDE)


def dot_tn(one, two):
    return lax.dot_general(one, two, (((0,), (0,)), ((), ())), preferred_element_type=WIDE)


def iota(shape, axis):
    return lax.broadcasted_iota(jnp.int32, shape, axis)


def silu(half):
    return half * jnp.tanh(half) + half


def silu_pair(half):
    gate = jnp.tanh(half)
    value = half * gate + half
    return value, (1.0 + gate) + value * (1.0 - gate)


def fold(values):
    rows, width = values.shape
    return jnp.sum(values.reshape(rows // 8, 8, width), axis=0)


def close(partial):
    return jnp.sum(partial, axis=0, keepdims=True)


def spans(rows, size):
    return [slice(at, at + size) for at in range(0, rows, size)]


def over(values, size):
    assert size & (size - 1) == 0
    return jnp.right_shift(values, size.bit_length() - 1), jnp.bitwise_and(values, size - 1)


def parity_order(image_rows, cols, axis=0):
    pixels = image_rows * cols
    half_cols = cols // 2
    line = (pixels, 1) if axis == 0 else (1, pixels)
    plane, inside = over(iota(line, axis), pixels // 4)
    row, col = over(inside, half_cols)
    row_parity, col_parity = over(plane, 2)
    pixel = (2 * row + row_parity) * cols + 2 * col + col_parity
    return (iota((pixels, pixels), 1 - axis) == pixel).astype(WIDE).astype(LOW)


def halo_order(images, cols):
    count = images * cols
    half_cols = cols // 2
    parity, inside = over(iota((count, 1), 0), count // 2)
    image, col = over(inside, half_cols)
    return (iota((count, count), 1) == image * cols + 2 * col + parity).astype(WIDE).astype(LOW)


def shifted_sums(ref, valid_ref, base, planes, images, quarter):
    width = ref.shape[1]
    total = jnp.zeros((8, width), WIDE)
    square = jnp.zeros((8, width), WIDE)
    for image in range(images):
        first = jnp.zeros((8, width), WIDE)
        second = jnp.zeros((8, width), WIDE)
        for plane in range(planes):
            at = (plane * images + image) * quarter
            gap = ref[at : at + quarter, :] - base
            first += fold(gap)
            second += fold(gap * gap)
        total += first * valid_ref[image]
        square += second * valid_ref[image]
    return close(total), close(square)


def moments_of(sums, base, count):
    offset = sums[0:1, :] / count
    variance = jnp.maximum(sums[1:2, :] / count - offset * offset, 0.0)
    return base + offset, lax.rsqrt(variance + EPS)


def row_of(values, w):
    return dot(jnp.broadcast_to(values, (16, values.shape[1])).astype(LOW), w)[0:1, :]


def reduce_kernel(dims, lead, valid_ref, x_ref, w_ref, planes_ref, reduced_ref, stats_ref, sampled_ref, kept_ref, order_ref):
    images, image_rows, cols = dims
    pixels = image_rows * cols
    quarter = pixels // 4
    plane_rows = images * quarter
    group = images // lead
    valid = valid_ref[0]
    for image in range(1, images):
        valid = valid + valid_ref[image]
    step = pl.program_id(0)

    @pl.when(step == 0)
    def _():
        sampled_ref[...] = jnp.zeros(sampled_ref.shape, WIDE)
        order_ref[...] = parity_order(image_rows, cols)

    @pl.when(step < lead)
    def _():
        order = order_ref[...]
        total = jnp.zeros((8, x_ref.shape[1]), WIDE)
        for member in range(group):
            image = step * group + member
            moved = dot(order, x_ref[member * pixels : (member + 1) * pixels, :])
            total += fold(moved[:quarter, :]) * valid_ref[image]
            moved = moved.astype(LOW)
            for plane in range(4):
                part = moved[plane * quarter : (plane + 1) * quarter, :]
                planes_ref[plane, member] = part
                at = plane * plane_rows + pl.multiple_of(image * quarter, quarter)
                kept_ref[pl.ds(at, quarter), :] = part
        sampled_ref[...] += close(total) / (valid * float(quarter))

    @pl.when(step >= lead)
    def _():
        for plane in range(4):
            at = slice(plane * plane_rows, (plane + 1) * plane_rows)
            reduced_ref[at, :] = dot(kept_ref[at, :], w_ref[...])
        count = valid * float(pixels)
        base = reduced_ref[0:1, :]
        total, square = shifted_sums(reduced_ref, valid_ref, base, 4, images, quarter)
        stats_ref[0:1, :] = jnp.full(base.shape, count, WIDE)
        stats_ref[1:2, :] = base + total / count
        stats_ref[2:3, :] = jnp.maximum(square - total * (total / count), 0.0)


def turn_kernel(own_ref, value_ref, out_ref):
    parts, rows, _ = out_ref.shape
    turned = value_ref[...].T
    for part in range(parts):
        out_ref[jnp.bitwise_xor(own_ref[0], part)] = turned[part * rows : (part + 1) * rows, :]


def project_kernel(quarter, valid_ref, x_ref, w_ref, sampled_ref, out_ref, sums_ref):
    out_ref[...] = dot(x_ref[...], w_ref[...])
    base = row_of(sampled_ref[...], w_ref[...])
    images = out_ref.shape[0] // quarter
    total, square = shifted_sums(out_ref, valid_ref, base, 1, images, quarter)
    sums_ref[0:1, :] = total
    sums_ref[1:2, :] = square
    sums_ref[2:3, :] = base


def group_mask(width):
    rows, _ = over(iota((width, 1), 0), GW)
    cols, _ = over(iota((1, width), 1), GW)
    return (rows == cols).astype(WIDE).astype(LOW)


def block_weights(w_ref, mask, tap):
    width = w_ref.shape[1]
    part = w_ref[tap * GW : (tap + 1) * GW, :]
    return jnp.concatenate([part] * (width // GW), axis=0) * mask


def shift_columns(values, cols, by):
    rows, width = values.shape
    moved = pltpu.roll(values, by % rows, 0)
    edge = 0 if by > 0 else cols - 1
    _, col = over(iota((rows, 1), 0), cols)
    return jnp.where(col == edge, 0.0, moved)


def activate(values, mean, scale, shift):
    return silu((values - mean) * scale + shift)


def windows(planes, odd, halves):
    even_even, even_odd, even_moved = planes
    images, deep, half_cols, width = odd[0].shape
    tall = deep - 1

    def part(ref, at):
        return ref[:, at : at + tall, :, :].reshape(images * tall * half_cols, width)

    result = []
    for row_tap in range(TAPS):
        if row_tap == 1:
            result += [even_moved[...], even_even[...], even_odd[...]]
        else:
            at = 0 if row_tap == 0 else 1
            result += [part(odd[2], at), part(odd[0], at), part(odd[1], at)]
    return result


def store_hidden(dims, get, halo, even, odd):
    images, tall, half_cols = dims
    quarter = tall * half_cols
    for image in range(images):
        at = slice(image * quarter, (image + 1) * quarter)
        even[0][at, :] = get(0, image).astype(LOW)
        values = get(1, image)
        even[1][at, :] = values.astype(LOW)
        even[2][at, :] = shift_columns(values, half_cols, 1).astype(LOW)
        values = get(2, image)
        width = values.shape[1]
        odd[0][image, 1:, :, :] = values.astype(LOW).reshape(tall, half_cols, width)
        values = get(3, image)
        odd[1][image, 1:, :, :] = values.astype(LOW).reshape(tall, half_cols, width)
        odd[2][image, 1:, :, :] = shift_columns(values, half_cols, 1).astype(LOW).reshape(tall, half_cols, width)
    width = halo[0].shape[1]
    odd[0][:, 0, :, :] = halo[0].astype(LOW).reshape(images, half_cols, width)
    odd[1][:, 0, :, :] = halo[1].astype(LOW).reshape(images, half_cols, width)
    odd[2][:, 0, :, :] = shift_columns(halo[1], half_cols, 1).astype(LOW).reshape(images, half_cols, width)


def window_scratch(images, tall, half_cols, width):
    flat = pltpu.VMEM((images * tall * half_cols, width), LOW)
    deep = pltpu.VMEM((images, tall + 1, half_cols, width), LOW)
    return [flat, flat, flat, deep, deep, deep]


def conv_kernel(
    dims,
    scalar_ref,
    valid_ref,
    reduced_ref,
    moments_ref,
    affine_ref,
    halo_ref,
    reduce_ref,
    group_ref,
    grouped_ref,
    sums_ref,
    base_ref,
    first_ref,
    edge_ref,
    moved_ref,
    *buffers,
):
    images, tall, half_cols = dims
    quarter = tall * half_cols
    plane_rows = images * quarter
    width = reduced_ref.shape[1]

    @pl.when(pl.program_id(0) == 0)
    def _():
        moved_ref[...] = dot(halo_order(images, 2 * half_cols), halo_ref[...]).astype(LOW)

    mean = moments_ref[0:1, :]
    scale = 0.5 * affine_ref[0:1, :] * lax.rsqrt(moments_ref[1:2, :] / scalar_ref[0] + EPS)
    shift = 0.5 * affine_ref[1:2, :]
    edge = activate(dot(moved_ref[...], reduce_ref[...]), mean, scale, shift) * scalar_ref[2]
    edge_ref[...] = edge.astype(LOW)
    half = edge.shape[0] // 2

    def get(plane, image):
        at = plane * plane_rows + image * quarter
        return activate(reduced_ref[at : at + quarter, :], mean, scale, shift)

    even, odd = buffers[:3], buffers[3:]
    store_hidden(dims, get, (edge[:half], edge[half:]), even, odd)
    mask = group_mask(width)
    total = None
    for tap, window in enumerate(windows(even, odd, half_cols)):
        term = dot(window, block_weights(group_ref, mask, tap))
        total = term if total is None else total + term
    grouped_ref[...] = total
    kernel = group_ref[0:GW, :].astype(WIDE)
    for tap in range(1, TAPS * TAPS):
        kernel = kernel + group_ref[tap * GW : (tap + 1) * GW, :].astype(WIDE)
    kernel = jnp.concatenate([kernel.astype(LOW)] * (width // GW), axis=0) * mask
    base = row_of(silu(shift), kernel)
    total, square = shifted_sums(grouped_ref, valid_ref, base, 1, images, quarter)
    sums_ref[0:1, :] = total
    sums_ref[1:2, :] = square
    base_ref[...] = base
    for image in range(images):
        at = image * quarter
        first_ref[image * half_cols : (image + 1) * half_cols, :] = grouped_ref[at : at + half_cols, :].astype(LOW)


def expand_kernel(
    quarter,
    scalar_ref,
    valid_ref,
    grouped_ref,
    sums_two_ref,
    base_two_ref,
    affine_ref,
    w_ref,
    side_ref,
    hidden_ref,
    out_ref,
    sums_ref,
    base_ref,
):
    shift = 0.5 * affine_ref[1:2, :]

    @pl.when(pl.program_id(0) == 0)
    def _():
        mean, inv = moments_of(sums_two_ref[...], base_two_ref[...], scalar_ref[1])
        scale = 0.5 * affine_ref[0:1, :] * inv
        for span in spans(grouped_ref.shape[0], 16):
            hidden_ref[span, :] = activate(grouped_ref[span, :], mean, scale, shift).astype(LOW)

    out_ref[...] = dot(hidden_ref[...], w_ref[...])
    base = row_of(silu(shift), w_ref[...])
    images = out_ref.shape[0] // quarter
    total, square = shifted_sums(out_ref, valid_ref, base, 1, images, quarter)
    sums_ref[0:1, :] = total
    sums_ref[1:2, :] = square
    sums_ref[2:4, :] = side_ref[0:2, :]
    base_ref[0:1, :] = base
    base_ref[1:2, :] = side_ref[2:3, :]


def tail_moments(sums_ref, base_ref, count):
    return (
        *moments_of(sums_ref[0:2, :], base_ref[0:1, :], count),
        *moments_of(sums_ref[2:4, :], base_ref[1:2, :], count),
    )


def tail_halves(moments, affine):
    return (
        0.5 * affine[0:1, :] * moments[1],
        0.5 * affine[2:3, :] * moments[3],
        0.5 * (affine[1:2, :] + affine[3:4, :]),
    )


def output_kernel(
    size,
    scalar_ref,
    valid_ref,
    expanded_ref,
    projected_ref,
    stats_ref,
    base_ref,
    affine_ref,
    cot_ref,
    out_ref,
    sums_ref,
):
    rows, width = out_ref.shape
    quarter = rows // valid_ref.shape[0]
    totals = [jnp.zeros((8, width), WIDE) for _ in range(3)]
    moments = tail_moments(stats_ref, base_ref, scalar_ref[1])
    one, two, both = tail_halves(moments, affine_ref[...])
    for span in spans(rows, size):
        first = expanded_ref[span, :] - moments[0]
        second = projected_ref[span, :] - moments[2]
        valid = valid_ref[span.start // quarter]
        value, slope = silu_pair(first * one + second * two + both)
        out_ref[span, :] = (valid * value).astype(LOW)
        upstream = (cot_ref[span, :].astype(WIDE) * (0.5 * valid)) * slope
        totals[0] += fold(upstream)
        totals[1] += fold(upstream * first)
        totals[2] += fold(upstream * second)
    sums_ref[0:1, :] = close(totals[0])
    sums_ref[1:2, :] = close(totals[1]) * moments[1]
    sums_ref[2:3, :] = close(totals[2]) * moments[3]


def weights_kernel(
    size,
    scalar_ref,
    valid_ref,
    expanded_ref,
    projected_ref,
    stats_ref,
    base_ref,
    affine_ref,
    sums_ref,
    cot_ref,
    hidden_ref,
    sampled_ref,
    d_expanded_ref,
    d_projected_ref,
    expand_low_ref,
    expand_high_ref,
    proj_low_ref,
    proj_high_ref,
):
    rows, width = d_expanded_ref.shape
    quarter = rows // valid_ref.shape[0]
    count = scalar_ref[1]
    moments = tail_moments(stats_ref, base_ref, count)
    affine = affine_ref[...]
    one, two, both = tail_halves(moments, affine)
    sums = sums_ref[...] / count
    gain_one = affine[0:1, :] * moments[1]
    gain_two = affine[2:3, :] * moments[3]
    pull_one = gain_one * moments[1] * sums[1:2, :]
    pull_two = gain_two * moments[3] * sums[2:3, :]
    for span in spans(rows, size):
        first = expanded_ref[span, :] - moments[0]
        second = projected_ref[span, :] - moments[2]
        valid = valid_ref[span.start // quarter]
        _, slope = silu_pair(first * one + second * two + both)
        upstream = (cot_ref[span, :].astype(WIDE) * 0.5) * slope - sums[0:1, :]
        d_expanded_ref[span, :] = (upstream * (gain_one * valid) - first * (pull_one * valid)).astype(LOW)
        d_projected_ref[span, :] = (upstream * (gain_two * valid) - second * (pull_two * valid)).astype(LOW)
    store_halves(sampled_ref[...], d_projected_ref[...], proj_low_ref, proj_high_ref)
    store_halves(hidden_ref[...], d_expanded_ref[...], expand_low_ref, expand_high_ref)


def store_halves(turned, grads, low_ref, high_ref):
    half = low_ref.shape[0]
    for at, ref in ((0, low_ref), (half, high_ref)):
        left = turned[at : at + half].reshape(half * turned.shape[1], turned.shape[2])
        ref[...] = dot(left, grads).astype(LOW).reshape(ref.shape)


def back_two_kernel(
    size, dims, scalar_ref, d_ref, w_ref, grouped_ref, sums_two_ref, base_two_ref, affine_ref, out_ref, sums_ref, first_ref
):
    rows, width = out_ref.shape
    images, tall, half_cols = dims
    mean, inv = moments_of(sums_two_ref[...], base_two_ref[...], scalar_ref[1])
    out_ref[...] = dot_nt(d_ref[...], w_ref[...])
    totals = [jnp.zeros((8, width), WIDE) for _ in range(2)]
    scale = 0.5 * affine_ref[0:1, :] * inv
    shift = 0.5 * affine_ref[1:2, :]
    for span in spans(rows, size):
        gap = grouped_ref[span, :] - mean
        _, slope = silu_pair(gap * scale + shift)
        grad = (out_ref[span, :] * 0.5) * slope
        out_ref[span, :] = grad
        totals[0] += fold(grad)
        totals[1] += fold(grad * gap)
    sums_ref[0:1, :] = close(totals[0])
    sums_ref[1:2, :] = close(totals[1]) * inv
    for image in range(images):
        at = image * tall * half_cols
        first_ref[image * half_cols : (image + 1) * half_cols, :] = out_ref[at : at + half_cols, :].astype(LOW)


def side_kernel(d_ref, w_ref, out_ref):
    out_ref[...] = dot_nt(d_ref[...], w_ref[...])


def norm_back_values(grad, values, mean, pull, valid):
    gain, offset, along = pull
    return (grad - offset) * (gain * valid) - (values - mean) * (along * valid)


def norm_pull(gain, inv, sums, count):
    return gain * inv, sums[0:1, :] / count, gain * inv * inv * (sums[1:2, :] / count)


def conv_back_kernel(
    dims,
    scalar_ref,
    own_ref,
    valid_ref,
    grad_ref,
    grouped_ref,
    below_grad_ref,
    below_grouped_ref,
    sums_two_ref,
    base_two_ref,
    affine_two_ref,
    grads_two_ref,
    reduced_ref,
    edge_ref,
    moments_one_ref,
    affine_one_ref,
    group_ref,
    out_ref,
    sums_ref,
    grad_group_ref,
    *buffers,
):
    images, tall, half_cols = dims
    quarter = tall * half_cols
    plane_rows = images * quarter
    width = reduced_ref.shape[1]
    even, odd, below = buffers[:3], buffers[3:6], buffers[6:8]
    count_in, count_out = scalar_ref[0], scalar_ref[1]

    mean, inv = moments_of(sums_two_ref[...], base_two_ref[...], count_out)
    pull = norm_pull(affine_two_ref[0:1, :], inv, grads_two_ref[...], count_out)
    for image in range(images):
        at = slice(image * quarter, (image + 1) * quarter)
        values = norm_back_values(grad_ref[at, :], grouped_ref[at, :], mean, pull, valid_ref[image])
        below[0][image, :tall, :, :] = values.astype(LOW).reshape(tall, half_cols, width)
        below[1][image, :tall, :, :] = (
            shift_columns(values, half_cols, -1).astype(LOW).reshape(tall, half_cols, width)
        )
        at = slice(image * half_cols, (image + 1) * half_cols)
        values = norm_back_values(
            below_grad_ref[at, :].astype(WIDE),
            below_grouped_ref[at, :].astype(WIDE),
            mean,
            pull,
            valid_ref[image] * scalar_ref[3],
        )
        below[0][image, tall, :, :] = values.astype(LOW)
        below[1][image, tall, :, :] = shift_columns(values, half_cols, -1).astype(LOW)

    def part(ref, at):
        return ref[:, at : at + tall, :, :].reshape(plane_rows, width)

    mask = group_mask(width)
    half_mask = mask * jnp.asarray(0.5, LOW)
    weights = [block_weights(group_ref, half_mask, tap) for tap in range(TAPS * TAPS)]
    here, left = part(below[0], 0), part(below[1], 0)
    next_here, next_left = part(below[0], 1), part(below[1], 1)
    out_ref[0:plane_rows, :] = dot_nt(here, weights[4])
    out_ref[plane_rows : 2 * plane_rows, :] = dot_nt(here, weights[5]) + dot_nt(left, weights[3])
    out_ref[2 * plane_rows : 3 * plane_rows, :] = dot_nt(here, weights[7]) + dot_nt(next_here, weights[1])
    out_ref[3 * plane_rows : 4 * plane_rows, :] = (
        dot_nt(here, weights[8])
        + dot_nt(left, weights[6])
        + dot_nt(next_here, weights[2])
        + dot_nt(next_left, weights[0])
    )

    mean_one = moments_one_ref[0:1, :]
    inv_one = lax.rsqrt(moments_one_ref[1:2, :] / count_in + EPS)
    scale = 0.5 * affine_one_ref[0:1, :] * inv_one
    shift = 0.5 * affine_one_ref[1:2, :]
    totals = [jnp.zeros((8, width), WIDE) for _ in range(2)]

    def get(plane, image):
        start = plane * plane_rows + image * quarter
        parts = []
        for span in spans(quarter, 32):
            at = slice(start + span.start, start + span.stop)
            gap = reduced_ref[at, :] - mean_one
            value, slope = silu_pair(gap * scale + shift)
            grad = out_ref[at, :] * slope
            out_ref[at, :] = grad
            totals[0] += fold(grad)
            totals[1] += fold(grad * gap)
            parts.append(value)
        return jnp.concatenate(parts, axis=0)

    half = edge_ref.shape[0] // 2
    edge = edge_ref[...].astype(WIDE)
    store_hidden(dims, get, (edge[:half], edge[half:]), even, odd)
    sums_ref[0:1, :] = close(totals[0])
    sums_ref[1:2, :] = close(totals[1]) * inv_one
    turned = here.T
    picked = jnp.bitwise_xor(iota((GW, 1), 0), own_ref[0])
    _, channel = over(iota((1, width), 1), GW)
    one_hot = (channel == picked).astype(WIDE).astype(LOW)
    for tap, window in enumerate(windows(even, odd, half_cols)):
        full = dot(turned, window).astype(LOW) * mask
        grad_group_ref[tap] = dot_nt(one_hot, full).astype(LOW)


def reduced_back_kernel(
    size,
    scalar_ref,
    valid_ref,
    grad_ref,
    reduced_ref,
    moments_ref,
    affine_ref,
    sums_ref,
    *refs,
):
    planes_refs, (d_ref, low_ref, high_ref) = refs[:4], refs[4:]
    rows, width = d_ref.shape
    images = valid_ref.shape[0]
    quarter = rows // (4 * images)
    mean = moments_ref[0:1, :]
    inv = lax.rsqrt(moments_ref[1:2, :] / scalar_ref[0] + EPS)
    pull = norm_pull(affine_ref[0:1, :], inv, sums_ref[...], scalar_ref[0])
    for span in spans(rows, size):
        valid = valid_ref[span.start // quarter % images]
        d_ref[span, :] = norm_back_values(grad_ref[span, :], reduced_ref[span, :], mean, pull, valid).astype(LOW)
    half = low_ref.shape[0]
    for at, ref in ((0, low_ref), (half, high_ref)):
        total = None
        for plane, planes_ref in enumerate(planes_refs):
            deep = planes_ref.shape[2]
            left = planes_ref[at : at + half].reshape(half * planes_ref.shape[1], deep)
            term = dot(left, d_ref[plane * deep : (plane + 1) * deep, :])
            total = term if total is None else total + term
        ref[...] = total.astype(LOW).reshape(ref.shape)


def images_back_kernel(dims, d_ref, w_ref, side_ref, *refs):
    out_ref, order_ref = refs[-2:]
    image_rows, cols = dims
    pixels = image_rows * cols
    quarter = pixels // 4

    @pl.when(pl.program_id(0) == 0)
    def _():
        order_ref[...] = parity_order(image_rows, cols, 1)

    values = dot_nt(d_ref[...].reshape(pixels, d_ref.shape[-1]), w_ref[...])
    first = values[:quarter] + side_ref[...]
    planes = jnp.concatenate([first, values[quarter:]], axis=0).astype(LOW)
    out_ref[...] = dot(order_ref[...], planes).astype(LOW)


def whole(shape):
    return pl.BlockSpec(shape, lambda i: (0,) * len(shape))


def wide_cols(rows, width):
    return pl.BlockSpec((rows, width), lambda i: (0, i))


SCALARS = pl.BlockSpec(memory_space=pltpu.SMEM)


def place(shape, kind):
    if math.prod(shape) * jnp.dtype(kind).itemsize >= 4 << 20:
        return pltpu.HBM(shape, kind)
    return jax.ShapeDtypeStruct(shape, kind)


def call(kernel, grid, in_specs, out_specs, out_shapes, cost, scratch=()):
    flops, moved = cost
    return pl.pallas_call(
        kernel,
        grid=(grid,),
        in_specs=in_specs,
        out_specs=out_specs,
        out_shape=[place(shape, kind) for shape, kind in out_shapes],
        scratch_shapes=list(scratch),
        compiler_params=pltpu.CompilerParams(vmem_limit_bytes=VMEM_LIMIT),
        cost_estimate=pl.CostEstimate(flops=flops, bytes_accessed=moved, transcendentals=0),
    )


def hbm(value):
    return pltpu.with_memory_space_constraint(value, pltpu.HBM)


def per_device(
    images_in,
    reduce_w,
    gain_one,
    shift_one,
    group_w,
    gain_two,
    shift_two,
    expand_w,
    gain_three,
    shift_three,
    proj_w,
    gain_proj,
    shift_proj,
    valid_mask,
    cotangent,
):
    images, image_rows, cols, chans = images_in.shape
    mid = reduce_w.shape[1]
    wide = expand_w.shape[1]
    tall, half_cols = image_rows // 2, cols // 2
    quarter = tall * half_cols
    rows = images * quarter
    pixels = images * image_rows * cols
    block = 256
    steps = mid // block
    strip = 512
    strips = wide // strip

    valid = valid_mask.astype(WIDE)
    row_index = lax.axis_index("ha")
    has_upper = (row_index > 0).astype(WIDE)
    has_lower = (row_index < lax.axis_size("ha") - 1).astype(WIDE)
    plain = ([CORE], [SIDE_ONE], [SIDE_TWO], [DEEP_ONE, DEEP_TWO])
    swapped = ([CORE], [SIDE_TWO], [SIDE_ONE], [DEEP_ONE, DEEP_TWO])
    short = ([CORE], [SIDE_TWO, SIDE_ONE], [DEEP_ONE, DEEP_TWO])
    own_one, own_two = own_part(plain).reshape(1), own_part(swapped).reshape(1)
    affine_one = jnp.stack([gain_one, shift_one])
    affine_two = jnp.stack([gain_two, shift_two])
    affine_out = jnp.stack([gain_three, shift_three, gain_proj, shift_proj])
    taps = TAPS * TAPS * GW
    group_flat = group_w.reshape(taps, mid)
    rounds = sum_plan(("ba", "ha"))
    back_rounds = sum_plan(("ha", "ba"))

    halo_images = shifted(images_in[:, -1], "ha", 1).reshape(images * cols, chans)
    lead = images // 2
    planes, reduced, stats, sampled = call(
        functools.partial(reduce_kernel, (images, image_rows, cols), lead),
        lead + steps,
        [
            SCALARS,
            pl.BlockSpec((pixels // lead, chans), lambda i: (jnp.minimum(i, lead - 1), 0)),
            pl.BlockSpec((chans, block), lambda i: (0, jnp.maximum(i - lead, 0))),
        ],
        [
            pl.BlockSpec((4, images // lead, quarter, chans), lambda i: (0, jnp.minimum(i, lead - 1), 0, 0)),
            pl.BlockSpec((pixels, block), lambda i: (0, jnp.maximum(i - lead, 0))),
            pl.BlockSpec((3, block), lambda i: (0, jnp.maximum(i - lead, 0))),
            whole((1, chans)),
        ],
        [((4, images, quarter, chans), LOW), ((pixels, mid), WIDE), ((3, mid), WIDE), ((1, chans), WIDE)],
        (2 * pixels * chans * (mid + 256), 20 << 20),
        [pltpu.VMEM((pixels, chans), LOW), pltpu.VMEM((image_rows * cols, image_rows * cols), LOW)],
    )(valid, hbm(images_in.reshape(pixels, chans)), hbm(reduce_w))
    planes = planes.reshape(pixels, chans)
    stats, halo_images = tie(jnp.concatenate([stats, sampled]), halo_images)
    stats = mesh_moments(stats, rounds)

    def turn(value, at, own):
        width = value.shape[1]
        return call(
            turn_kernel,
            1,
            [SCALARS, pl.BlockSpec((rows, width), lambda i: (at or 0, 0))],
            [whole((PARTS, width // PARTS, rows))],
            [((PARTS, width // PARTS, rows), LOW)],
            (0, 2 << 20),
        )(own, value if at is None else hbm(value))[0]

    planes_turned = [turn(planes, plane, own_two) for plane in range(4)]
    stats, *planes_turned = tie(stats, *planes_turned)
    count_in, moments_one, sampled_mean = stats[0, 0], stats[1:3], stats[3:4]
    scalars = jnp.stack([count_in, count_in / 4.0, has_upper, has_lower])

    grouped, sums, base_two, first_row, edge = call(
        functools.partial(conv_kernel, (images, tall, half_cols)),
        steps,
        [
            SCALARS,
            SCALARS,
            wide_cols(pixels, block),
            wide_cols(2, block),
            wide_cols(2, block),
            whole((images * cols, chans)),
            wide_cols(chans, block),
            wide_cols(taps, block),
        ],
        [
            wide_cols(rows, block),
            wide_cols(2, block),
            wide_cols(1, block),
            wide_cols(images * half_cols, block),
            wide_cols(images * cols, block),
        ],
        [
            ((rows, mid), WIDE),
            ((2, mid), WIDE),
            ((1, mid), WIDE),
            ((images * half_cols, mid), LOW),
            ((images * cols, mid), LOW),
        ],
        (2 * rows * mid * 9 * 256, 14 << 20),
        [pltpu.VMEM((images * cols, chans), LOW)] + window_scratch(images, tall, half_cols, block),
    )(scalars, valid, hbm(reduced), moments_one, affine_one, halo_images, hbm(reduce_w), group_flat)
    sums_two = mesh_sum(sums, rounds)
    below_grouped = shifted(first_row, "ha", -1)
    sums_two, below_grouped = tie(sums_two, below_grouped)
    projected, side = call(
        functools.partial(project_kernel, quarter),
        strips,
        [SCALARS, whole((rows, chans)), wide_cols(chans, strip), whole((1, chans))],
        [wide_cols(rows, strip), wide_cols(3, strip)],
        [((rows, wide), WIDE), ((3, wide), WIDE)],
        (2 * rows * chans * wide, 10 << 20),
    )(valid, hbm(planes), proj_w, sampled_mean)

    hidden_two, expanded, sums, base_out = call(
        functools.partial(expand_kernel, quarter),
        strips,
        [
            SCALARS,
            SCALARS,
            whole((rows, mid)),
            whole((2, mid)),
            whole((1, mid)),
            whole((2, mid)),
            wide_cols(mid, strip),
            wide_cols(3, strip),
        ],
        [whole((rows, mid)), wide_cols(rows, strip), wide_cols(4, strip), wide_cols(2, strip)],
        [((rows, mid), LOW), ((rows, wide), WIDE), ((4, wide), WIDE), ((2, wide), WIDE)],
        (2 * rows * mid * wide, 12 << 20),
    )(scalars, valid, grouped, sums_two, base_two, affine_two, expand_w, side)
    stats_out = mesh_sum(sums, rounds)
    stats_out, hidden_turned = tie(stats_out, turn(hidden_two, None, own_one))

    cot = cotangent.reshape(rows, wide)
    output, sums = call(
        functools.partial(output_kernel, 16),
        strips,
        [
            SCALARS,
            SCALARS,
            wide_cols(rows, strip),
            wide_cols(rows, strip),
            wide_cols(4, strip),
            wide_cols(2, strip),
            wide_cols(4, strip),
            wide_cols(rows, strip),
        ],
        [wide_cols(rows, strip), wide_cols(3, strip)],
        [((rows, wide), LOW), ((3, wide), WIDE)],
        (20 * rows * wide, 12 << 20),
    )(scalars, valid, hbm(expanded), hbm(projected), stats_out, base_out, affine_out, cot)
    sums_out = mesh_sum(sums, rounds)

    def halves_specs(height, width):
        return [pl.BlockSpec((PARTS // 2, height // PARTS, width), lambda i: (0, 0, i))] * 2

    def halves_shapes(height, width):
        return [((PARTS // 2, height // PARTS, width), LOW)] * 2

    d_expanded, d_projected, *halves = call(
        functools.partial(weights_kernel, 16),
        strips,
        [
            SCALARS,
            SCALARS,
            wide_cols(rows, strip),
            wide_cols(rows, strip),
            wide_cols(4, strip),
            wide_cols(2, strip),
            wide_cols(4, strip),
            wide_cols(3, strip),
            wide_cols(rows, strip),
            whole((PARTS, mid // PARTS, rows)),
            whole((PARTS, chans // PARTS, rows)),
        ],
        [wide_cols(rows, strip), wide_cols(rows, strip)] + halves_specs(mid, strip) + halves_specs(chans, strip),
        [((rows, wide), LOW), ((rows, wide), LOW)] + halves_shapes(mid, wide) + halves_shapes(chans, wide),
        (4 * rows * mid * wide, 24 << 20),
    )(
        scalars,
        valid,
        hbm(expanded),
        hbm(projected),
        stats_out,
        base_out,
        affine_out,
        sums_out,
        cot,
        hidden_turned,
        planes_turned[0],
    )
    expand_sum = Gradient(halves[:2], plain)
    proj_sum = Gradient(halves[2:], swapped)
    pair = [expand_sum, proj_sum]
    for grad in pair:
        grad.send()

    grad_two, sums, first_row = call(
        functools.partial(back_two_kernel, 16, (images, tall, half_cols)),
        steps,
        [
            SCALARS,
            whole((rows, wide)),
            pl.BlockSpec((block, wide), lambda i: (i, 0)),
            wide_cols(rows, block),
            wide_cols(2, block),
            wide_cols(1, block),
            wide_cols(2, block),
        ],
        [wide_cols(rows, block), wide_cols(2, block), wide_cols(images * half_cols, block)],
        [((rows, mid), WIDE), ((2, mid), WIDE), ((images * half_cols, mid), LOW)],
        (2 * rows * mid * wide, 10 << 20),
    )(scalars, d_expanded, expand_w, grouped, sums_two, base_two, affine_two)
    sums = mesh_sum(sums, back_rounds[:1])
    sums, first_row = arrive(pair, sums, first_row)
    below_grad = shifted(first_row, "ha", -1)
    sums = mesh_sum(sums, back_rounds[1:2])
    sums, below_grad = arrive(pair, sums, below_grad)
    for grad in pair:
        grad.step()
    grads_two = mesh_sum(sums, back_rounds[2:])
    (d_projected,) = tie(d_projected)
    side_grad = call(
        side_kernel,
        1,
        [whole((rows, wide)), whole((chans, wide))],
        [whole((rows, chans))],
        [((rows, chans), WIDE)],
        (2 * rows * chans * wide, 8 << 20),
    )(d_projected, proj_w)[0]

    deep = pltpu.VMEM((images, tall + 1, half_cols, block), LOW)
    grads_two, side_grad = tie(grads_two, side_grad)
    grad_one, sums, parts_group = call(
        functools.partial(conv_back_kernel, (images, tall, half_cols)),
        steps,
        [
            SCALARS,
            SCALARS,
            SCALARS,
            wide_cols(rows, block),
            wide_cols(rows, block),
            wide_cols(images * half_cols, block),
            wide_cols(images * half_cols, block),
            wide_cols(2, block),
            wide_cols(1, block),
            wide_cols(2, block),
            wide_cols(2, block),
            wide_cols(pixels, block),
            wide_cols(images * cols, block),
            wide_cols(2, block),
            wide_cols(2, block),
            wide_cols(taps, block),
        ],
        [wide_cols(pixels, block), wide_cols(2, block), pl.BlockSpec((TAPS * TAPS, GW, block), lambda i: (0, 0, i))],
        [((pixels, mid), WIDE), ((2, mid), WIDE), ((TAPS * TAPS, GW, mid), LOW)],
        (4 * rows * mid * 9 * 256, 24 << 20),
        window_scratch(images, tall, half_cols, block) + [deep, deep],
    )(
        scalars,
        own_two,
        valid,
        grad_two,
        grouped,
        below_grad,
        below_grouped,
        sums_two,
        base_two,
        affine_two,
        grads_two,
        hbm(reduced),
        edge,
        moments_one,
        affine_one,
        group_flat,
    )
    parts_group = jnp.pad(jnp.transpose(parts_group, (1, 0, 2)), ((0, 0), (0, 16 - TAPS * TAPS), (0, 0)))
    (sums,) = arrive(pair, sums)
    sums = mesh_sum(sums, back_rounds[:1])
    (sums,) = arrive(pair, sums)
    for grad in pair:
        grad.step()
    grads_one = mesh_sum(sums, back_rounds[1:])
    grads_one, parts_group = arrive(pair, grads_one, parts_group)
    for grad in pair:
        grad.take()
    both = join(pair)
    both.send()

    d_reduced, *halves = call(
        functools.partial(reduced_back_kernel, 16),
        steps,
        [
            SCALARS,
            SCALARS,
            wide_cols(pixels, block),
            wide_cols(pixels, block),
            wide_cols(2, block),
            wide_cols(2, block),
            wide_cols(2, block),
        ]
        + [whole((PARTS, chans // PARTS, rows))] * 4,
        [wide_cols(pixels, block)] + halves_specs(chans, block),
        [((pixels, mid), LOW)] + halves_shapes(chans, mid),
        (2 * pixels * mid * chans, 26 << 20),
    )(scalars, valid, hbm(grad_one), hbm(reduced), moments_one, affine_one, grads_one, *planes_turned)
    d_reduced, *halves = arrive([both], d_reduced, *halves)
    parts_group = [parts_group[: PARTS // 2], parts_group[PARTS // 2 :]]
    halves = [jnp.concatenate(members, axis=1) for members in zip(halves, parts_group)]
    reduce_sum = Gradient(halves, short)
    reduce_sum.send()

    def images_back(d_part, side_part, half, before):
        part = images // 2
        kept = [] if before is None else [before]
        return pl.pallas_call(
            functools.partial(images_back_kernel, (image_rows, cols)),
            grid=(part,),
            in_specs=[
                pl.BlockSpec((4, None, quarter, mid), lambda i: (0, i + half * part, 0, 0)),
                whole((chans, mid)),
                pl.BlockSpec((quarter, chans), lambda i: (i + half * part, 0)),
            ]
            + [pl.BlockSpec(memory_space=pl.ANY)] * len(kept),
            out_specs=pl.BlockSpec((None, image_rows * cols, chans), lambda i: (i + half * part, 0, 0)),
            out_shape=place((images, image_rows * cols, chans), LOW),
            input_output_aliases={3: 0} if kept else {},
            scratch_shapes=[pltpu.VMEM((image_rows * cols, image_rows * cols), LOW)],
            compiler_params=pltpu.CompilerParams(vmem_limit_bytes=VMEM_LIMIT),
            cost_estimate=pl.CostEstimate(
                flops=pixels * mid * chans, bytes_accessed=8 << 20, transcendentals=0
            ),
        )(d_part, reduce_w, side_part, *kept)

    d_reduced = d_reduced.reshape(4, images, quarter, mid)
    both.step()
    (d_reduced,) = arrive([reduce_sum], d_reduced)
    reduce_sum.step()
    grad_images = images_back(d_reduced, side_grad, 0, None)
    grad_images, both.got[0] = tie(grad_images, both.got[0])
    grad_images = images_back(d_reduced, side_grad, 1, grad_images)
    (grad_images,) = arrive([both, reduce_sum], grad_images)
    both.take()
    part_again(both, pair)
    for grad in pair:
        grad.send()
    everyone = pair + [reduce_sum]
    reduce_sum.step()
    while pair[0].left() > 1:
        arrive(everyone)
        for grad in everyone:
            grad.step()
    done = []
    for grad, width in zip(pair, (mid, chans)):
        if done:
            done[0] = arrive([grad], done[0])[0]
        grad.take()
        done += grad.finish(width // PARTS)
    grad_expand, grad_proj = done
    (grad_proj,) = arrive([reduce_sum], grad_proj)
    reduce_sum.step()
    while reduce_sum.left():
        reduce_sum.step()
    grad_reduce, grad_group = reduce_sum.finish(chans // PARTS, TAPS * TAPS)
    return (
        output.reshape(cotangent.shape),
        grad_images.reshape(images_in.shape),
        grad_reduce.reshape(reduce_w.shape),
        grads_one[1],
        grads_one[0],
        grad_group.reshape(group_w.shape),
        grads_two[1],
        grads_two[0],
        grad_expand.reshape(expand_w.shape),
        sums_out[1],
        sums_out[0],
        grad_proj.reshape(proj_w.shape),
        sums_out[2],
        sums_out[0],
    )


def solution(mesh):
    split = P("ba", "ha", None, None)
    rest = (P(),) * 12
    return jax.shard_map(
        per_device,
        mesh=mesh,
        in_specs=(split,) + rest + (P("ba"), split),
        out_specs=(split, split) + rest,
        check_vma=False,
    )
```

```python
import functools
import math

import jax
import jax.numpy as jnp
from jax import lax
from jax.experimental import pallas as pl
from jax.experimental.pallas import tpu as pltpu
from jax.sharding import PartitionSpec as P

GW = 32
EPS = 1e-05
VMEM_LIMIT = 40 * 1024 * 1024


def shifted(value, axis, by):
    peers = lax.axis_size(axis)
    pairs = [(i, i + by) for i in range(peers) if 0 <= i + by < peers]
    return lax.ppermute(value, axis, pairs)


def exchange(value, axis, mask):
    peers = lax.axis_size(axis)
    return lax.ppermute(value, axis, [(i, i ^ mask) for i in range(peers)])


def sum_plan(axes):
    rounds = []
    for axis in axes:
        bits = [1 << b for b in range(lax.axis_size(axis).bit_length() - 1)]
        if axis == "ba" and bits:
            rounds.append((axis, bits[:1]))
            bits = bits[1:]
        while bits:
            rounds.append((axis, bits[:2]))
            bits = bits[2:]
    return rounds


def meet(value, axis, masks):
    offsets = [0]
    for mask in masks:
        offsets = offsets + [o ^ mask for o in offsets]
    return [value] + [exchange(value, axis, o) for o in offsets[1:]]


def add_round(value, axis, masks):
    parts = meet(value, axis, masks)
    while len(parts) > 1:
        parts = [parts[i] + parts[i + 1] for i in range(0, len(parts), 2)]
    return parts[0]


def mesh_sum(value, rounds):
    for axis, masks in rounds:
        value = add_round(value, axis, masks)
    return value


def merge(one, two):
    count = one[0] + two[0]
    gap = two[1] - one[1]
    return (
        count,
        (one[0] * one[1] + two[0] * two[1]) / count,
        one[2] + two[2] + gap * gap * (one[0] * two[0] / count),
        (one[0] * one[3] + two[0] * two[3]) / count,
    )


def mesh_moments(packed, rounds):
    for axis, masks in rounds:
        parts = [tuple(part) for part in meet(packed, axis, masks)]
        while len(parts) > 1:
            parts = [merge(parts[i], parts[i + 1]) for i in range(0, len(parts), 2)]
        packed = jnp.stack(parts[0])
    return packed


PARTS = 32
SPREAD = 8
CORE, SIDE_ONE, SIDE_TWO, DEEP_ONE, DEEP_TWO = ("ba", 1), ("ha", 1), ("ha", 2), ("ba", 2), ("ba", 4)


def own_part(rounds):
    index = jnp.int32(0)
    for axis, mask in [bit for bits in rounds for bit in bits]:
        bit = jnp.bitwise_and(lax.axis_index(axis), mask) // mask
        index = index * 2 + bit.astype(jnp.int32)
    return index


def partners(bits):
    masks = [0]
    for _, mask in bits:
        masks = [old ^ new for old in masks for new in (0, mask)]
    return [(bits[0][0], mask) for mask in masks[1:]]


def spread_kernel(order, own_ref, low_ref, high_ref, *out_refs):
    half = low_ref.shape[0]
    rows = out_refs[0].shape[1]
    for part in range(2 * half):
        at = jnp.bitwise_xor(own_ref[0], order[part])
        ref = low_ref if part < half else high_ref
        out_refs[0][at] = ref[part % half, :rows, :].astype(jnp.float32)
        if len(out_refs) > 1:
            more = out_refs[1].shape[0]
            extra = ref[part % half, rows : rows + more, :].astype(jnp.float32)
            for row in range(more):
                out_refs[1][row, pl.ds(at, 1), :] = extra[row : row + 1, :]


def plain_order(low, high, own, order, rows, more):
    half, deep, cols = low.shape
    width = 512
    shapes = [(2 * half, rows)] + ([(more, 2 * half)] if more else [])
    block = pl.BlockSpec((half, deep, width), lambda i: (0, 0, i))
    return pl.pallas_call(
        functools.partial(spread_kernel, order),
        grid=(cols // width,),
        in_specs=[pl.BlockSpec(memory_space=pltpu.SMEM), block, block],
        out_specs=[pl.BlockSpec(shape + (width,), lambda i: (0, 0, i)) for shape in shapes],
        out_shape=[jax.ShapeDtypeStruct(shape + (cols,), jnp.float32) for shape in shapes],
        compiler_params=pltpu.CompilerParams(vmem_limit_bytes=VMEM_LIMIT),
        cost_estimate=pl.CostEstimate(flops=0, bytes_accessed=12 * low.size, transcendentals=0),
    )(own.reshape(1), low, high)


def add_low(parts):
    total = parts[0].astype(jnp.float32)
    for part in parts[1:]:
        total = total + part.astype(jnp.float32)
    return total.astype(jnp.bfloat16)


def tie(*values):
    return lax.optimization_barrier(values)


class Gradient:
    def __init__(self, pieces, rounds, joins=None):
        self.pieces, self.rounds, self.own = list(pieces), rounds, own_part(rounds)
        self.joins = tuple(reversed(joins or rounds))
        self.at = 0
        self.got = None

    def left(self):
        return len(self.rounds) + len(self.joins) - self.at

    def send(self):
        count = len(self.rounds)
        if self.at < count:
            pairs = zip(self.pieces[1:], partners(self.rounds[self.at]))
        else:
            pairs = [(self.pieces[0], peer) for peer in partners(self.joins[self.at - count])]
        self.got = [exchange(piece, *peer) for piece, peer in pairs]

    def take(self):
        count = len(self.rounds)
        parts = [self.pieces[0]] + self.got
        self.got = None
        self.at += 1
        if self.at < count:
            blocks = add_low(parts)
            pieces = 1 << len(self.rounds[self.at])
            size = blocks.shape[0] // pieces
            self.pieces = [blocks[at * size : (at + 1) * size] for at in range(pieces)]
        elif self.at == count:
            part = add_low(parts)
            mask = SPREAD
            while mask < lax.axis_size("ba"):
                part = add_low([part, exchange(part, "ba", mask)])
                mask *= 2
            self.pieces = [part]
        elif self.left():
            self.pieces = [jnp.concatenate(parts, axis=0)]
        else:
            self.pieces = parts

    def step(self):
        self.take()
        if self.left():
            self.send()

    def finish(self, rows, more=0):
        cut = [bit for bits in self.rounds for bit in bits]
        joined = [bit for bits in reversed(self.joins) for bit in bits]
        places = [1 << (len(cut) - 1 - cut.index(bit)) for bit in reversed(joined)]
        order = [sum(place for at, place in enumerate(places) if part >> at & 1) for part in range(PARTS)]
        return plain_order(*self.pieces, self.own, order, rows, more)


def join(grads):
    both = Gradient.__new__(Gradient)
    both.rounds, both.joins, both.at, both.got = grads[0].rounds, grads[0].joins, grads[0].at, None
    both.pieces = [jnp.concatenate(pieces, axis=1) for pieces in zip(*[grad.pieces for grad in grads])]
    return both


def part_again(both, grads):
    rows = both.pieces[0].shape[1] // len(grads)
    for at, grad in enumerate(grads):
        grad.at, grad.got = both.at, None
        grad.pieces = [piece[:, at * rows : (at + 1) * rows] for piece in both.pieces]


def arrive(grads, *values):
    flat = [got for grad in grads for got in grad.got]
    held = list(tie(*values, *flat))
    rest = held[len(values) :]
    for grad in grads:
        grad.got, rest = rest[: len(grad.got)], rest[len(grad.got) :]
    return held[: len(values)]


LOW = jnp.bfloat16
WIDE = jnp.float32
TAPS = 3
SMEM = pltpu.SMEM


def dot(one, two):
    return jnp.dot(one, two, preferred_element_type=WIDE)


def dot_nt(one, two):
    return lax.dot_general(one, two, (((1,), (1,)), ((), ())), preferred_element_type=WIDE)


def dot_tn(one, two):
    return lax.dot_general(one, two, (((0,), (0,)), ((), ())), preferred_element_type=WIDE)


def iota(shape, axis):
    return lax.broadcasted_iota(jnp.int32, shape, axis)


def silu(half):
    return half * jnp.tanh(half) + half


def silu_pair(half):
    gate = jnp.tanh(half)
    value = half * gate + half
    return value, (1.0 + gate) + value * (1.0 - gate)


def fold(values):
    rows, width = values.shape
    return jnp.sum(values.reshape(rows // 8, 8, width), axis=0)


def close(partial):
    return jnp.sum(partial, axis=0, keepdims=True)


def spans(rows, size):
    return [slice(at, at + size) for at in range(0, rows, size)]


def over(values, size):
    assert size & (size - 1) == 0
    return jnp.right_shift(values, size.bit_length() - 1), jnp.bitwise_and(values, size - 1)


def parity_order(image_rows, cols, axis=0):
    pixels = image_rows * cols
    half_cols = cols // 2
    line = (pixels, 1) if axis == 0 else (1, pixels)
    plane, inside = over(iota(line, axis), pixels // 4)
    row, col = over(inside, half_cols)
    row_parity, col_parity = over(plane, 2)
    pixel = (2 * row + row_parity) * cols + 2 * col + col_parity
    return (iota((pixels, pixels), 1 - axis) == pixel).astype(WIDE).astype(LOW)


def halo_order(images, cols):
    count = images * cols
    half_cols = cols // 2
    parity, inside = over(iota((count, 1), 0), count // 2)
    image, col = over(inside, half_cols)
    return (iota((count, count), 1) == image * cols + 2 * col + parity).astype(WIDE).astype(LOW)


class Sums:
    def __init__(self, valid_ref, base, quarter):
        self.valid_ref, self.base, self.quarter = valid_ref, base, quarter
        self.total = jnp.zeros((8, base.shape[1]), WIDE)
        self.square = jnp.zeros((8, base.shape[1]), WIDE)

    def add(self, ref, start, cols):
        for image in range(self.valid_ref.shape[0]):
            at = start + image * self.quarter
            first = jnp.zeros(self.total.shape, WIDE)
            second = jnp.zeros(self.total.shape, WIDE)
            for span in spans(self.quarter, 32):
                gap = ref[at + span.start : at + span.stop, cols] - self.base
                first += fold(gap)
                second += fold(gap * gap)
            self.total += first * self.valid_ref[image]
            self.square += second * self.valid_ref[image]

    def close(self):
        return close(self.total), close(self.square)


def moments_of(sums, base, count):
    offset = sums[0:1, :] / count
    variance = jnp.maximum(sums[1:2, :] / count - offset * offset, 0.0)
    return base + offset, lax.rsqrt(variance + EPS)


def row_of(values, w):
    return dot(jnp.broadcast_to(values, (16, values.shape[1])).astype(LOW), w)[0:1, :]


def reduce_kernel(dims, lead, valid_ref, x_ref, w_ref, planes_ref, reduced_ref, stats_ref, sampled_ref, kept_ref, order_ref):
    images, image_rows, cols = dims
    pixels = image_rows * cols
    quarter = pixels // 4
    plane_rows = images * quarter
    group = images // lead
    valid = valid_ref[0]
    for image in range(1, images):
        valid = valid + valid_ref[image]
    step = pl.program_id(0)

    @pl.when(step == 0)
    def _():
        sampled_ref[...] = jnp.zeros(sampled_ref.shape, WIDE)
        order_ref[...] = parity_order(image_rows, cols)

    @pl.when(step < lead)
    def _():
        order = order_ref[...]
        total = jnp.zeros((8, x_ref.shape[1]), WIDE)
        for member in range(group):
            image = step * group + member
            moved = dot(order, x_ref[member * pixels : (member + 1) * pixels, :])
            total += fold(moved[:quarter, :]) * valid_ref[image]
            moved = moved.astype(LOW)
            for plane in range(4):
                part = moved[plane * quarter : (plane + 1) * quarter, :]
                planes_ref[plane, member] = part
                at = plane * plane_rows + pl.multiple_of(image * quarter, quarter)
                kept_ref[pl.ds(at, quarter), :] = part
        sampled_ref[...] += close(total) / (valid * float(quarter))

    @pl.when(step >= lead)
    def _():
        count = valid * float(pixels)
        base = dot(kept_ref[0:16, :], w_ref[...])[0:1, :]
        sums = Sums(valid_ref, base, quarter)
        for plane in range(4):
            start = plane * plane_rows
            reduced_ref[start : start + plane_rows, :] = dot(kept_ref[start : start + plane_rows, :], w_ref[...])
            sums.add(reduced_ref, start, slice(None))
        total, square = sums.close()
        stats_ref[0:1, :] = jnp.full(base.shape, count, WIDE)
        stats_ref[1:2, :] = base + total / count
        stats_ref[2:3, :] = jnp.maximum(square - total * (total / count), 0.0)


def turn_kernel(own_ref, value_ref, out_ref):
    parts, rows, _ = out_ref.shape
    turned = value_ref[...].T
    for part in range(parts):
        out_ref[jnp.bitwise_xor(own_ref[0], part)] = turned[part * rows : (part + 1) * rows, :]


def product_sums(quarter, valid_ref, x_ref, w_ref, base, out_ref, sums_ref):
    for cols in spans(out_ref.shape[1], 256):
        out_ref[:, cols] = dot(x_ref[...], w_ref[:, cols])
        sums = Sums(valid_ref, base[:, cols], quarter)
        sums.add(out_ref, 0, cols)
        sums_ref[0:1, cols], sums_ref[1:2, cols] = sums.close()


def project_kernel(quarter, valid_ref, x_ref, w_ref, sampled_ref, out_ref, sums_ref):
    base = row_of(sampled_ref[...], w_ref[...])
    sums_ref[2:3, :] = base
    product_sums(quarter, valid_ref, x_ref, w_ref, base, out_ref, sums_ref)


def group_mask(width):
    rows, _ = over(iota((width, 1), 0), GW)
    cols, _ = over(iota((1, width), 1), GW)
    return (rows == cols).astype(WIDE).astype(LOW)


def block_weights(w_ref, mask, tap):
    width = w_ref.shape[1]
    part = w_ref[tap * GW : (tap + 1) * GW, :]
    return jnp.concatenate([part] * (width // GW), axis=0) * mask


def shift_columns(values, cols, by):
    rows, width = values.shape
    moved = pltpu.roll(values, by % rows, 0)
    edge = 0 if by > 0 else cols - 1
    _, col = over(iota((rows, 1), 0), cols)
    return jnp.where(col == edge, 0.0, moved)


def activate(values, mean, scale, shift):
    return silu((values - mean) * scale + shift)


def plane_windows(plane, even, odd):
    images, deep, half_cols, width = odd[0].shape
    tall = deep - 1

    def part(ref, at):
        return ref[:, at : at + tall, :, :].reshape(images * tall * half_cols, width)

    if plane == 0:
        return [(4, even[0][...])]
    if plane == 1:
        return [(3, even[2][...]), (5, even[1][...])]
    if plane == 2:
        return [(1, part(odd[0], 0)), (7, part(odd[0], 1))]
    return [(0, part(odd[2], 0)), (2, part(odd[1], 0)), (6, part(odd[2], 1)), (8, part(odd[1], 1))]


def store_plane(dims, plane, get, halo, even, odd):
    images, tall, half_cols = dims
    quarter = tall * half_cols

    def deep(values):
        return values.astype(LOW).reshape(values.shape[0] // half_cols, half_cols, values.shape[1])

    for image in range(images):
        at = slice(image * quarter, (image + 1) * quarter)
        values = get(image)
        if plane < 2:
            even[plane][at, :] = values.astype(LOW)
        else:
            odd[plane - 2][image, 1:, :, :] = deep(values)
        if plane == 1:
            even[2][at, :] = shift_columns(values, half_cols, 1).astype(LOW)
        if plane == 3:
            odd[2][image, 1:, :, :] = deep(shift_columns(values, half_cols, 1))
    if plane >= 2:
        odd[plane - 2][:, 0, :, :] = deep(halo)
    if plane == 3:
        odd[2][:, 0, :, :] = deep(shift_columns(halo, half_cols, 1))


def window_scratch(images, tall, half_cols, width):
    flat = pltpu.VMEM((images * tall * half_cols, width), LOW)
    deep = pltpu.VMEM((images, tall + 1, half_cols, width), LOW)
    return [flat, flat, flat, deep, deep, deep]


def conv_kernel(
    dims,
    scalar_ref,
    valid_ref,
    reduced_ref,
    moments_ref,
    affine_ref,
    halo_ref,
    reduce_ref,
    group_ref,
    grouped_ref,
    sums_ref,
    base_ref,
    first_ref,
    edge_ref,
    moved_ref,
    *buffers,
):
    images, tall, half_cols = dims
    quarter = tall * half_cols
    plane_rows = images * quarter
    width = reduced_ref.shape[1]

    @pl.when(pl.program_id(0) == 0)
    def _():
        moved_ref[...] = dot(halo_order(images, 2 * half_cols), halo_ref[...]).astype(LOW)

    mean = moments_ref[0:1, :]
    scale = 0.5 * affine_ref[0:1, :] * lax.rsqrt(moments_ref[1:2, :] / scalar_ref[0] + EPS)
    shift = 0.5 * affine_ref[1:2, :]
    edge = activate(dot(moved_ref[...], reduce_ref[...]), mean, scale, shift) * scalar_ref[2]
    edge_ref[...] = edge.astype(LOW)
    half = edge.shape[0] // 2

    even, odd = buffers[:3], buffers[3:]
    mask = group_mask(width)
    for plane in range(4):

        def get(image):
            start = plane * plane_rows + image * quarter
            parts = []
            for span in spans(quarter, 32):
                part = reduced_ref[start + span.start : start + span.stop, :]
                parts.append(activate(part, mean, scale, shift))
            return jnp.concatenate(parts, axis=0)

        halo = (None, None, edge[:half], edge[half:])[plane]
        store_plane(dims, plane, get, halo, even, odd)
        total = None
        for tap, window in plane_windows(plane, even, odd):
            term = dot(window, block_weights(group_ref, mask, tap))
            total = term if total is None else total + term
        if plane == 0:
            grouped_ref[...] = total
        else:
            grouped_ref[...] += total
    kernel = group_ref[0:GW, :].astype(WIDE)
    for tap in range(1, TAPS * TAPS):
        kernel = kernel + group_ref[tap * GW : (tap + 1) * GW, :].astype(WIDE)
    kernel = jnp.concatenate([kernel.astype(LOW)] * (width // GW), axis=0) * mask
    base = row_of(silu(shift), kernel)
    sums = Sums(valid_ref, base, quarter)
    sums.add(grouped_ref, 0, slice(None))
    sums_ref[0:1, :], sums_ref[1:2, :] = sums.close()
    base_ref[...] = base
    for image in range(images):
        at = image * quarter
        first_ref[image * half_cols : (image + 1) * half_cols, :] = grouped_ref[at : at + half_cols, :].astype(LOW)


def expand_kernel(
    quarter,
    scalar_ref,
    valid_ref,
    grouped_ref,
    sums_two_ref,
    base_two_ref,
    affine_ref,
    w_ref,
    side_ref,
    hidden_ref,
    out_ref,
    sums_ref,
    base_ref,
):
    shift = 0.5 * affine_ref[1:2, :]

    @pl.when(pl.program_id(0) == 0)
    def _():
        mean, inv = moments_of(sums_two_ref[...], base_two_ref[...], scalar_ref[1])
        scale = 0.5 * affine_ref[0:1, :] * inv
        for span in spans(grouped_ref.shape[0], 16):
            hidden_ref[span, :] = activate(grouped_ref[span, :], mean, scale, shift).astype(LOW)

    base = row_of(silu(shift), w_ref[...])
    product_sums(quarter, valid_ref, hidden_ref, w_ref, base, out_ref, sums_ref)
    sums_ref[2:4, :] = side_ref[0:2, :]
    base_ref[0:1, :] = base
    base_ref[1:2, :] = side_ref[2:3, :]


def tail_moments(sums_ref, base_ref, count):
    return (
        *moments_of(sums_ref[0:2, :], base_ref[0:1, :], count),
        *moments_of(sums_ref[2:4, :], base_ref[1:2, :], count),
    )


def tail_halves(moments, affine):
    return (
        0.5 * affine[0:1, :] * moments[1],
        0.5 * affine[2:3, :] * moments[3],
        0.5 * (affine[1:2, :] + affine[3:4, :]),
    )


def output_kernel(
    size,
    scalar_ref,
    valid_ref,
    expanded_ref,
    projected_ref,
    stats_ref,
    base_ref,
    affine_ref,
    cot_ref,
    out_ref,
    sums_ref,
):
    rows, width = out_ref.shape
    quarter = rows // valid_ref.shape[0]
    totals = [jnp.zeros((8, width), WIDE) for _ in range(3)]
    moments = tail_moments(stats_ref, base_ref, scalar_ref[1])
    one, two, both = tail_halves(moments, affine_ref[...])
    for span in spans(rows, size):
        first = expanded_ref[span, :] - moments[0]
        second = projected_ref[span, :] - moments[2]
        valid = valid_ref[span.start // quarter]
        value, slope = silu_pair(first * one + second * two + both)
        out_ref[span, :] = (valid * value).astype(LOW)
        upstream = (cot_ref[span, :].astype(WIDE) * (0.5 * valid)) * slope
        totals[0] += fold(upstream)
        totals[1] += fold(upstream * first)
        totals[2] += fold(upstream * second)
    sums_ref[0:1, :] = close(totals[0])
    sums_ref[1:2, :] = close(totals[1]) * moments[1]
    sums_ref[2:3, :] = close(totals[2]) * moments[3]


def weights_kernel(
    size,
    scalar_ref,
    valid_ref,
    expanded_ref,
    projected_ref,
    stats_ref,
    base_ref,
    affine_ref,
    sums_ref,
    cot_ref,
    hidden_ref,
    sampled_ref,
    d_expanded_ref,
    d_projected_ref,
    expand_low_ref,
    expand_high_ref,
    proj_low_ref,
    proj_high_ref,
):
    rows, width = d_expanded_ref.shape
    quarter = rows // valid_ref.shape[0]
    count = scalar_ref[1]
    moments = tail_moments(stats_ref, base_ref, count)
    affine = affine_ref[...]
    one, two, both = tail_halves(moments, affine)
    sums = sums_ref[...] / count
    gain_one = affine[0:1, :] * moments[1]
    gain_two = affine[2:3, :] * moments[3]
    pull_one = gain_one * moments[1] * sums[1:2, :]
    pull_two = gain_two * moments[3] * sums[2:3, :]
    for cols in spans(width, 256):
        for span in spans(rows, size):
            first = expanded_ref[span, cols] - moments[0][:, cols]
            second = projected_ref[span, cols] - moments[2][:, cols]
            valid = valid_ref[span.start // quarter]
            _, slope = silu_pair(first * one[:, cols] + second * two[:, cols] + both[:, cols])
            upstream = (cot_ref[span, cols].astype(WIDE) * 0.5) * slope - sums[0:1, cols]
            along = first * (pull_one[:, cols] * valid)
            d_expanded_ref[span, cols] = (upstream * (gain_one[:, cols] * valid) - along).astype(LOW)
            along = second * (pull_two[:, cols] * valid)
            d_projected_ref[span, cols] = (upstream * (gain_two[:, cols] * valid) - along).astype(LOW)
        store_halves(sampled_ref, d_projected_ref[:, cols], proj_low_ref, proj_high_ref, cols)
        store_halves(hidden_ref, d_expanded_ref[:, cols], expand_low_ref, expand_high_ref, cols)


def store_halves(turned_ref, grads, low_ref, high_ref, cols):
    half, rows, _ = low_ref.shape
    for at, ref in ((0, low_ref), (half, high_ref)):
        left = turned_ref[at : at + half].reshape(half * rows, turned_ref.shape[2])
        ref[:, :, cols] = dot(left, grads).astype(LOW).reshape(half, rows, grads.shape[1])


def back_two_kernel(
    size, dims, scalar_ref, d_ref, w_ref, grouped_ref, sums_two_ref, base_two_ref, affine_ref, out_ref, sums_ref, first_ref
):
    rows, width = out_ref.shape
    images, tall, half_cols = dims
    mean, inv = moments_of(sums_two_ref[...], base_two_ref[...], scalar_ref[1])
    out_ref[...] = dot_nt(d_ref[...], w_ref[...])
    totals = [jnp.zeros((8, width), WIDE) for _ in range(2)]
    scale = 0.5 * affine_ref[0:1, :] * inv
    shift = 0.5 * affine_ref[1:2, :]
    for span in spans(rows, size):
        gap = grouped_ref[span, :] - mean
        _, slope = silu_pair(gap * scale + shift)
        grad = (out_ref[span, :] * 0.5) * slope
        out_ref[span, :] = grad
        totals[0] += fold(grad)
        totals[1] += fold(grad * gap)
    sums_ref[0:1, :] = close(totals[0])
    sums_ref[1:2, :] = close(totals[1]) * inv
    for image in range(images):
        at = image * tall * half_cols
        first_ref[image * half_cols : (image + 1) * half_cols, :] = out_ref[at : at + half_cols, :].astype(LOW)


def side_kernel(d_ref, w_ref, out_ref):
    out_ref[...] = dot_nt(d_ref[...], w_ref[...])


def norm_back_values(grad, values, mean, pull, valid):
    gain, offset, along = pull
    return (grad - offset) * (gain * valid) - (values - mean) * (along * valid)


def norm_pull(gain, inv, sums, count):
    return gain * inv, sums[0:1, :] / count, gain * inv * inv * (sums[1:2, :] / count)


def conv_back_kernel(
    dims,
    scalar_ref,
    own_ref,
    valid_ref,
    grad_ref,
    grouped_ref,
    below_grad_ref,
    below_grouped_ref,
    sums_two_ref,
    base_two_ref,
    affine_two_ref,
    grads_two_ref,
    reduced_ref,
    edge_ref,
    moments_one_ref,
    affine_one_ref,
    group_ref,
    out_ref,
    sums_ref,
    grad_group_ref,
    *buffers,
):
    images, tall, half_cols = dims
    quarter = tall * half_cols
    plane_rows = images * quarter
    width = reduced_ref.shape[1]
    even, odd, below = buffers[:3], buffers[3:6], buffers[6:8]
    count_in, count_out = scalar_ref[0], scalar_ref[1]

    mean, inv = moments_of(sums_two_ref[...], base_two_ref[...], count_out)
    pull = norm_pull(affine_two_ref[0:1, :], inv, grads_two_ref[...], count_out)
    for image in range(images):
        at = slice(image * quarter, (image + 1) * quarter)
        values = norm_back_values(grad_ref[at, :], grouped_ref[at, :], mean, pull, valid_ref[image])
        below[0][image, :tall, :, :] = values.astype(LOW).reshape(tall, half_cols, width)
        below[1][image, :tall, :, :] = (
            shift_columns(values, half_cols, -1).astype(LOW).reshape(tall, half_cols, width)
        )
        at = slice(image * half_cols, (image + 1) * half_cols)
        values = norm_back_values(
            below_grad_ref[at, :].astype(WIDE),
            below_grouped_ref[at, :].astype(WIDE),
            mean,
            pull,
            valid_ref[image] * scalar_ref[3],
        )
        below[0][image, tall, :, :] = values.astype(LOW)
        below[1][image, tall, :, :] = shift_columns(values, half_cols, -1).astype(LOW)

    def part(ref, at):
        return ref[:, at : at + tall, :, :].reshape(plane_rows, width)

    mask = group_mask(width)
    half_mask = mask * jnp.asarray(0.5, LOW)
    weights = [block_weights(group_ref, half_mask, tap) for tap in range(TAPS * TAPS)]
    here, left = part(below[0], 0), part(below[1], 0)
    next_here, next_left = part(below[0], 1), part(below[1], 1)
    terms = (
        [(here, 4)],
        [(here, 5), (left, 3)],
        [(here, 7), (next_here, 1)],
        [(here, 8), (left, 6), (next_here, 2), (next_left, 0)],
    )

    turned = here.T
    picked = jnp.bitwise_xor(iota((GW, 1), 0), own_ref[0])
    _, channel = over(iota((1, width), 1), GW)
    one_hot = (channel == picked).astype(WIDE).astype(LOW)
    mean_one = moments_one_ref[0:1, :]
    inv_one = lax.rsqrt(moments_one_ref[1:2, :] / count_in + EPS)
    scale = 0.5 * affine_one_ref[0:1, :] * inv_one
    shift = 0.5 * affine_one_ref[1:2, :]
    totals = [jnp.zeros((8, width), WIDE) for _ in range(2)]
    half = edge_ref.shape[0] // 2
    edge = edge_ref[...].astype(WIDE)
    for plane in range(4):
        base = plane * plane_rows
        total = None
        for grads, tap in terms[plane]:
            term = dot_nt(grads, weights[tap])
            total = term if total is None else total + term
        out_ref[base : base + plane_rows, :] = total

        def get(image):
            start = base + image * quarter
            parts = []
            for span in spans(quarter, 32):
                at = slice(start + span.start, start + span.stop)
                gap = reduced_ref[at, :] - mean_one
                value, slope = silu_pair(gap * scale + shift)
                grad = out_ref[at, :] * slope
                out_ref[at, :] = grad
                totals[0] += fold(grad)
                totals[1] += fold(grad * gap)
                parts.append(value)
            return jnp.concatenate(parts, axis=0)

        halo = (None, None, edge[:half], edge[half:])[plane]
        store_plane(dims, plane, get, halo, even, odd)
        for tap, window in plane_windows(plane, even, odd):
            full = dot(turned, window).astype(LOW) * mask
            grad_group_ref[tap] = dot_nt(one_hot, full).astype(LOW)
    sums_ref[0:1, :] = close(totals[0])
    sums_ref[1:2, :] = close(totals[1]) * inv_one


def reduced_back_kernel(
    size,
    scalar_ref,
    valid_ref,
    grad_ref,
    reduced_ref,
    moments_ref,
    affine_ref,
    sums_ref,
    *refs,
):
    planes_refs, (d_ref, low_ref, high_ref) = refs[:4], refs[4:]
    rows, width = d_ref.shape
    images = valid_ref.shape[0]
    quarter = rows // (4 * images)
    mean = moments_ref[0:1, :]
    inv = lax.rsqrt(moments_ref[1:2, :] / scalar_ref[0] + EPS)
    pull = norm_pull(affine_ref[0:1, :], inv, sums_ref[...], scalar_ref[0])
    for span in spans(rows, size):
        valid = valid_ref[span.start // quarter % images]
        d_ref[span, :] = norm_back_values(grad_ref[span, :], reduced_ref[span, :], mean, pull, valid).astype(LOW)
    half = low_ref.shape[0]
    for at, ref in ((0, low_ref), (half, high_ref)):
        total = None
        for plane, planes_ref in enumerate(planes_refs):
            deep = planes_ref.shape[2]
            left = planes_ref[at : at + half].reshape(half * planes_ref.shape[1], deep)
            term = dot(left, d_ref[plane * deep : (plane + 1) * deep, :])
            total = term if total is None else total + term
        ref[...] = total.astype(LOW).reshape(ref.shape)


def images_back_kernel(dims, d_ref, w_ref, side_ref, *refs):
    out_ref, order_ref = refs[-2:]
    image_rows, cols = dims
    pixels = image_rows * cols
    quarter = pixels // 4

    @pl.when(pl.program_id(0) == 0)
    def _():
        order_ref[...] = parity_order(image_rows, cols, 1)

    values = dot_nt(d_ref[...].reshape(pixels, d_ref.shape[-1]), w_ref[...])
    first = values[:quarter] + side_ref[...]
    planes = jnp.concatenate([first, values[quarter:]], axis=0).astype(LOW)
    out_ref[...] = dot(order_ref[...], planes).astype(LOW)


def whole(shape):
    return pl.BlockSpec(shape, lambda i: (0,) * len(shape))


def wide_cols(rows, width):
    return pl.BlockSpec((rows, width), lambda i: (0, i))


SCALARS = pl.BlockSpec(memory_space=pltpu.SMEM)


def place(shape, kind):
    if math.prod(shape) * jnp.dtype(kind).itemsize >= 4 << 20:
        return pltpu.HBM(shape, kind)
    return jax.ShapeDtypeStruct(shape, kind)


def call(kernel, grid, in_specs, out_specs, out_shapes, cost, scratch=()):
    flops, moved = cost
    return pl.pallas_call(
        kernel,
        grid=(grid,),
        in_specs=in_specs,
        out_specs=out_specs,
        out_shape=[place(shape, kind) for shape, kind in out_shapes],
        scratch_shapes=list(scratch),
        compiler_params=pltpu.CompilerParams(vmem_limit_bytes=VMEM_LIMIT),
        cost_estimate=pl.CostEstimate(flops=flops, bytes_accessed=moved, transcendentals=0),
    )


def hbm(value):
    return pltpu.with_memory_space_constraint(value, pltpu.HBM)


def per_device(
    images_in,
    reduce_w,
    gain_one,
    shift_one,
    group_w,
    gain_two,
    shift_two,
    expand_w,
    gain_three,
    shift_three,
    proj_w,
    gain_proj,
    shift_proj,
    valid_mask,
    cotangent,
):
    images, image_rows, cols, chans = images_in.shape
    mid = reduce_w.shape[1]
    wide = expand_w.shape[1]
    tall, half_cols = image_rows // 2, cols // 2
    quarter = tall * half_cols
    rows = images * quarter
    pixels = images * image_rows * cols
    block = 256
    steps = mid // block
    strip = 512
    strips = wide // strip

    valid = valid_mask.astype(WIDE)
    row_index = lax.axis_index("ha")
    has_upper = (row_index > 0).astype(WIDE)
    has_lower = (row_index < lax.axis_size("ha") - 1).astype(WIDE)
    plain = ([CORE], [SIDE_ONE], [SIDE_TWO], [DEEP_ONE, DEEP_TWO])
    swapped = ([CORE], [SIDE_TWO], [SIDE_ONE], [DEEP_ONE, DEEP_TWO])
    short = ([CORE], [SIDE_TWO, SIDE_ONE], [DEEP_ONE, DEEP_TWO])
    own_one, own_two = own_part(plain).reshape(1), own_part(swapped).reshape(1)
    affine_one = jnp.stack([gain_one, shift_one])
    affine_two = jnp.stack([gain_two, shift_two])
    affine_out = jnp.stack([gain_three, shift_three, gain_proj, shift_proj])
    taps = TAPS * TAPS * GW
    group_flat = group_w.reshape(taps, mid)
    rounds = sum_plan(("ba", "ha"))
    back_rounds = sum_plan(("ha", "ba"))

    halo_images = shifted(images_in[:, -1], "ha", 1).reshape(images * cols, chans)
    lead = images // 4
    planes, reduced, stats, sampled = call(
        functools.partial(reduce_kernel, (images, image_rows, cols), lead),
        lead + steps,
        [
            SCALARS,
            pl.BlockSpec((pixels // lead, chans), lambda i: (jnp.minimum(i, lead - 1), 0)),
            pl.BlockSpec((chans, block), lambda i: (0, jnp.maximum(i - lead, 0))),
        ],
        [
            pl.BlockSpec((4, images // lead, quarter, chans), lambda i: (0, jnp.minimum(i, lead - 1), 0, 0)),
            pl.BlockSpec((pixels, block), lambda i: (0, jnp.maximum(i - lead, 0))),
            pl.BlockSpec((3, block), lambda i: (0, jnp.maximum(i - lead, 0))),
            whole((1, chans)),
        ],
        [((4, images, quarter, chans), LOW), ((pixels, mid), WIDE), ((3, mid), WIDE), ((1, chans), WIDE)],
        (2 * pixels * chans * (mid + 256), 20 << 20),
        [pltpu.VMEM((pixels, chans), LOW), pltpu.VMEM((image_rows * cols, image_rows * cols), LOW)],
    )(valid, hbm(images_in.reshape(pixels, chans)), hbm(reduce_w))
    planes = planes.reshape(pixels, chans)
    stats, halo_images = tie(jnp.concatenate([stats, sampled]), halo_images)
    stats = mesh_moments(stats, rounds)

    def turn(value, at, own):
        width = value.shape[1]
        return call(
            turn_kernel,
            1,
            [SCALARS, pl.BlockSpec((rows, width), lambda i: (at or 0, 0))],
            [whole((PARTS, width // PARTS, rows))],
            [((PARTS, width // PARTS, rows), LOW)],
            (0, 2 << 20),
        )(own, value if at is None else hbm(value))[0]

    sampled_turned = turn(planes, 0, own_two)
    stats, sampled_turned = tie(stats, sampled_turned)
    count_in, moments_one, sampled_mean = stats[0, 0], stats[1:3], stats[3:4]
    scalars = jnp.stack([count_in, count_in / 4.0, has_upper, has_lower])

    grouped, sums, base_two, first_row, edge = call(
        functools.partial(conv_kernel, (images, tall, half_cols)),
        steps,
        [
            SCALARS,
            SCALARS,
            wide_cols(pixels, block),
            wide_cols(2, block),
            wide_cols(2, block),
            whole((images * cols, chans)),
            wide_cols(chans, block),
            wide_cols(taps, block),
        ],
        [
            wide_cols(rows, block),
            wide_cols(2, block),
            wide_cols(1, block),
            wide_cols(images * half_cols, block),
            wide_cols(images * cols, block),
        ],
        [
            ((rows, mid), WIDE),
            ((2, mid), WIDE),
            ((1, mid), WIDE),
            ((images * half_cols, mid), LOW),
            ((images * cols, mid), LOW),
        ],
        (2 * rows * mid * 9 * 256, 14 << 20),
        [pltpu.VMEM((images * cols, chans), LOW)] + window_scratch(images, tall, half_cols, block),
    )(scalars, valid, hbm(reduced), moments_one, affine_one, halo_images, hbm(reduce_w), group_flat)
    sums_two = mesh_sum(sums, rounds)
    below_grouped = shifted(first_row, "ha", -1)
    sums_two, below_grouped = tie(sums_two, below_grouped)
    projected, side = call(
        functools.partial(project_kernel, quarter),
        strips,
        [SCALARS, whole((rows, chans)), wide_cols(chans, strip), whole((1, chans))],
        [wide_cols(rows, strip), wide_cols(3, strip)],
        [((rows, wide), WIDE), ((3, wide), WIDE)],
        (2 * rows * chans * wide, 10 << 20),
    )(valid, hbm(planes), proj_w, sampled_mean)

    hidden_two, expanded, sums, base_out = call(
        functools.partial(expand_kernel, quarter),
        strips,
        [
            SCALARS,
            SCALARS,
            whole((rows, mid)),
            whole((2, mid)),
            whole((1, mid)),
            whole((2, mid)),
            wide_cols(mid, strip),
            wide_cols(3, strip),
        ],
        [whole((rows, mid)), wide_cols(rows, strip), wide_cols(4, strip), wide_cols(2, strip)],
        [((rows, mid), LOW), ((rows, wide), WIDE), ((4, wide), WIDE), ((2, wide), WIDE)],
        (2 * rows * mid * wide, 12 << 20),
    )(scalars, valid, grouped, sums_two, base_two, affine_two, expand_w, side)
    stats_out = mesh_sum(sums, rounds)
    stats_out, hidden_turned = tie(stats_out, turn(hidden_two, None, own_one))

    cot = cotangent.reshape(rows, wide)
    output, sums = call(
        functools.partial(output_kernel, 16),
        strips,
        [
            SCALARS,
            SCALARS,
            wide_cols(rows, strip),
            wide_cols(rows, strip),
            wide_cols(4, strip),
            wide_cols(2, strip),
            wide_cols(4, strip),
            wide_cols(rows, strip),
        ],
        [wide_cols(rows, strip), wide_cols(3, strip)],
        [((rows, wide), LOW), ((3, wide), WIDE)],
        (20 * rows * wide, 12 << 20),
    )(scalars, valid, hbm(expanded), hbm(projected), stats_out, base_out, affine_out, cot)
    sums_out = mesh_sum(sums, rounds)

    def halves_specs(height, width):
        return [pl.BlockSpec((PARTS // 2, height // PARTS, width), lambda i: (0, 0, i))] * 2

    def halves_shapes(height, width):
        return [((PARTS // 2, height // PARTS, width), LOW)] * 2

    d_expanded, d_projected, *halves = call(
        functools.partial(weights_kernel, 16),
        strips,
        [
            SCALARS,
            SCALARS,
            wide_cols(rows, strip),
            wide_cols(rows, strip),
            wide_cols(4, strip),
            wide_cols(2, strip),
            wide_cols(4, strip),
            wide_cols(3, strip),
            wide_cols(rows, strip),
            whole((PARTS, mid // PARTS, rows)),
            whole((PARTS, chans // PARTS, rows)),
        ],
        [wide_cols(rows, strip), wide_cols(rows, strip)] + halves_specs(mid, strip) + halves_specs(chans, strip),
        [((rows, wide), LOW), ((rows, wide), LOW)] + halves_shapes(mid, wide) + halves_shapes(chans, wide),
        (4 * rows * mid * wide, 24 << 20),
    )(
        scalars,
        valid,
        hbm(expanded),
        hbm(projected),
        stats_out,
        base_out,
        affine_out,
        sums_out,
        cot,
        hidden_turned,
        sampled_turned,
    )
    expand_sum = Gradient(halves[:2], plain, plain[:3] + ([DEEP_ONE], [DEEP_TWO]))
    proj_sum = Gradient(halves[2:], swapped, swapped[:3] + ([DEEP_ONE], [DEEP_TWO]))
    pair = [expand_sum, proj_sum]
    for grad in pair:
        grad.send()

    grad_two, sums, first_row = call(
        functools.partial(back_two_kernel, 16, (images, tall, half_cols)),
        steps,
        [
            SCALARS,
            whole((rows, wide)),
            pl.BlockSpec((block, wide), lambda i: (i, 0)),
            wide_cols(rows, block),
            wide_cols(2, block),
            wide_cols(1, block),
            wide_cols(2, block),
        ],
        [wide_cols(rows, block), wide_cols(2, block), wide_cols(images * half_cols, block)],
        [((rows, mid), WIDE), ((2, mid), WIDE), ((images * half_cols, mid), LOW)],
        (2 * rows * mid * wide, 10 << 20),
    )(scalars, d_expanded, expand_w, grouped, sums_two, base_two, affine_two)
    sums = mesh_sum(sums, back_rounds[:1])
    sums, first_row = arrive(pair, sums, first_row)
    below_grad = shifted(first_row, "ha", -1)
    sums = mesh_sum(sums, back_rounds[1:2])
    side_grad = call(
        side_kernel,
        1,
        [whole((rows, wide)), whole((chans, wide))],
        [whole((rows, chans))],
        [((rows, chans), WIDE)],
        (2 * rows * chans * wide, 8 << 20),
    )(d_projected, proj_w)[0]
    planes_turned = [sampled_turned] + [turn(planes, plane, own_two) for plane in range(1, 4)]
    sums, below_grad, side_grad, *planes_turned = arrive(pair, sums, below_grad, side_grad, *planes_turned)
    for grad in pair:
        grad.step()
    grads_two = mesh_sum(sums, back_rounds[2:])
    deep = pltpu.VMEM((images, tall + 1, half_cols, block), LOW)
    grads_two, side_grad = tie(grads_two, side_grad)
    grad_one, sums, parts_group = call(
        functools.partial(conv_back_kernel, (images, tall, half_cols)),
        steps,
        [
            SCALARS,
            SCALARS,
            SCALARS,
            wide_cols(rows, block),
            wide_cols(rows, block),
            wide_cols(images * half_cols, block),
            wide_cols(images * half_cols, block),
            wide_cols(2, block),
            wide_cols(1, block),
            wide_cols(2, block),
            wide_cols(2, block),
            wide_cols(pixels, block),
            wide_cols(images * cols, block),
            wide_cols(2, block),
            wide_cols(2, block),
            wide_cols(taps, block),
        ],
        [wide_cols(pixels, block), wide_cols(2, block), pl.BlockSpec((TAPS * TAPS, GW, block), lambda i: (0, 0, i))],
        [((pixels, mid), WIDE), ((2, mid), WIDE), ((TAPS * TAPS, GW, mid), LOW)],
        (4 * rows * mid * 9 * 256, 24 << 20),
        window_scratch(images, tall, half_cols, block) + [deep, deep],
    )(
        scalars,
        own_two,
        valid,
        grad_two,
        grouped,
        below_grad,
        below_grouped,
        sums_two,
        base_two,
        affine_two,
        grads_two,
        hbm(reduced),
        edge,
        moments_one,
        affine_one,
        group_flat,
    )
    parts_group = jnp.pad(jnp.transpose(parts_group, (1, 0, 2)), ((0, 0), (0, 16 - TAPS * TAPS), (0, 0)))
    (sums,) = arrive(pair, sums)
    sums = mesh_sum(sums, back_rounds[:1])
    (sums,) = arrive(pair, sums)
    for grad in pair:
        grad.step()
    grads_one = mesh_sum(sums, back_rounds[1:])
    grads_one, parts_group = arrive(pair, grads_one, parts_group)
    for grad in pair:
        grad.take()
    both = join(pair)
    both.send()

    d_reduced, *halves = call(
        functools.partial(reduced_back_kernel, 16),
        steps,
        [
            SCALARS,
            SCALARS,
            wide_cols(pixels, block),
            wide_cols(pixels, block),
            wide_cols(2, block),
            wide_cols(2, block),
            wide_cols(2, block),
        ]
        + [whole((PARTS, chans // PARTS, rows))] * 4,
        [wide_cols(pixels, block)] + halves_specs(chans, block),
        [((pixels, mid), LOW)] + halves_shapes(chans, mid),
        (2 * pixels * mid * chans, 26 << 20),
    )(scalars, valid, hbm(grad_one), hbm(reduced), moments_one, affine_one, grads_one, *planes_turned)
    d_reduced, *halves = arrive([both], d_reduced, *halves)
    parts_group = [parts_group[: PARTS // 2], parts_group[PARTS // 2 :]]
    halves = [jnp.concatenate(members, axis=1) for members in zip(halves, parts_group)]
    reduce_sum = Gradient(halves, short)
    reduce_sum.send()

    def images_back(d_part, side_part):
        return call(
            functools.partial(images_back_kernel, (image_rows, cols)),
            images,
            [
                pl.BlockSpec((4, None, quarter, mid), lambda i: (0, i, 0, 0)),
                whole((chans, mid)),
                pl.BlockSpec((quarter, chans), lambda i: (i, 0)),
            ],
            [pl.BlockSpec((None, image_rows * cols, chans), lambda i: (i, 0, 0))],
            [((images, image_rows * cols, chans), LOW)],
            (2 * pixels * mid * chans, 16 << 20),
            [pltpu.VMEM((image_rows * cols, image_rows * cols), LOW)],
        )(d_part, reduce_w, side_part)[0]

    everyone = pair + [reduce_sum]
    both.step()
    arrive([reduce_sum])
    reduce_sum.step()
    both.got[0], *reduce_sum.got[:2] = tie(both.got[0], *reduce_sum.got[:2])
    both.step()
    arrive([both, reduce_sum])
    both.take()
    part_again(both, pair)
    for grad in pair:
        grad.send()
    reduce_sum.step()
    (d_reduced,) = arrive(everyone, d_reduced)
    for grad in everyone:
        grad.step()
    d_reduced = d_reduced.reshape(4, images, quarter, mid)
    grad_images = images_back(d_reduced, side_grad)
    (grad_images,) = arrive(everyone, grad_images)
    for grad in everyone:
        grad.step()
    done = []
    for grad, width in zip(pair, (mid, chans)):
        if done:
            done[0] = arrive([grad], done[0])[0]
        grad.take()
        done += grad.finish(width // PARTS)
    grad_expand, grad_proj = done
    (grad_proj,) = arrive([reduce_sum], grad_proj)
    reduce_sum.step()
    reduce_sum.take()
    grad_reduce, grad_group = reduce_sum.finish(chans // PARTS, TAPS * TAPS)
    return (
        output.reshape(cotangent.shape),
        grad_images.reshape(images_in.shape),
        grad_reduce.reshape(reduce_w.shape),
        grads_one[1],
        grads_one[0],
        grad_group.reshape(group_w.shape),
        grads_two[1],
        grads_two[0],
        grad_expand.reshape(expand_w.shape),
        sums_out[1],
        sums_out[0],
        grad_proj.reshape(proj_w.shape),
        sums_out[2],
        sums_out[0],
    )


def solution(mesh):
    split = P("ba", "ha", None, None)
    rest = (P(),) * 12
    return jax.shard_map(
        per_device,
        mesh=mesh,
        in_specs=(split,) + rest + (P("ba"), split),
        out_specs=(split, split) + rest,
        check_vma=False,
    )
```

```python
import functools
import math

import jax
import jax.numpy as jnp
from jax import lax
from jax.experimental import pallas as pl
from jax.experimental.pallas import tpu as pltpu
from jax.sharding import PartitionSpec as P

GW = 32
EPS = 1e-05
VMEM_LIMIT = 36 * 1024 * 1024


def shifted(value, axis, by):
    peers = lax.axis_size(axis)
    pairs = [(i, i + by) for i in range(peers) if 0 <= i + by < peers]
    return lax.ppermute(value, axis, pairs)


def exchange(value, axis, mask):
    peers = lax.axis_size(axis)
    return lax.ppermute(value, axis, [(i, i ^ mask) for i in range(peers)])


def sum_plan(axes):
    rounds = []
    for axis in axes:
        bits = [1 << b for b in range(lax.axis_size(axis).bit_length() - 1)]
        if axis == "ba" and bits:
            rounds.append((axis, bits[:1]))
            bits = bits[1:]
        while bits:
            rounds.append((axis, bits[:2]))
            bits = bits[2:]
    return rounds


def meet(value, axis, masks):
    offsets = [0]
    for mask in masks:
        offsets = offsets + [o ^ mask for o in offsets]
    return [value] + [exchange(value, axis, o) for o in offsets[1:]]


def add_round(value, axis, masks):
    parts = meet(value, axis, masks)
    while len(parts) > 1:
        parts = [parts[i] + parts[i + 1] for i in range(0, len(parts), 2)]
    return parts[0]


def mesh_sum(value, rounds):
    for axis, masks in rounds:
        value = add_round(value, axis, masks)
    return value


def merge(one, two):
    count = one[0] + two[0]
    gap = two[1] - one[1]
    return (
        count,
        (one[0] * one[1] + two[0] * two[1]) / count,
        one[2] + two[2] + gap * gap * (one[0] * two[0] / count),
        (one[0] * one[3] + two[0] * two[3]) / count,
    )


def mesh_moments(packed, rounds):
    for axis, masks in rounds:
        parts = [tuple(part) for part in meet(packed, axis, masks)]
        while len(parts) > 1:
            parts = [merge(parts[i], parts[i + 1]) for i in range(0, len(parts), 2)]
        packed = jnp.stack(parts[0])
    return packed


PARTS = 32
SPREAD = 8
CORE, SIDE_ONE, SIDE_TWO, DEEP_ONE, DEEP_TWO = ("ba", 1), ("ha", 1), ("ha", 2), ("ba", 2), ("ba", 4)


def own_part(rounds):
    index = jnp.int32(0)
    for axis, mask in [bit for bits in rounds for bit in bits]:
        bit = jnp.bitwise_and(lax.axis_index(axis), mask) // mask
        index = index * 2 + bit.astype(jnp.int32)
    return index


def partners(bits):
    masks = [0]
    for _, mask in bits:
        masks = [old ^ new for old in masks for new in (0, mask)]
    return [(bits[0][0], mask) for mask in masks[1:]]


def spread_kernel(order, own_ref, low_ref, high_ref, *out_refs):
    half = low_ref.shape[0]
    rows = out_refs[0].shape[1]
    for part in range(2 * half):
        at = jnp.bitwise_xor(own_ref[0], order[part])
        ref = low_ref if part < half else high_ref
        out_refs[0][at] = ref[part % half, :rows, :].astype(jnp.float32)
        if len(out_refs) > 1:
            more = out_refs[1].shape[0]
            extra = ref[part % half, rows : rows + more, :].astype(jnp.float32)
            for row in range(more):
                out_refs[1][row, pl.ds(at, 1), :] = extra[row : row + 1, :]


def plain_order(low, high, own, order, rows, more):
    half, deep, cols = low.shape
    width = 512
    shapes = [(2 * half, rows)] + ([(more, 2 * half)] if more else [])
    block = pl.BlockSpec((half, deep, width), lambda i: (0, 0, i))
    return pl.pallas_call(
        functools.partial(spread_kernel, order),
        grid=(cols // width,),
        in_specs=[pl.BlockSpec(memory_space=pltpu.SMEM), block, block],
        out_specs=[pl.BlockSpec(shape + (width,), lambda i: (0, 0, i)) for shape in shapes],
        out_shape=[jax.ShapeDtypeStruct(shape + (cols,), jnp.float32) for shape in shapes],
        compiler_params=pltpu.CompilerParams(vmem_limit_bytes=VMEM_LIMIT),
        cost_estimate=pl.CostEstimate(flops=0, bytes_accessed=12 * low.size, transcendentals=0),
    )(own.reshape(1), low, high)


def add_low(parts):
    total = parts[0].astype(jnp.float32)
    for part in parts[1:]:
        total = total + part.astype(jnp.float32)
    return total.astype(jnp.bfloat16)


def tie(*values):
    return lax.optimization_barrier(values)


class Gradient:
    def __init__(self, pieces, rounds, joins=None):
        self.pieces, self.rounds, self.own = list(pieces), rounds, own_part(rounds)
        self.joins = tuple(reversed(joins or rounds))
        self.at = 0
        self.got = None

    def left(self):
        return len(self.rounds) + len(self.joins) - self.at

    def send(self):
        count = len(self.rounds)
        if self.at < count:
            pairs = zip(self.pieces[1:], partners(self.rounds[self.at]))
        else:
            pairs = [(self.pieces[0], peer) for peer in partners(self.joins[self.at - count])]
        self.got = [exchange(piece, *peer) for piece, peer in pairs]

    def take(self):
        count = len(self.rounds)
        parts = [self.pieces[0]] + self.got
        self.got = None
        self.at += 1
        if self.at < count:
            blocks = add_low(parts)
            pieces = 1 << len(self.rounds[self.at])
            size = blocks.shape[0] // pieces
            self.pieces = [blocks[at * size : (at + 1) * size] for at in range(pieces)]
        elif self.at == count:
            part = add_low(parts)
            mask = SPREAD
            while mask < lax.axis_size("ba"):
                part = add_low([part, exchange(part, "ba", mask)])
                mask *= 2
            self.pieces = [part]
        elif self.left():
            self.pieces = [jnp.concatenate(parts, axis=0)]
        else:
            self.pieces = parts

    def step(self):
        self.take()
        if self.left():
            self.send()

    def finish(self, rows, more=0):
        cut = [bit for bits in self.rounds for bit in bits]
        joined = [bit for bits in reversed(self.joins) for bit in bits]
        places = [1 << (len(cut) - 1 - cut.index(bit)) for bit in reversed(joined)]
        order = [sum(place for at, place in enumerate(places) if part >> at & 1) for part in range(PARTS)]
        return plain_order(*self.pieces, self.own, order, rows, more)


def join(grads):
    both = Gradient.__new__(Gradient)
    both.rounds, both.joins, both.at, both.got = grads[0].rounds, grads[0].joins, grads[0].at, None
    both.pieces = [jnp.concatenate(pieces, axis=1) for pieces in zip(*[grad.pieces for grad in grads])]
    return both


def part_again(both, grads):
    rows = both.pieces[0].shape[1] // len(grads)
    for at, grad in enumerate(grads):
        grad.at, grad.got = both.at, None
        grad.pieces = [piece[:, at * rows : (at + 1) * rows] for piece in both.pieces]


def arrive(grads, *values):
    flat = [got for grad in grads for got in grad.got]
    held = list(tie(*values, *flat))
    rest = held[len(values) :]
    for grad in grads:
        grad.got, rest = rest[: len(grad.got)], rest[len(grad.got) :]
    return held[: len(values)]


LOW = jnp.bfloat16
WIDE = jnp.float32
TAPS = 3
SMEM = pltpu.SMEM


def dot(one, two):
    return jnp.dot(one, two, preferred_element_type=WIDE)


def dot_nt(one, two):
    return lax.dot_general(one, two, (((1,), (1,)), ((), ())), preferred_element_type=WIDE)


def dot_tn(one, two):
    return lax.dot_general(one, two, (((0,), (0,)), ((), ())), preferred_element_type=WIDE)


def iota(shape, axis):
    return lax.broadcasted_iota(jnp.int32, shape, axis)


def silu(half):
    return half * jnp.tanh(half) + half


def silu_pair(half):
    gate = jnp.tanh(half)
    value = half * gate + half
    return value, (1.0 + gate) + value * (1.0 - gate)


def fold(values):
    rows, width = values.shape
    return jnp.sum(values.reshape(rows // 8, 8, width), axis=0)


def close(partial):
    return jnp.sum(partial, axis=0, keepdims=True)


def spans(rows, size):
    return [slice(at, at + size) for at in range(0, rows, size)]


def over(values, size):
    assert size & (size - 1) == 0
    return jnp.right_shift(values, size.bit_length() - 1), jnp.bitwise_and(values, size - 1)


def parity_order(image_rows, cols, axis=0):
    pixels = image_rows * cols
    half_cols = cols // 2
    line = (pixels, 1) if axis == 0 else (1, pixels)
    plane, inside = over(iota(line, axis), pixels // 4)
    row, col = over(inside, half_cols)
    row_parity, col_parity = over(plane, 2)
    pixel = (2 * row + row_parity) * cols + 2 * col + col_parity
    return (iota((pixels, pixels), 1 - axis) == pixel).astype(WIDE).astype(LOW)


def halo_order(images, cols):
    count = images * cols
    half_cols = cols // 2
    parity, inside = over(iota((count, 1), 0), count // 2)
    image, col = over(inside, half_cols)
    return (iota((count, count), 1) == image * cols + 2 * col + parity).astype(WIDE).astype(LOW)


class Sums:
    def __init__(self, valid_ref, base, quarter):
        self.valid_ref, self.base, self.quarter = valid_ref, base, quarter
        self.total = jnp.zeros((8, base.shape[1]), WIDE)
        self.square = jnp.zeros((8, base.shape[1]), WIDE)

    def add(self, ref, start, cols):
        for image in range(self.valid_ref.shape[0]):
            at = start + image * self.quarter
            first = jnp.zeros(self.total.shape, WIDE)
            second = jnp.zeros(self.total.shape, WIDE)
            for span in spans(self.quarter, 32):
                gap = ref[at + span.start : at + span.stop, cols] - self.base
                first += fold(gap)
                second += fold(gap * gap)
            self.total += first * self.valid_ref[image]
            self.square += second * self.valid_ref[image]

    def close(self):
        return close(self.total), close(self.square)


def moments_of(sums, base, count):
    offset = sums[0:1, :] / count
    variance = jnp.maximum(sums[1:2, :] / count - offset * offset, 0.0)
    return base + offset, lax.rsqrt(variance + EPS)


def row_of(values, w):
    return dot(jnp.broadcast_to(values, (16, values.shape[1])).astype(LOW), w)[0:1, :]


def reduce_kernel(dims, lead, valid_ref, x_ref, w_ref, planes_ref, reduced_ref, stats_ref, sampled_ref, kept_ref, order_ref):
    images, image_rows, cols = dims
    pixels = image_rows * cols
    quarter = pixels // 4
    plane_rows = images * quarter
    group = images // lead
    valid = valid_ref[0]
    for image in range(1, images):
        valid = valid + valid_ref[image]
    step = pl.program_id(0)

    @pl.when(step == 0)
    def _():
        sampled_ref[...] = jnp.zeros(sampled_ref.shape, WIDE)
        order_ref[...] = parity_order(image_rows, cols)

    @pl.when(step < lead)
    def _():
        order = order_ref[...]
        total = jnp.zeros((8, x_ref.shape[1]), WIDE)
        for member in range(group):
            image = step * group + member
            moved = dot(order, x_ref[member * pixels : (member + 1) * pixels, :])
            total += fold(moved[:quarter, :]) * valid_ref[image]
            moved = moved.astype(LOW)
            for plane in range(4):
                part = moved[plane * quarter : (plane + 1) * quarter, :]
                planes_ref[plane, member] = part
                at = plane * plane_rows + pl.multiple_of(image * quarter, quarter)
                kept_ref[pl.ds(at, quarter), :] = part
        sampled_ref[...] += close(total) / (valid * float(quarter))

    @pl.when(step >= lead)
    def _():
        count = valid * float(pixels)
        base = dot(kept_ref[0:16, :], w_ref[...])[0:1, :]
        sums = Sums(valid_ref, base, quarter)
        for plane in range(4):
            start = plane * plane_rows
            reduced_ref[start : start + plane_rows, :] = dot(kept_ref[start : start + plane_rows, :], w_ref[...])
            sums.add(reduced_ref, start, slice(None))
        total, square = sums.close()
        stats_ref[0:1, :] = jnp.full(base.shape, count, WIDE)
        stats_ref[1:2, :] = base + total / count
        stats_ref[2:3, :] = jnp.maximum(square - total * (total / count), 0.0)


def turn_kernel(own_ref, value_ref, out_ref):
    parts, rows, _ = out_ref.shape
    turned = value_ref[...].T
    for part in range(parts):
        out_ref[jnp.bitwise_xor(own_ref[0], part)] = turned[part * rows : (part + 1) * rows, :]


def product_sums(quarter, valid_ref, x_ref, w_ref, base, out_ref, sums_ref):
    for cols in spans(out_ref.shape[1], 256):
        out_ref[:, cols] = dot(x_ref[...], w_ref[:, cols])
        sums = Sums(valid_ref, base[:, cols], quarter)
        sums.add(out_ref, 0, cols)
        sums_ref[0:1, cols], sums_ref[1:2, cols] = sums.close()


def project_kernel(quarter, valid_ref, x_ref, w_ref, sampled_ref, out_ref, sums_ref):
    base = row_of(sampled_ref[...], w_ref[...])
    sums_ref[2:3, :] = base
    product_sums(quarter, valid_ref, x_ref, w_ref, base, out_ref, sums_ref)


def group_mask(width):
    rows, _ = over(iota((width, 1), 0), GW)
    cols, _ = over(iota((1, width), 1), GW)
    return (rows == cols).astype(WIDE).astype(LOW)


def block_weights(w_ref, mask, tap):
    width = w_ref.shape[1]
    part = w_ref[tap * GW : (tap + 1) * GW, :]
    return jnp.concatenate([part] * (width // GW), axis=0) * mask


def shift_columns(values, cols, by):
    rows, width = values.shape
    moved = pltpu.roll(values, by % rows, 0)
    edge = 0 if by > 0 else cols - 1
    _, col = over(iota((rows, 1), 0), cols)
    return jnp.where(col == edge, 0.0, moved)


def activate(values, mean, scale, shift):
    return silu((values - mean) * scale + shift)


def plane_windows(plane, even, odd):
    images, deep, half_cols, width = odd[0].shape
    tall = deep - 1

    def part(ref, at):
        return ref[:, at : at + tall, :, :].reshape(images * tall * half_cols, width)

    if plane == 0:
        return [(4, even[0][...])]
    if plane == 1:
        return [(3, even[2][...]), (5, even[1][...])]
    if plane == 2:
        return [(1, part(odd[0], 0)), (7, part(odd[0], 1))]
    return [(0, part(odd[2], 0)), (2, part(odd[1], 0)), (6, part(odd[2], 1)), (8, part(odd[1], 1))]


def store_plane(dims, plane, get, halo, even, odd):
    images, tall, half_cols = dims
    quarter = tall * half_cols

    def deep(values):
        return values.astype(LOW).reshape(values.shape[0] // half_cols, half_cols, values.shape[1])

    for image in range(images):
        at = slice(image * quarter, (image + 1) * quarter)
        values = get(image)
        if plane < 2:
            even[plane][at, :] = values.astype(LOW)
        else:
            odd[plane - 2][image, 1:, :, :] = deep(values)
        if plane == 1:
            even[2][at, :] = shift_columns(values, half_cols, 1).astype(LOW)
        if plane == 3:
            odd[2][image, 1:, :, :] = deep(shift_columns(values, half_cols, 1))
    if plane >= 2:
        odd[plane - 2][:, 0, :, :] = deep(halo)
    if plane == 3:
        odd[2][:, 0, :, :] = deep(shift_columns(halo, half_cols, 1))


def window_scratch(images, tall, half_cols, width):
    flat = pltpu.VMEM((images * tall * half_cols, width), LOW)
    deep = pltpu.VMEM((images, tall + 1, half_cols, width), LOW)
    return [flat, flat, flat, deep, deep, deep]


def conv_kernel(
    dims,
    scalar_ref,
    valid_ref,
    reduced_ref,
    moments_ref,
    affine_ref,
    halo_ref,
    reduce_ref,
    group_ref,
    grouped_ref,
    sums_ref,
    base_ref,
    first_ref,
    edge_ref,
    moved_ref,
    *buffers,
):
    images, tall, half_cols = dims
    quarter = tall * half_cols
    plane_rows = images * quarter
    width = reduced_ref.shape[1]

    @pl.when(pl.program_id(0) == 0)
    def _():
        moved_ref[...] = dot(halo_order(images, 2 * half_cols), halo_ref[...]).astype(LOW)

    mean = moments_ref[0:1, :]
    scale = 0.5 * affine_ref[0:1, :] * lax.rsqrt(moments_ref[1:2, :] / scalar_ref[0] + EPS)
    shift = 0.5 * affine_ref[1:2, :]
    edge = activate(dot(moved_ref[...], reduce_ref[...]), mean, scale, shift) * scalar_ref[2]
    edge_ref[...] = edge.astype(LOW)
    half = edge.shape[0] // 2

    even, odd = buffers[:3], buffers[3:]
    mask = group_mask(width)
    for plane in range(4):

        def get(image):
            start = plane * plane_rows + image * quarter
            parts = []
            for span in spans(quarter, 32):
                part = reduced_ref[start + span.start : start + span.stop, :]
                parts.append(activate(part, mean, scale, shift))
            return jnp.concatenate(parts, axis=0)

        halo = (None, None, edge[:half], edge[half:])[plane]
        store_plane(dims, plane, get, halo, even, odd)
        total = None
        for tap, window in plane_windows(plane, even, odd):
            term = dot(window, block_weights(group_ref, mask, tap))
            total = term if total is None else total + term
        if plane == 0:
            grouped_ref[...] = total
        else:
            grouped_ref[...] += total
    kernel = group_ref[0:GW, :].astype(WIDE)
    for tap in range(1, TAPS * TAPS):
        kernel = kernel + group_ref[tap * GW : (tap + 1) * GW, :].astype(WIDE)
    kernel = jnp.concatenate([kernel.astype(LOW)] * (width // GW), axis=0) * mask
    base = row_of(silu(shift), kernel)
    sums = Sums(valid_ref, base, quarter)
    sums.add(grouped_ref, 0, slice(None))
    sums_ref[0:1, :], sums_ref[1:2, :] = sums.close()
    base_ref[...] = base
    for image in range(images):
        at = image * quarter
        first_ref[image * half_cols : (image + 1) * half_cols, :] = grouped_ref[at : at + half_cols, :].astype(LOW)


def expand_kernel(
    quarter,
    scalar_ref,
    valid_ref,
    grouped_ref,
    sums_two_ref,
    base_two_ref,
    affine_ref,
    w_ref,
    side_ref,
    hidden_ref,
    out_ref,
    sums_ref,
    base_ref,
):
    shift = 0.5 * affine_ref[1:2, :]

    @pl.when(pl.program_id(0) == 0)
    def _():
        mean, inv = moments_of(sums_two_ref[...], base_two_ref[...], scalar_ref[1])
        scale = 0.5 * affine_ref[0:1, :] * inv
        for span in spans(grouped_ref.shape[0], 16):
            hidden_ref[span, :] = activate(grouped_ref[span, :], mean, scale, shift).astype(LOW)

    base = row_of(silu(shift), w_ref[...])
    product_sums(quarter, valid_ref, hidden_ref, w_ref, base, out_ref, sums_ref)
    sums_ref[2:4, :] = side_ref[0:2, :]
    base_ref[0:1, :] = base
    base_ref[1:2, :] = side_ref[2:3, :]


def tail_moments(sums_ref, base_ref, count):
    return (
        *moments_of(sums_ref[0:2, :], base_ref[0:1, :], count),
        *moments_of(sums_ref[2:4, :], base_ref[1:2, :], count),
    )


def tail_halves(moments, affine):
    return (
        0.5 * affine[0:1, :] * moments[1],
        0.5 * affine[2:3, :] * moments[3],
        0.5 * (affine[1:2, :] + affine[3:4, :]),
    )


def output_kernel(
    size,
    scalar_ref,
    valid_ref,
    expanded_ref,
    projected_ref,
    stats_ref,
    base_ref,
    affine_ref,
    cot_ref,
    out_ref,
    sums_ref,
):
    rows, width = out_ref.shape
    quarter = rows // valid_ref.shape[0]
    totals = [jnp.zeros((8, width), WIDE) for _ in range(3)]
    moments = tail_moments(stats_ref, base_ref, scalar_ref[1])
    one, two, both = tail_halves(moments, affine_ref[...])
    for span in spans(rows, size):
        first = expanded_ref[span, :] - moments[0]
        second = projected_ref[span, :] - moments[2]
        valid = valid_ref[span.start // quarter]
        value, slope = silu_pair(first * one + second * two + both)
        out_ref[span, :] = (valid * value).astype(LOW)
        upstream = (cot_ref[span, :].astype(WIDE) * (0.5 * valid)) * slope
        totals[0] += fold(upstream)
        totals[1] += fold(upstream * first)
        totals[2] += fold(upstream * second)
    sums_ref[0:1, :] = close(totals[0])
    sums_ref[1:2, :] = close(totals[1]) * moments[1]
    sums_ref[2:3, :] = close(totals[2]) * moments[3]


def weights_kernel(
    size,
    scalar_ref,
    valid_ref,
    expanded_ref,
    projected_ref,
    stats_ref,
    base_ref,
    affine_ref,
    sums_ref,
    cot_ref,
    hidden_ref,
    sampled_ref,
    d_expanded_ref,
    d_projected_ref,
    expand_low_ref,
    expand_high_ref,
    proj_low_ref,
    proj_high_ref,
):
    rows, width = d_expanded_ref.shape
    quarter = rows // valid_ref.shape[0]
    count = scalar_ref[1]
    moments = tail_moments(stats_ref, base_ref, count)
    affine = affine_ref[...]
    one, two, both = tail_halves(moments, affine)
    sums = sums_ref[...] / count
    gain_one = affine[0:1, :] * moments[1]
    gain_two = affine[2:3, :] * moments[3]
    pull_one = gain_one * moments[1] * sums[1:2, :]
    pull_two = gain_two * moments[3] * sums[2:3, :]
    for cols in spans(width, 256):
        for span in spans(rows, size):
            first = expanded_ref[span, cols] - moments[0][:, cols]
            second = projected_ref[span, cols] - moments[2][:, cols]
            valid = valid_ref[span.start // quarter]
            _, slope = silu_pair(first * one[:, cols] + second * two[:, cols] + both[:, cols])
            upstream = (cot_ref[span, cols].astype(WIDE) * 0.5) * slope - sums[0:1, cols]
            along = first * (pull_one[:, cols] * valid)
            d_expanded_ref[span, cols] = (upstream * (gain_one[:, cols] * valid) - along).astype(LOW)
            along = second * (pull_two[:, cols] * valid)
            d_projected_ref[span, cols] = (upstream * (gain_two[:, cols] * valid) - along).astype(LOW)
        store_halves(sampled_ref, d_projected_ref[:, cols], proj_low_ref, proj_high_ref, cols)
        store_halves(hidden_ref, d_expanded_ref[:, cols], expand_low_ref, expand_high_ref, cols)


def store_halves(turned_ref, grads, low_ref, high_ref, cols):
    half, rows, _ = low_ref.shape
    for at, ref in ((0, low_ref), (half, high_ref)):
        left = turned_ref[at : at + half].reshape(half * rows, turned_ref.shape[2])
        ref[:, :, cols] = dot(left, grads).astype(LOW).reshape(half, rows, grads.shape[1])


def back_two_kernel(
    size, dims, scalar_ref, d_ref, w_ref, grouped_ref, sums_two_ref, base_two_ref, affine_ref, out_ref, sums_ref, first_ref
):
    rows, width = out_ref.shape
    images, tall, half_cols = dims
    mean, inv = moments_of(sums_two_ref[...], base_two_ref[...], scalar_ref[1])
    out_ref[...] = dot_nt(d_ref[...], w_ref[...])
    totals = [jnp.zeros((8, width), WIDE) for _ in range(2)]
    scale = 0.5 * affine_ref[0:1, :] * inv
    shift = 0.5 * affine_ref[1:2, :]
    for span in spans(rows, size):
        gap = grouped_ref[span, :] - mean
        _, slope = silu_pair(gap * scale + shift)
        grad = (out_ref[span, :] * 0.5) * slope
        out_ref[span, :] = grad
        totals[0] += fold(grad)
        totals[1] += fold(grad * gap)
    sums_ref[0:1, :] = close(totals[0])
    sums_ref[1:2, :] = close(totals[1]) * inv
    for image in range(images):
        at = image * tall * half_cols
        first_ref[image * half_cols : (image + 1) * half_cols, :] = out_ref[at : at + half_cols, :].astype(LOW)


def side_kernel(d_ref, w_ref, out_ref):
    out_ref[...] = dot_nt(d_ref[...], w_ref[...])


def norm_back_values(grad, values, mean, pull, valid):
    gain, offset, along = pull
    return (grad - offset) * (gain * valid) - (values - mean) * (along * valid)


def norm_pull(gain, inv, sums, count):
    return gain * inv, sums[0:1, :] / count, gain * inv * inv * (sums[1:2, :] / count)


def conv_back_kernel(
    dims,
    scalar_ref,
    own_ref,
    valid_ref,
    grad_ref,
    grouped_ref,
    below_grad_ref,
    below_grouped_ref,
    sums_two_ref,
    base_two_ref,
    affine_two_ref,
    grads_two_ref,
    reduced_ref,
    edge_ref,
    moments_one_ref,
    affine_one_ref,
    group_ref,
    out_ref,
    sums_ref,
    grad_group_ref,
    *buffers,
):
    images, tall, half_cols = dims
    quarter = tall * half_cols
    plane_rows = images * quarter
    width = reduced_ref.shape[1]
    even, odd, below = buffers[:3], buffers[3:6], buffers[6:8]
    count_in, count_out = scalar_ref[0], scalar_ref[1]

    mean, inv = moments_of(sums_two_ref[...], base_two_ref[...], count_out)
    pull = norm_pull(affine_two_ref[0:1, :], inv, grads_two_ref[...], count_out)
    for image in range(images):
        at = slice(image * quarter, (image + 1) * quarter)
        values = norm_back_values(grad_ref[at, :], grouped_ref[at, :], mean, pull, valid_ref[image])
        below[0][image, :tall, :, :] = values.astype(LOW).reshape(tall, half_cols, width)
        below[1][image, :tall, :, :] = (
            shift_columns(values, half_cols, -1).astype(LOW).reshape(tall, half_cols, width)
        )
        at = slice(image * half_cols, (image + 1) * half_cols)
        values = norm_back_values(
            below_grad_ref[at, :].astype(WIDE),
            below_grouped_ref[at, :].astype(WIDE),
            mean,
            pull,
            valid_ref[image] * scalar_ref[3],
        )
        below[0][image, tall, :, :] = values.astype(LOW)
        below[1][image, tall, :, :] = shift_columns(values, half_cols, -1).astype(LOW)

    def part(ref, at):
        return ref[:, at : at + tall, :, :].reshape(plane_rows, width)

    mask = group_mask(width)
    half_mask = mask * jnp.asarray(0.5, LOW)
    weights = [block_weights(group_ref, half_mask, tap) for tap in range(TAPS * TAPS)]
    here, left = part(below[0], 0), part(below[1], 0)
    next_here, next_left = part(below[0], 1), part(below[1], 1)
    terms = (
        [(here, 4)],
        [(here, 5), (left, 3)],
        [(here, 7), (next_here, 1)],
        [(here, 8), (left, 6), (next_here, 2), (next_left, 0)],
    )

    turned = here.T
    picked = jnp.bitwise_xor(iota((GW, 1), 0), own_ref[0])
    _, channel = over(iota((1, width), 1), GW)
    one_hot = (channel == picked).astype(WIDE).astype(LOW)
    mean_one = moments_one_ref[0:1, :]
    inv_one = lax.rsqrt(moments_one_ref[1:2, :] / count_in + EPS)
    scale = 0.5 * affine_one_ref[0:1, :] * inv_one
    shift = 0.5 * affine_one_ref[1:2, :]
    totals = [jnp.zeros((8, width), WIDE) for _ in range(2)]
    half = edge_ref.shape[0] // 2
    edge = edge_ref[...].astype(WIDE)
    for plane in range(4):
        base = plane * plane_rows
        total = None
        for grads, tap in terms[plane]:
            term = dot_nt(grads, weights[tap])
            total = term if total is None else total + term
        out_ref[base : base + plane_rows, :] = total

        def get(image):
            start = base + image * quarter
            parts = []
            for span in spans(quarter, 32):
                at = slice(start + span.start, start + span.stop)
                gap = reduced_ref[at, :] - mean_one
                value, slope = silu_pair(gap * scale + shift)
                grad = out_ref[at, :] * slope
                out_ref[at, :] = grad
                totals[0] += fold(grad)
                totals[1] += fold(grad * gap)
                parts.append(value)
            return jnp.concatenate(parts, axis=0)

        halo = (None, None, edge[:half], edge[half:])[plane]
        store_plane(dims, plane, get, halo, even, odd)
        for tap, window in plane_windows(plane, even, odd):
            full = dot(turned, window).astype(LOW) * mask
            grad_group_ref[tap] = dot_nt(one_hot, full).astype(LOW)
    sums_ref[0:1, :] = close(totals[0])
    sums_ref[1:2, :] = close(totals[1]) * inv_one


def reduced_back_kernel(
    size,
    scalar_ref,
    valid_ref,
    grad_ref,
    reduced_ref,
    moments_ref,
    affine_ref,
    sums_ref,
    *refs,
):
    planes_refs, (d_ref, low_ref, high_ref) = refs[:4], refs[4:]
    rows, width = d_ref.shape
    images = valid_ref.shape[0]
    quarter = rows // (4 * images)
    mean = moments_ref[0:1, :]
    inv = lax.rsqrt(moments_ref[1:2, :] / scalar_ref[0] + EPS)
    pull = norm_pull(affine_ref[0:1, :], inv, sums_ref[...], scalar_ref[0])
    for span in spans(rows, size):
        valid = valid_ref[span.start // quarter % images]
        d_ref[span, :] = norm_back_values(grad_ref[span, :], reduced_ref[span, :], mean, pull, valid).astype(LOW)
    half = low_ref.shape[0]
    for at, ref in ((0, low_ref), (half, high_ref)):
        total = None
        for plane, planes_ref in enumerate(planes_refs):
            deep = planes_ref.shape[2]
            left = planes_ref[at : at + half].reshape(half * planes_ref.shape[1], deep)
            term = dot(left, d_ref[plane * deep : (plane + 1) * deep, :])
            total = term if total is None else total + term
        ref[...] = total.astype(LOW).reshape(ref.shape)


def images_back_kernel(dims, d_ref, w_ref, side_ref, *refs):
    out_ref, order_ref = refs[-2:]
    image_rows, cols = dims
    pixels = image_rows * cols
    quarter = pixels // 4

    @pl.when(pl.program_id(0) == 0)
    def _():
        order_ref[...] = parity_order(image_rows, cols, 1)

    values = dot_nt(d_ref[...].reshape(pixels, d_ref.shape[-1]), w_ref[...])
    first = values[:quarter] + side_ref[...]
    planes = jnp.concatenate([first, values[quarter:]], axis=0).astype(LOW)
    out_ref[...] = dot(order_ref[...], planes).astype(LOW)


def whole(shape):
    return pl.BlockSpec(shape, lambda i: (0,) * len(shape))


def wide_cols(rows, width):
    return pl.BlockSpec((rows, width), lambda i: (0, i))


SCALARS = pl.BlockSpec(memory_space=pltpu.SMEM)


def place(shape, kind):
    if math.prod(shape) * jnp.dtype(kind).itemsize >= 4 << 20:
        return pltpu.HBM(shape, kind)
    return jax.ShapeDtypeStruct(shape, kind)


def call(kernel, grid, in_specs, out_specs, out_shapes, cost, scratch=()):
    flops, moved = cost
    return pl.pallas_call(
        kernel,
        grid=(grid,),
        in_specs=in_specs,
        out_specs=out_specs,
        out_shape=[place(shape, kind) for shape, kind in out_shapes],
        scratch_shapes=list(scratch),
        compiler_params=pltpu.CompilerParams(vmem_limit_bytes=VMEM_LIMIT),
        cost_estimate=pl.CostEstimate(flops=flops, bytes_accessed=moved, transcendentals=0),
    )


def hbm(value):
    return pltpu.with_memory_space_constraint(value, pltpu.HBM)


def per_device(
    images_in,
    reduce_w,
    gain_one,
    shift_one,
    group_w,
    gain_two,
    shift_two,
    expand_w,
    gain_three,
    shift_three,
    proj_w,
    gain_proj,
    shift_proj,
    valid_mask,
    cotangent,
):
    images, image_rows, cols, chans = images_in.shape
    mid = reduce_w.shape[1]
    wide = expand_w.shape[1]
    tall, half_cols = image_rows // 2, cols // 2
    quarter = tall * half_cols
    rows = images * quarter
    pixels = images * image_rows * cols
    block = 256
    steps = mid // block
    strip = 512
    strips = wide // strip

    valid = valid_mask.astype(WIDE)
    row_index = lax.axis_index("ha")
    has_upper = (row_index > 0).astype(WIDE)
    has_lower = (row_index < lax.axis_size("ha") - 1).astype(WIDE)
    plain = ([CORE], [SIDE_ONE], [SIDE_TWO], [DEEP_ONE, DEEP_TWO])
    swapped = ([CORE], [SIDE_TWO], [SIDE_ONE], [DEEP_ONE, DEEP_TWO])
    short = ([CORE], [SIDE_TWO, SIDE_ONE], [DEEP_ONE, DEEP_TWO])
    own_one, own_two = own_part(plain).reshape(1), own_part(swapped).reshape(1)
    affine_one = jnp.stack([gain_one, shift_one])
    affine_two = jnp.stack([gain_two, shift_two])
    affine_out = jnp.stack([gain_three, shift_three, gain_proj, shift_proj])
    taps = TAPS * TAPS * GW
    group_flat = group_w.reshape(taps, mid)
    rounds = sum_plan(("ba", "ha"))
    back_rounds = sum_plan(("ha", "ba"))

    halo_images = shifted(images_in[:, -1], "ha", 1).reshape(images * cols, chans)
    lead = images // 4
    planes, reduced, stats, sampled = call(
        functools.partial(reduce_kernel, (images, image_rows, cols), lead),
        lead + steps,
        [
            SCALARS,
            pl.BlockSpec((pixels // lead, chans), lambda i: (jnp.minimum(i, lead - 1), 0)),
            pl.BlockSpec((chans, block), lambda i: (0, jnp.maximum(i - lead, 0))),
        ],
        [
            pl.BlockSpec((4, images // lead, quarter, chans), lambda i: (0, jnp.minimum(i, lead - 1), 0, 0)),
            pl.BlockSpec((pixels, block), lambda i: (0, jnp.maximum(i - lead, 0))),
            pl.BlockSpec((3, block), lambda i: (0, jnp.maximum(i - lead, 0))),
            whole((1, chans)),
        ],
        [((4, images, quarter, chans), LOW), ((pixels, mid), WIDE), ((3, mid), WIDE), ((1, chans), WIDE)],
        (2 * pixels * chans * (mid + 256), 20 << 20),
        [pltpu.VMEM((pixels, chans), LOW), pltpu.VMEM((image_rows * cols, image_rows * cols), LOW)],
    )(valid, hbm(images_in.reshape(pixels, chans)), hbm(reduce_w))
    planes = planes.reshape(pixels, chans)
    stats, halo_images = tie(jnp.concatenate([stats, sampled]), halo_images)
    stats = mesh_moments(stats, rounds)

    def turn(value, at, own):
        width = value.shape[1]
        return call(
            turn_kernel,
            1,
            [SCALARS, pl.BlockSpec((rows, width), lambda i: (at or 0, 0))],
            [whole((PARTS, width // PARTS, rows))],
            [((PARTS, width // PARTS, rows), LOW)],
            (0, 2 << 20),
        )(own, value if at is None else hbm(value))[0]

    sampled_turned = turn(planes, 0, own_two)
    stats, sampled_turned = tie(stats, sampled_turned)
    count_in, moments_one, sampled_mean = stats[0, 0], stats[1:3], stats[3:4]
    scalars = jnp.stack([count_in, count_in / 4.0, has_upper, has_lower])

    grouped, sums, base_two, first_row, edge = call(
        functools.partial(conv_kernel, (images, tall, half_cols)),
        steps,
        [
            SCALARS,
            SCALARS,
            wide_cols(pixels, block),
            wide_cols(2, block),
            wide_cols(2, block),
            whole((images * cols, chans)),
            wide_cols(chans, block),
            wide_cols(taps, block),
        ],
        [
            wide_cols(rows, block),
            wide_cols(2, block),
            wide_cols(1, block),
            wide_cols(images * half_cols, block),
            wide_cols(images * cols, block),
        ],
        [
            ((rows, mid), WIDE),
            ((2, mid), WIDE),
            ((1, mid), WIDE),
            ((images * half_cols, mid), LOW),
            ((images * cols, mid), LOW),
        ],
        (2 * rows * mid * 9 * 256, 14 << 20),
        [pltpu.VMEM((images * cols, chans), LOW)] + window_scratch(images, tall, half_cols, block),
    )(scalars, valid, hbm(reduced), moments_one, affine_one, halo_images, hbm(reduce_w), group_flat)
    sums_two = mesh_sum(sums, rounds)
    below_grouped = shifted(first_row, "ha", -1)
    sums_two, below_grouped = tie(sums_two, below_grouped)
    projected, side = call(
        functools.partial(project_kernel, quarter),
        strips,
        [SCALARS, whole((rows, chans)), wide_cols(chans, strip), whole((1, chans))],
        [wide_cols(rows, strip), wide_cols(3, strip)],
        [((rows, wide), WIDE), ((3, wide), WIDE)],
        (2 * rows * chans * wide, 10 << 20),
    )(valid, hbm(planes), proj_w, sampled_mean)

    hidden_two, expanded, sums, base_out = call(
        functools.partial(expand_kernel, quarter),
        strips,
        [
            SCALARS,
            SCALARS,
            whole((rows, mid)),
            whole((2, mid)),
            whole((1, mid)),
            whole((2, mid)),
            wide_cols(mid, strip),
            wide_cols(3, strip),
        ],
        [whole((rows, mid)), wide_cols(rows, strip), wide_cols(4, strip), wide_cols(2, strip)],
        [((rows, mid), LOW), ((rows, wide), WIDE), ((4, wide), WIDE), ((2, wide), WIDE)],
        (2 * rows * mid * wide, 12 << 20),
    )(scalars, valid, grouped, sums_two, base_two, affine_two, expand_w, side)
    stats_out = mesh_sum(sums, rounds)
    stats_out, hidden_turned = tie(stats_out, turn(hidden_two, None, own_one))

    cot = cotangent.reshape(rows, wide)
    output, sums = call(
        functools.partial(output_kernel, 16),
        strips,
        [
            SCALARS,
            SCALARS,
            wide_cols(rows, strip),
            wide_cols(rows, strip),
            wide_cols(4, strip),
            wide_cols(2, strip),
            wide_cols(4, strip),
            wide_cols(rows, strip),
        ],
        [wide_cols(rows, strip), wide_cols(3, strip)],
        [((rows, wide), LOW), ((3, wide), WIDE)],
        (20 * rows * wide, 12 << 20),
    )(scalars, valid, hbm(expanded), hbm(projected), stats_out, base_out, affine_out, cot)
    sums_out = mesh_sum(sums, rounds)

    def halves_specs(height, width):
        return [pl.BlockSpec((PARTS // 2, height // PARTS, width), lambda i: (0, 0, i))] * 2

    def halves_shapes(height, width):
        return [((PARTS // 2, height // PARTS, width), LOW)] * 2

    d_expanded, d_projected, *halves = call(
        functools.partial(weights_kernel, 16),
        strips,
        [
            SCALARS,
            SCALARS,
            wide_cols(rows, strip),
            wide_cols(rows, strip),
            wide_cols(4, strip),
            wide_cols(2, strip),
            wide_cols(4, strip),
            wide_cols(3, strip),
            wide_cols(rows, strip),
            whole((PARTS, mid // PARTS, rows)),
            whole((PARTS, chans // PARTS, rows)),
        ],
        [wide_cols(rows, strip), wide_cols(rows, strip)] + halves_specs(mid, strip) + halves_specs(chans, strip),
        [((rows, wide), LOW), ((rows, wide), LOW)] + halves_shapes(mid, wide) + halves_shapes(chans, wide),
        (4 * rows * mid * wide, 24 << 20),
    )(
        scalars,
        valid,
        hbm(expanded),
        hbm(projected),
        stats_out,
        base_out,
        affine_out,
        sums_out,
        cot,
        hidden_turned,
        sampled_turned,
    )
    expand_sum = Gradient(halves[:2], plain, plain[:3] + ([DEEP_ONE], [DEEP_TWO]))
    proj_sum = Gradient(halves[2:], swapped, swapped[:3] + ([DEEP_ONE], [DEEP_TWO]))
    pair = [expand_sum, proj_sum]
    for grad in pair:
        grad.send()

    grad_two, sums, first_row = call(
        functools.partial(back_two_kernel, 16, (images, tall, half_cols)),
        steps,
        [
            SCALARS,
            whole((rows, wide)),
            pl.BlockSpec((block, wide), lambda i: (i, 0)),
            wide_cols(rows, block),
            wide_cols(2, block),
            wide_cols(1, block),
            wide_cols(2, block),
        ],
        [wide_cols(rows, block), wide_cols(2, block), wide_cols(images * half_cols, block)],
        [((rows, mid), WIDE), ((2, mid), WIDE), ((images * half_cols, mid), LOW)],
        (2 * rows * mid * wide, 10 << 20),
    )(scalars, d_expanded, expand_w, grouped, sums_two, base_two, affine_two)
    sums = mesh_sum(sums, back_rounds[:1])
    sums, first_row = arrive(pair, sums, first_row)
    below_grad = shifted(first_row, "ha", -1)
    sums = mesh_sum(sums, back_rounds[1:2])
    side_grad = call(
        side_kernel,
        1,
        [whole((rows, wide)), whole((chans, wide))],
        [whole((rows, chans))],
        [((rows, chans), WIDE)],
        (2 * rows * chans * wide, 8 << 20),
    )(d_projected, proj_w)[0]
    planes_turned = [sampled_turned, turn(planes, 1, own_two)]
    sums, below_grad, side_grad, *planes_turned = arrive(pair, sums, below_grad, side_grad, *planes_turned)
    for grad in pair:
        grad.step()
    grads_two = mesh_sum(sums, back_rounds[2:])
    deep = pltpu.VMEM((images, tall + 1, half_cols, block), LOW)
    grads_two, side_grad = tie(grads_two, side_grad)
    grad_one, sums, parts_group = call(
        functools.partial(conv_back_kernel, (images, tall, half_cols)),
        steps,
        [
            SCALARS,
            SCALARS,
            SCALARS,
            wide_cols(rows, block),
            wide_cols(rows, block),
            wide_cols(images * half_cols, block),
            wide_cols(images * half_cols, block),
            wide_cols(2, block),
            wide_cols(1, block),
            wide_cols(2, block),
            wide_cols(2, block),
            wide_cols(pixels, block),
            wide_cols(images * cols, block),
            wide_cols(2, block),
            wide_cols(2, block),
            wide_cols(taps, block),
        ],
        [wide_cols(pixels, block), wide_cols(2, block), pl.BlockSpec((TAPS * TAPS, GW, block), lambda i: (0, 0, i))],
        [((pixels, mid), WIDE), ((2, mid), WIDE), ((TAPS * TAPS, GW, mid), LOW)],
        (4 * rows * mid * 9 * 256, 24 << 20),
        window_scratch(images, tall, half_cols, block) + [deep, deep],
    )(
        scalars,
        own_two,
        valid,
        grad_two,
        grouped,
        below_grad,
        below_grouped,
        sums_two,
        base_two,
        affine_two,
        grads_two,
        hbm(reduced),
        edge,
        moments_one,
        affine_one,
        group_flat,
    )
    parts_group = jnp.pad(jnp.transpose(parts_group, (1, 0, 2)), ((0, 0), (0, 16 - TAPS * TAPS), (0, 0)))
    (sums,) = arrive(pair, sums)
    sums = mesh_sum(sums, back_rounds[:1])
    (sums,) = arrive(pair, sums)
    for grad in pair:
        grad.step()
    grads_one = mesh_sum(sums, back_rounds[1:])
    planes_turned += [turn(planes, plane, own_two) for plane in (2, 3)]
    grads_one, parts_group, *planes_turned = arrive(pair, grads_one, parts_group, *planes_turned)
    for grad in pair:
        grad.take()
    both = join(pair)
    both.send()

    d_reduced, *halves = call(
        functools.partial(reduced_back_kernel, 16),
        steps,
        [
            SCALARS,
            SCALARS,
            wide_cols(pixels, block),
            wide_cols(pixels, block),
            wide_cols(2, block),
            wide_cols(2, block),
            wide_cols(2, block),
        ]
        + [whole((PARTS, chans // PARTS, rows))] * 4,
        [wide_cols(pixels, block)] + halves_specs(chans, block),
        [((pixels, mid), LOW)] + halves_shapes(chans, mid),
        (2 * pixels * mid * chans, 26 << 20),
    )(scalars, valid, hbm(grad_one), hbm(reduced), moments_one, affine_one, grads_one, *planes_turned)
    d_reduced, *halves = arrive([both], d_reduced, *halves)
    parts_group = [parts_group[: PARTS // 2], parts_group[PARTS // 2 :]]
    halves = [jnp.concatenate(members, axis=1) for members in zip(halves, parts_group)]
    reduce_sum = Gradient(halves, short)
    reduce_sum.send()

    def images_back(d_part, side_part):
        return call(
            functools.partial(images_back_kernel, (image_rows, cols)),
            images,
            [
                pl.BlockSpec((4, None, quarter, mid), lambda i: (0, i, 0, 0)),
                whole((chans, mid)),
                pl.BlockSpec((quarter, chans), lambda i: (i, 0)),
            ],
            [pl.BlockSpec((None, image_rows * cols, chans), lambda i: (i, 0, 0))],
            [((images, image_rows * cols, chans), LOW)],
            (2 * pixels * mid * chans, 16 << 20),
            [pltpu.VMEM((image_rows * cols, image_rows * cols), LOW)],
        )(d_part, reduce_w, side_part)[0]

    everyone = pair + [reduce_sum]
    both.step()
    arrive([reduce_sum])
    reduce_sum.step()
    both.got[0], *reduce_sum.got[:2] = tie(both.got[0], *reduce_sum.got[:2])
    both.step()
    arrive([both, reduce_sum])
    both.take()
    part_again(both, pair)
    for grad in pair:
        grad.send()
    reduce_sum.step()
    (d_reduced,) = arrive(everyone, d_reduced)
    for grad in everyone:
        grad.step()
    d_reduced = d_reduced.reshape(4, images, quarter, mid)
    grad_images = images_back(d_reduced, side_grad)
    (grad_images,) = arrive(everyone, grad_images)
    for grad in everyone:
        grad.step()
    done = []
    for grad, width in zip(pair, (mid, chans)):
        if done:
            done[0] = arrive([grad], done[0])[0]
        grad.take()
        done += grad.finish(width // PARTS)
    grad_expand, grad_proj = done
    (grad_proj,) = arrive([reduce_sum], grad_proj)
    reduce_sum.step()
    reduce_sum.take()
    grad_reduce, grad_group = reduce_sum.finish(chans // PARTS, TAPS * TAPS)
    return (
        output.reshape(cotangent.shape),
        grad_images.reshape(images_in.shape),
        grad_reduce.reshape(reduce_w.shape),
        grads_one[1],
        grads_one[0],
        grad_group.reshape(group_w.shape),
        grads_two[1],
        grads_two[0],
        grad_expand.reshape(expand_w.shape),
        sums_out[1],
        sums_out[0],
        grad_proj.reshape(proj_w.shape),
        sums_out[2],
        sums_out[0],
    )


def solution(mesh):
    split = P("ba", "ha", None, None)
    rest = (P(),) * 12
    return jax.shard_map(
        per_device,
        mesh=mesh,
        in_specs=(split,) + rest + (P("ba"), split),
        out_specs=(split, split) + rest,
        check_vma=False,
    )
```

```python
import functools
import math

import jax
import jax.numpy as jnp
from jax import lax
from jax.experimental import pallas as pl
from jax.experimental.pallas import tpu as pltpu
from jax.sharding import PartitionSpec as P

GW = 32
EPS = 1e-05
VMEM_LIMIT = 40 * 1024 * 1024


def shifted(value, axis, by):
    peers = lax.axis_size(axis)
    pairs = [(i, i + by) for i in range(peers) if 0 <= i + by < peers]
    return lax.ppermute(value, axis, pairs)


def exchange(value, axis, mask):
    peers = lax.axis_size(axis)
    return lax.ppermute(value, axis, [(i, i ^ mask) for i in range(peers)])


def sum_plan(axes):
    rounds = []
    for axis in axes:
        bits = [1 << b for b in range(lax.axis_size(axis).bit_length() - 1)]
        if axis == "ba" and bits:
            rounds.append((axis, bits[:1]))
            bits = bits[1:]
        while bits:
            rounds.append((axis, bits[:2]))
            bits = bits[2:]
    return rounds


def meet(value, axis, masks):
    offsets = [0]
    for mask in masks:
        offsets = offsets + [o ^ mask for o in offsets]
    return [value] + [exchange(value, axis, o) for o in offsets[1:]]


def add_round(value, axis, masks):
    parts = meet(value, axis, masks)
    while len(parts) > 1:
        parts = [parts[i] + parts[i + 1] for i in range(0, len(parts), 2)]
    return parts[0]


def mesh_sum(value, rounds):
    for axis, masks in rounds:
        value = add_round(value, axis, masks)
    return value


def merge(one, two):
    count = one[0] + two[0]
    gap = two[1] - one[1]
    return (
        count,
        (one[0] * one[1] + two[0] * two[1]) / count,
        one[2] + two[2] + gap * gap * (one[0] * two[0] / count),
        (one[0] * one[3] + two[0] * two[3]) / count,
    )


def mesh_moments(packed, rounds):
    for axis, masks in rounds:
        parts = [tuple(part) for part in meet(packed, axis, masks)]
        while len(parts) > 1:
            parts = [merge(parts[i], parts[i + 1]) for i in range(0, len(parts), 2)]
        packed = jnp.stack(parts[0])
    return packed


PARTS = 32
SPREAD = 8
CORE, SIDE_ONE, SIDE_TWO, DEEP_ONE, DEEP_TWO = ("ba", 1), ("ha", 1), ("ha", 2), ("ba", 2), ("ba", 4)


def own_part(rounds):
    index = jnp.int32(0)
    for axis, mask in [bit for bits in rounds for bit in bits]:
        bit = jnp.bitwise_and(lax.axis_index(axis), mask) // mask
        index = index * 2 + bit.astype(jnp.int32)
    return index


def partners(bits):
    masks = [0]
    for _, mask in bits:
        masks = [old ^ new for old in masks for new in (0, mask)]
    return [(bits[0][0], mask) for mask in masks[1:]]


def spread_kernel(order, own_ref, low_ref, high_ref, *out_refs):
    half = low_ref.shape[0]
    rows = out_refs[0].shape[1]
    for part in range(2 * half):
        at = jnp.bitwise_xor(own_ref[0], order[part])
        ref = low_ref if part < half else high_ref
        out_refs[0][at] = ref[part % half, :rows, :].astype(jnp.float32)
        if len(out_refs) > 1:
            more = out_refs[1].shape[0]
            extra = ref[part % half, rows : rows + more, :].astype(jnp.float32)
            for row in range(more):
                out_refs[1][row, pl.ds(at, 1), :] = extra[row : row + 1, :]


def plain_order(low, high, own, order, rows, more):
    half, deep, cols = low.shape
    width = 512
    shapes = [(2 * half, rows)] + ([(more, 2 * half)] if more else [])
    block = pl.BlockSpec((half, deep, width), lambda i: (0, 0, i))
    return pl.pallas_call(
        functools.partial(spread_kernel, order),
        grid=(cols // width,),
        in_specs=[pl.BlockSpec(memory_space=pltpu.SMEM), block, block],
        out_specs=[pl.BlockSpec(shape + (width,), lambda i: (0, 0, i)) for shape in shapes],
        out_shape=[jax.ShapeDtypeStruct(shape + (cols,), jnp.float32) for shape in shapes],
        compiler_params=pltpu.CompilerParams(vmem_limit_bytes=VMEM_LIMIT),
        cost_estimate=pl.CostEstimate(flops=0, bytes_accessed=12 * low.size, transcendentals=0),
    )(own.reshape(1), low, high)


def add_low(parts):
    total = parts[0].astype(jnp.float32)
    for part in parts[1:]:
        total = total + part.astype(jnp.float32)
    return total.astype(jnp.bfloat16)


def tie(*values):
    return lax.optimization_barrier(values)


class Gradient:
    def __init__(self, pieces, rounds, joins=None):
        self.pieces, self.rounds, self.own = list(pieces), rounds, own_part(rounds)
        self.joins = tuple(reversed(joins or rounds))
        self.at = 0
        self.got = None

    def left(self):
        return len(self.rounds) + len(self.joins) - self.at

    def send(self):
        count = len(self.rounds)
        if self.at < count:
            pairs = zip(self.pieces[1:], partners(self.rounds[self.at]))
        else:
            pairs = [(self.pieces[0], peer) for peer in partners(self.joins[self.at - count])]
        self.got = [exchange(piece, *peer) for piece, peer in pairs]

    def take(self):
        count = len(self.rounds)
        parts = [self.pieces[0]] + self.got
        self.got = None
        self.at += 1
        if self.at < count:
            blocks = add_low(parts)
            pieces = 1 << len(self.rounds[self.at])
            size = blocks.shape[0] // pieces
            self.pieces = [blocks[at * size : (at + 1) * size] for at in range(pieces)]
        elif self.at == count:
            part = add_low(parts)
            mask = SPREAD
            while mask < lax.axis_size("ba"):
                part = add_low([part, exchange(part, "ba", mask)])
                mask *= 2
            self.pieces = [part]
        elif self.left():
            self.pieces = [jnp.concatenate(parts, axis=0)]
        else:
            self.pieces = parts

    def step(self):
        self.take()
        if self.left():
            self.send()

    def finish(self, rows, more=0):
        cut = [bit for bits in self.rounds for bit in bits]
        joined = [bit for bits in reversed(self.joins) for bit in bits]
        places = [1 << (len(cut) - 1 - cut.index(bit)) for bit in reversed(joined)]
        order = [sum(place for at, place in enumerate(places) if part >> at & 1) for part in range(PARTS)]
        return plain_order(*self.pieces, self.own, order, rows, more)


def join(grads):
    both = Gradient.__new__(Gradient)
    both.rounds, both.joins, both.at, both.got = grads[0].rounds, grads[0].joins, grads[0].at, None
    both.pieces = [jnp.concatenate(pieces, axis=1) for pieces in zip(*[grad.pieces for grad in grads])]
    return both


def part_again(both, grads):
    rows = both.pieces[0].shape[1] // len(grads)
    for at, grad in enumerate(grads):
        grad.at, grad.got = both.at, None
        grad.pieces = [piece[:, at * rows : (at + 1) * rows] for piece in both.pieces]


def arrive(grads, *values):
    flat = [got for grad in grads for got in grad.got]
    held = list(tie(*values, *flat))
    rest = held[len(values) :]
    for grad in grads:
        grad.got, rest = rest[: len(grad.got)], rest[len(grad.got) :]
    return held[: len(values)]


LOW = jnp.bfloat16
WIDE = jnp.float32
TAPS = 3
SMEM = pltpu.SMEM


def dot(one, two):
    return jnp.dot(one, two, preferred_element_type=WIDE)


def dot_nt(one, two):
    return lax.dot_general(one, two, (((1,), (1,)), ((), ())), preferred_element_type=WIDE)


def dot_tn(one, two):
    return lax.dot_general(one, two, (((0,), (0,)), ((), ())), preferred_element_type=WIDE)


def iota(shape, axis):
    return lax.broadcasted_iota(jnp.int32, shape, axis)


def silu(half):
    return half * jnp.tanh(half) + half


def silu_pair(half):
    gate = jnp.tanh(half)
    value = half * gate + half
    return value, (1.0 + gate) + value * (1.0 - gate)


def fold(values):
    rows, width = values.shape
    return jnp.sum(values.reshape(rows // 8, 8, width), axis=0)


def close(partial):
    return jnp.sum(partial, axis=0, keepdims=True)


def spans(rows, size):
    return [slice(at, at + size) for at in range(0, rows, size)]


def over(values, size):
    assert size & (size - 1) == 0
    return jnp.right_shift(values, size.bit_length() - 1), jnp.bitwise_and(values, size - 1)


def parity_order(image_rows, cols, axis=0):
    pixels = image_rows * cols
    half_cols = cols // 2
    line = (pixels, 1) if axis == 0 else (1, pixels)
    plane, inside = over(iota(line, axis), pixels // 4)
    row, col = over(inside, half_cols)
    row_parity, col_parity = over(plane, 2)
    pixel = (2 * row + row_parity) * cols + 2 * col + col_parity
    return (iota((pixels, pixels), 1 - axis) == pixel).astype(WIDE).astype(LOW)


def halo_order(images, cols):
    count = images * cols
    half_cols = cols // 2
    parity, inside = over(iota((count, 1), 0), count // 2)
    image, col = over(inside, half_cols)
    return (iota((count, count), 1) == image * cols + 2 * col + parity).astype(WIDE).astype(LOW)


class Sums:
    def __init__(self, valid_ref, base, quarter):
        self.valid_ref, self.base, self.quarter = valid_ref, base, quarter
        self.total = jnp.zeros((8, base.shape[1]), WIDE)
        self.square = jnp.zeros((8, base.shape[1]), WIDE)

    def add(self, ref, start, cols):
        for image in range(self.valid_ref.shape[0]):
            at = start + image * self.quarter
            first = jnp.zeros(self.total.shape, WIDE)
            second = jnp.zeros(self.total.shape, WIDE)
            for span in spans(self.quarter, 32):
                gap = ref[at + span.start : at + span.stop, cols] - self.base
                first += fold(gap)
                second += fold(gap * gap)
            self.total += first * self.valid_ref[image]
            self.square += second * self.valid_ref[image]

    def close(self):
        return close(self.total), close(self.square)


def moments_of(sums, base, count):
    offset = sums[0:1, :] / count
    variance = jnp.maximum(sums[1:2, :] / count - offset * offset, 0.0)
    return base + offset, lax.rsqrt(variance + EPS)


def row_of(values, w):
    return dot(jnp.broadcast_to(values, (16, values.shape[1])).astype(LOW), w)[0:1, :]


def reduce_kernel(dims, lead, valid_ref, x_ref, w_ref, planes_ref, reduced_ref, stats_ref, sampled_ref, kept_ref, order_ref):
    images, image_rows, cols = dims
    pixels = image_rows * cols
    quarter = pixels // 4
    plane_rows = images * quarter
    group = images // lead
    valid = valid_ref[0]
    for image in range(1, images):
        valid = valid + valid_ref[image]
    step = pl.program_id(0)

    @pl.when(step == 0)
    def _():
        sampled_ref[...] = jnp.zeros(sampled_ref.shape, WIDE)
        order_ref[...] = parity_order(image_rows, cols)

    @pl.when(step < lead)
    def _():
        order = order_ref[...]
        total = jnp.zeros((8, x_ref.shape[1]), WIDE)
        for member in range(group):
            image = step * group + member
            moved = dot(order, x_ref[member * pixels : (member + 1) * pixels, :])
            total += fold(moved[:quarter, :]) * valid_ref[image]
            moved = moved.astype(LOW)
            for plane in range(4):
                part = moved[plane * quarter : (plane + 1) * quarter, :]
                planes_ref[plane, member] = part
                at = plane * plane_rows + pl.multiple_of(image * quarter, quarter)
                kept_ref[pl.ds(at, quarter), :] = part
        sampled_ref[...] += close(total) / (valid * float(quarter))

    @pl.when(step >= lead)
    def _():
        count = valid * float(pixels)
        base = dot(kept_ref[0:16, :], w_ref[...])[0:1, :]
        sums = Sums(valid_ref, base, quarter)
        for plane in range(4):
            start = plane * plane_rows
            reduced_ref[start : start + plane_rows, :] = dot(kept_ref[start : start + plane_rows, :], w_ref[...])
            sums.add(reduced_ref, start, slice(None))
        total, square = sums.close()
        stats_ref[0:1, :] = jnp.full(base.shape, count, WIDE)
        stats_ref[1:2, :] = base + total / count
        stats_ref[2:3, :] = jnp.maximum(square - total * (total / count), 0.0)


def turn_kernel(own_ref, value_ref, out_ref):
    parts, rows, _ = out_ref.shape
    turned = value_ref[...].T
    for part in range(parts):
        out_ref[jnp.bitwise_xor(own_ref[0], part)] = turned[part * rows : (part + 1) * rows, :]


def product_sums(quarter, valid_ref, x_ref, w_ref, base, out_ref, sums_ref):
    for cols in spans(out_ref.shape[1], 256):
        out_ref[:, cols] = dot(x_ref[...], w_ref[:, cols])
        sums = Sums(valid_ref, base[:, cols], quarter)
        sums.add(out_ref, 0, cols)
        sums_ref[0:1, cols], sums_ref[1:2, cols] = sums.close()


def project_kernel(quarter, valid_ref, x_ref, w_ref, sampled_ref, out_ref, sums_ref):
    base = row_of(sampled_ref[...], w_ref[...])
    sums_ref[2:3, :] = base
    product_sums(quarter, valid_ref, x_ref, w_ref, base, out_ref, sums_ref)


def group_mask(width):
    rows, _ = over(iota((width, 1), 0), GW)
    cols, _ = over(iota((1, width), 1), GW)
    return (rows == cols).astype(WIDE).astype(LOW)


def block_weights(w_ref, mask, tap):
    width = w_ref.shape[1]
    part = w_ref[tap * GW : (tap + 1) * GW, :]
    return jnp.concatenate([part] * (width // GW), axis=0) * mask


def shift_columns(values, cols, by):
    rows, width = values.shape
    moved = pltpu.roll(values, by % rows, 0)
    edge = 0 if by > 0 else cols - 1
    _, col = over(iota((rows, 1), 0), cols)
    return jnp.where(col == edge, 0.0, moved)


def activate(values, mean, scale, shift):
    return silu((values - mean) * scale + shift)


def plane_windows(plane, even, odd):
    images, deep, half_cols, width = odd[0].shape
    tall = deep - 1

    def part(ref, at):
        return ref[:, at : at + tall, :, :].reshape(images * tall * half_cols, width)

    if plane == 0:
        return [(4, even[0][...])]
    if plane == 1:
        return [(3, even[2][...]), (5, even[1][...])]
    if plane == 2:
        return [(1, part(odd[0], 0)), (7, part(odd[0], 1))]
    return [(0, part(odd[2], 0)), (2, part(odd[1], 0)), (6, part(odd[2], 1)), (8, part(odd[1], 1))]


def store_plane(dims, plane, get, halo, even, odd):
    images, tall, half_cols = dims
    quarter = tall * half_cols

    def deep(values):
        return values.astype(LOW).reshape(values.shape[0] // half_cols, half_cols, values.shape[1])

    for image in range(images):
        at = slice(image * quarter, (image + 1) * quarter)
        values = get(image)
        if plane < 2:
            even[plane][at, :] = values.astype(LOW)
        else:
            odd[plane - 2][image, 1:, :, :] = deep(values)
        if plane == 1:
            even[2][at, :] = shift_columns(values, half_cols, 1).astype(LOW)
        if plane == 3:
            odd[2][image, 1:, :, :] = deep(shift_columns(values, half_cols, 1))
    if plane >= 2:
        odd[plane - 2][:, 0, :, :] = deep(halo)
    if plane == 3:
        odd[2][:, 0, :, :] = deep(shift_columns(halo, half_cols, 1))


def window_scratch(images, tall, half_cols, width):
    flat = pltpu.VMEM((images * tall * half_cols, width), LOW)
    deep = pltpu.VMEM((images, tall + 1, half_cols, width), LOW)
    return [flat, flat, flat, deep, deep, deep]


def conv_kernel(
    dims,
    scalar_ref,
    valid_ref,
    reduced_ref,
    moments_ref,
    affine_ref,
    halo_ref,
    reduce_ref,
    group_ref,
    grouped_ref,
    sums_ref,
    base_ref,
    first_ref,
    edge_ref,
    moved_ref,
    *buffers,
):
    images, tall, half_cols = dims
    quarter = tall * half_cols
    plane_rows = images * quarter
    width = reduced_ref.shape[1]

    @pl.when(pl.program_id(0) == 0)
    def _():
        moved_ref[...] = dot(halo_order(images, 2 * half_cols), halo_ref[...]).astype(LOW)

    mean = moments_ref[0:1, :]
    scale = 0.5 * affine_ref[0:1, :] * lax.rsqrt(moments_ref[1:2, :] / scalar_ref[0] + EPS)
    shift = 0.5 * affine_ref[1:2, :]
    edge = activate(dot(moved_ref[...], reduce_ref[...]), mean, scale, shift) * scalar_ref[2]
    edge_ref[...] = edge.astype(LOW)
    half = edge.shape[0] // 2

    even, odd = buffers[:3], buffers[3:]
    mask = group_mask(width)
    for plane in range(4):

        def get(image):
            start = plane * plane_rows + image * quarter
            parts = []
            for span in spans(quarter, 32):
                part = reduced_ref[start + span.start : start + span.stop, :]
                parts.append(activate(part, mean, scale, shift))
            return jnp.concatenate(parts, axis=0)

        halo = (None, None, edge[:half], edge[half:])[plane]
        store_plane(dims, plane, get, halo, even, odd)
        total = None
        for tap, window in plane_windows(plane, even, odd):
            term = dot(window, block_weights(group_ref, mask, tap))
            total = term if total is None else total + term
        if plane == 0:
            grouped_ref[...] = total
        else:
            grouped_ref[...] += total
    kernel = group_ref[0:GW, :].astype(WIDE)
    for tap in range(1, TAPS * TAPS):
        kernel = kernel + group_ref[tap * GW : (tap + 1) * GW, :].astype(WIDE)
    kernel = jnp.concatenate([kernel.astype(LOW)] * (width // GW), axis=0) * mask
    base = row_of(silu(shift), kernel)
    sums = Sums(valid_ref, base, quarter)
    sums.add(grouped_ref, 0, slice(None))
    sums_ref[0:1, :], sums_ref[1:2, :] = sums.close()
    base_ref[...] = base
    for image in range(images):
        at = image * quarter
        first_ref[image * half_cols : (image + 1) * half_cols, :] = grouped_ref[at : at + half_cols, :].astype(LOW)


def expand_kernel(
    quarter,
    scalar_ref,
    valid_ref,
    grouped_ref,
    sums_two_ref,
    base_two_ref,
    affine_ref,
    w_ref,
    side_ref,
    hidden_ref,
    out_ref,
    sums_ref,
    base_ref,
):
    shift = 0.5 * affine_ref[1:2, :]

    @pl.when(pl.program_id(0) == 0)
    def _():
        mean, inv = moments_of(sums_two_ref[...], base_two_ref[...], scalar_ref[1])
        scale = 0.5 * affine_ref[0:1, :] * inv
        for span in spans(grouped_ref.shape[0], 16):
            hidden_ref[span, :] = activate(grouped_ref[span, :], mean, scale, shift).astype(LOW)

    base = row_of(silu(shift), w_ref[...])
    product_sums(quarter, valid_ref, hidden_ref, w_ref, base, out_ref, sums_ref)
    sums_ref[2:4, :] = side_ref[0:2, :]
    base_ref[0:1, :] = base
    base_ref[1:2, :] = side_ref[2:3, :]


def tail_moments(sums_ref, base_ref, count):
    return (
        *moments_of(sums_ref[0:2, :], base_ref[0:1, :], count),
        *moments_of(sums_ref[2:4, :], base_ref[1:2, :], count),
    )


def tail_halves(moments, affine):
    return (
        0.5 * affine[0:1, :] * moments[1],
        0.5 * affine[2:3, :] * moments[3],
        0.5 * (affine[1:2, :] + affine[3:4, :]),
    )


def output_kernel(
    size,
    scalar_ref,
    valid_ref,
    expanded_ref,
    projected_ref,
    stats_ref,
    base_ref,
    affine_ref,
    cot_ref,
    out_ref,
    sums_ref,
):
    rows, width = out_ref.shape
    quarter = rows // valid_ref.shape[0]
    totals = [jnp.zeros((8, width), WIDE) for _ in range(3)]
    moments = tail_moments(stats_ref, base_ref, scalar_ref[1])
    one, two, both = tail_halves(moments, affine_ref[...])
    for span in spans(rows, size):
        first = expanded_ref[span, :] - moments[0]
        second = projected_ref[span, :] - moments[2]
        valid = valid_ref[span.start // quarter]
        value, slope = silu_pair(first * one + second * two + both)
        out_ref[span, :] = (valid * value).astype(LOW)
        upstream = (cot_ref[span, :].astype(WIDE) * (0.5 * valid)) * slope
        totals[0] += fold(upstream)
        totals[1] += fold(upstream * first)
        totals[2] += fold(upstream * second)
    sums_ref[0:1, :] = close(totals[0])
    sums_ref[1:2, :] = close(totals[1]) * moments[1]
    sums_ref[2:3, :] = close(totals[2]) * moments[3]


def weights_kernel(
    size,
    scalar_ref,
    valid_ref,
    expanded_ref,
    projected_ref,
    stats_ref,
    base_ref,
    affine_ref,
    sums_ref,
    cot_ref,
    hidden_ref,
    sampled_ref,
    d_expanded_ref,
    d_projected_ref,
    expand_low_ref,
    expand_high_ref,
    proj_low_ref,
    proj_high_ref,
):
    rows, width = d_expanded_ref.shape
    quarter = rows // valid_ref.shape[0]
    count = scalar_ref[1]
    moments = tail_moments(stats_ref, base_ref, count)
    affine = affine_ref[...]
    one, two, both = tail_halves(moments, affine)
    sums = sums_ref[...] / count
    gain_one = affine[0:1, :] * moments[1]
    gain_two = affine[2:3, :] * moments[3]
    pull_one = gain_one * moments[1] * sums[1:2, :]
    pull_two = gain_two * moments[3] * sums[2:3, :]
    for cols in spans(width, 256):
        for span in spans(rows, size):
            first = expanded_ref[span, cols] - moments[0][:, cols]
            second = projected_ref[span, cols] - moments[2][:, cols]
            valid = valid_ref[span.start // quarter]
            _, slope = silu_pair(first * one[:, cols] + second * two[:, cols] + both[:, cols])
            upstream = (cot_ref[span, cols].astype(WIDE) * 0.5) * slope - sums[0:1, cols]
            along = first * (pull_one[:, cols] * valid)
            d_expanded_ref[span, cols] = (upstream * (gain_one[:, cols] * valid) - along).astype(LOW)
            along = second * (pull_two[:, cols] * valid)
            d_projected_ref[span, cols] = (upstream * (gain_two[:, cols] * valid) - along).astype(LOW)
        store_halves(sampled_ref, d_projected_ref[:, cols], proj_low_ref, proj_high_ref, cols)
        store_halves(hidden_ref, d_expanded_ref[:, cols], expand_low_ref, expand_high_ref, cols)


def store_halves(turned_ref, grads, low_ref, high_ref, cols):
    half, rows, _ = low_ref.shape
    for at, ref in ((0, low_ref), (half, high_ref)):
        left = turned_ref[at : at + half].reshape(half * rows, turned_ref.shape[2])
        ref[:, :, cols] = dot(left, grads).astype(LOW).reshape(half, rows, grads.shape[1])


def back_two_kernel(
    size, dims, scalar_ref, d_ref, w_ref, grouped_ref, sums_two_ref, base_two_ref, affine_ref, out_ref, sums_ref, first_ref
):
    rows, width = out_ref.shape
    images, tall, half_cols = dims
    mean, inv = moments_of(sums_two_ref[...], base_two_ref[...], scalar_ref[1])
    out_ref[...] = dot_nt(d_ref[...], w_ref[...])
    totals = [jnp.zeros((8, width), WIDE) for _ in range(2)]
    scale = 0.5 * affine_ref[0:1, :] * inv
    shift = 0.5 * affine_ref[1:2, :]
    for span in spans(rows, size):
        gap = grouped_ref[span, :] - mean
        _, slope = silu_pair(gap * scale + shift)
        grad = (out_ref[span, :] * 0.5) * slope
        out_ref[span, :] = grad
        totals[0] += fold(grad)
        totals[1] += fold(grad * gap)
    sums_ref[0:1, :] = close(totals[0])
    sums_ref[1:2, :] = close(totals[1]) * inv
    for image in range(images):
        at = image * tall * half_cols
        first_ref[image * half_cols : (image + 1) * half_cols, :] = out_ref[at : at + half_cols, :].astype(LOW)


def side_kernel(d_ref, w_ref, out_ref):
    out_ref[...] = dot_nt(d_ref[...], w_ref[...])


def norm_back_values(grad, values, mean, pull, valid):
    gain, offset, along = pull
    return (grad - offset) * (gain * valid) - (values - mean) * (along * valid)


def norm_pull(gain, inv, sums, count):
    return gain * inv, sums[0:1, :] / count, gain * inv * inv * (sums[1:2, :] / count)


def conv_back_kernel(
    dims,
    scalar_ref,
    own_ref,
    valid_ref,
    grad_ref,
    grouped_ref,
    below_grad_ref,
    below_grouped_ref,
    sums_two_ref,
    base_two_ref,
    affine_two_ref,
    grads_two_ref,
    reduced_ref,
    edge_ref,
    moments_one_ref,
    affine_one_ref,
    group_ref,
    out_ref,
    sums_ref,
    grad_group_ref,
    *buffers,
):
    images, tall, half_cols = dims
    quarter = tall * half_cols
    plane_rows = images * quarter
    width = reduced_ref.shape[1]
    even, odd, below = buffers[:3], buffers[3:6], buffers[6:8]
    count_in, count_out = scalar_ref[0], scalar_ref[1]

    mean, inv = moments_of(sums_two_ref[...], base_two_ref[...], count_out)
    pull = norm_pull(affine_two_ref[0:1, :], inv, grads_two_ref[...], count_out)
    for image in range(images):
        at = slice(image * quarter, (image + 1) * quarter)
        values = norm_back_values(grad_ref[at, :], grouped_ref[at, :], mean, pull, valid_ref[image])
        below[0][image, :tall, :, :] = values.astype(LOW).reshape(tall, half_cols, width)
        below[1][image, :tall, :, :] = (
            shift_columns(values, half_cols, -1).astype(LOW).reshape(tall, half_cols, width)
        )
        at = slice(image * half_cols, (image + 1) * half_cols)
        values = norm_back_values(
            below_grad_ref[at, :].astype(WIDE),
            below_grouped_ref[at, :].astype(WIDE),
            mean,
            pull,
            valid_ref[image] * scalar_ref[3],
        )
        below[0][image, tall, :, :] = values.astype(LOW)
        below[1][image, tall, :, :] = shift_columns(values, half_cols, -1).astype(LOW)

    def part(ref, at):
        return ref[:, at : at + tall, :, :].reshape(plane_rows, width)

    mask = group_mask(width)
    half_mask = mask * jnp.asarray(0.5, LOW)
    weights = [block_weights(group_ref, half_mask, tap) for tap in range(TAPS * TAPS)]
    here, left = part(below[0], 0), part(below[1], 0)
    next_here, next_left = part(below[0], 1), part(below[1], 1)
    terms = (
        [(here, 4)],
        [(here, 5), (left, 3)],
        [(here, 7), (next_here, 1)],
        [(here, 8), (left, 6), (next_here, 2), (next_left, 0)],
    )

    turned = here.T
    picked = jnp.bitwise_xor(iota((GW, 1), 0), own_ref[0])
    _, channel = over(iota((1, width), 1), GW)
    one_hot = (channel == picked).astype(WIDE).astype(LOW)
    mean_one = moments_one_ref[0:1, :]
    inv_one = lax.rsqrt(moments_one_ref[1:2, :] / count_in + EPS)
    scale = 0.5 * affine_one_ref[0:1, :] * inv_one
    shift = 0.5 * affine_one_ref[1:2, :]
    totals = [jnp.zeros((8, width), WIDE) for _ in range(2)]
    half = edge_ref.shape[0] // 2
    edge = edge_ref[...].astype(WIDE)
    for plane in range(4):
        base = plane * plane_rows
        total = None
        for grads, tap in terms[plane]:
            term = dot_nt(grads, weights[tap])
            total = term if total is None else total + term
        out_ref[base : base + plane_rows, :] = total

        def get(image):
            start = base + image * quarter
            parts = []
            for span in spans(quarter, 32):
                at = slice(start + span.start, start + span.stop)
                gap = reduced_ref[at, :] - mean_one
                value, slope = silu_pair(gap * scale + shift)
                grad = out_ref[at, :] * slope
                out_ref[at, :] = grad
                totals[0] += fold(grad)
                totals[1] += fold(grad * gap)
                parts.append(value)
            return jnp.concatenate(parts, axis=0)

        halo = (None, None, edge[:half], edge[half:])[plane]
        store_plane(dims, plane, get, halo, even, odd)
        for tap, window in plane_windows(plane, even, odd):
            full = dot(turned, window).astype(LOW) * mask
            grad_group_ref[tap] = dot_nt(one_hot, full).astype(LOW)
    sums_ref[0:1, :] = close(totals[0])
    sums_ref[1:2, :] = close(totals[1]) * inv_one


def reduced_back_kernel(
    size,
    scalar_ref,
    valid_ref,
    grad_ref,
    reduced_ref,
    moments_ref,
    affine_ref,
    sums_ref,
    *refs,
):
    planes_refs, (d_ref, low_ref, high_ref) = refs[:4], refs[4:]
    rows, width = d_ref.shape
    images = valid_ref.shape[0]
    quarter = rows // (4 * images)
    mean = moments_ref[0:1, :]
    inv = lax.rsqrt(moments_ref[1:2, :] / scalar_ref[0] + EPS)
    pull = norm_pull(affine_ref[0:1, :], inv, sums_ref[...], scalar_ref[0])
    for span in spans(rows, size):
        valid = valid_ref[span.start // quarter % images]
        d_ref[span, :] = norm_back_values(grad_ref[span, :], reduced_ref[span, :], mean, pull, valid).astype(LOW)
    half = low_ref.shape[0]
    for at, ref in ((0, low_ref), (half, high_ref)):
        total = None
        for plane, planes_ref in enumerate(planes_refs):
            deep = planes_ref.shape[2]
            left = planes_ref[at : at + half].reshape(half * planes_ref.shape[1], deep)
            term = dot(left, d_ref[plane * deep : (plane + 1) * deep, :])
            total = term if total is None else total + term
        ref[...] = total.astype(LOW).reshape(ref.shape)


def images_back_kernel(dims, d_ref, w_ref, side_ref, *refs):
    out_ref, order_ref = refs[-2:]
    image_rows, cols = dims
    pixels = image_rows * cols
    quarter = pixels // 4

    @pl.when(pl.program_id(0) == 0)
    def _():
        order_ref[...] = parity_order(image_rows, cols, 1)

    values = dot_nt(d_ref[...].reshape(pixels, d_ref.shape[-1]), w_ref[...])
    first = values[:quarter] + side_ref[...]
    planes = jnp.concatenate([first, values[quarter:]], axis=0).astype(LOW)
    out_ref[...] = dot(order_ref[...], planes).astype(LOW)


def whole(shape):
    return pl.BlockSpec(shape, lambda i: (0,) * len(shape))


def wide_cols(rows, width):
    return pl.BlockSpec((rows, width), lambda i: (0, i))


SCALARS = pl.BlockSpec(memory_space=pltpu.SMEM)


def place(shape, kind):
    if math.prod(shape) * jnp.dtype(kind).itemsize >= 4 << 20:
        return pltpu.HBM(shape, kind)
    return jax.ShapeDtypeStruct(shape, kind)


def call(kernel, grid, in_specs, out_specs, out_shapes, cost, scratch=()):
    flops, moved = cost
    return pl.pallas_call(
        kernel,
        grid=(grid,),
        in_specs=in_specs,
        out_specs=out_specs,
        out_shape=[place(shape, kind) for shape, kind in out_shapes],
        scratch_shapes=list(scratch),
        compiler_params=pltpu.CompilerParams(vmem_limit_bytes=VMEM_LIMIT),
        cost_estimate=pl.CostEstimate(flops=flops, bytes_accessed=moved, transcendentals=0),
    )


def hbm(value):
    return pltpu.with_memory_space_constraint(value, pltpu.HBM)


def per_device(
    images_in,
    reduce_w,
    gain_one,
    shift_one,
    group_w,
    gain_two,
    shift_two,
    expand_w,
    gain_three,
    shift_three,
    proj_w,
    gain_proj,
    shift_proj,
    valid_mask,
    cotangent,
):
    images, image_rows, cols, chans = images_in.shape
    mid = reduce_w.shape[1]
    wide = expand_w.shape[1]
    tall, half_cols = image_rows // 2, cols // 2
    quarter = tall * half_cols
    rows = images * quarter
    pixels = images * image_rows * cols
    block = 256
    steps = mid // block
    strip = 1024
    strips = wide // strip

    valid = valid_mask.astype(WIDE)
    row_index = lax.axis_index("ha")
    has_upper = (row_index > 0).astype(WIDE)
    has_lower = (row_index < lax.axis_size("ha") - 1).astype(WIDE)
    plain = ([CORE], [SIDE_ONE], [SIDE_TWO], [DEEP_ONE, DEEP_TWO])
    swapped = ([CORE], [SIDE_TWO], [SIDE_ONE], [DEEP_ONE, DEEP_TWO])
    short = ([CORE], [SIDE_TWO, SIDE_ONE], [DEEP_ONE, DEEP_TWO])
    own_one, own_two = own_part(plain).reshape(1), own_part(swapped).reshape(1)
    affine_one = jnp.stack([gain_one, shift_one])
    affine_two = jnp.stack([gain_two, shift_two])
    affine_out = jnp.stack([gain_three, shift_three, gain_proj, shift_proj])
    taps = TAPS * TAPS * GW
    group_flat = group_w.reshape(taps, mid)
    rounds = sum_plan(("ba", "ha"))
    back_rounds = sum_plan(("ha", "ba"))

    halo_images = shifted(images_in[:, -1], "ha", 1).reshape(images * cols, chans)
    lead = images // 4
    planes, reduced, stats, sampled = call(
        functools.partial(reduce_kernel, (images, image_rows, cols), lead),
        lead + steps,
        [
            SCALARS,
            pl.BlockSpec((pixels // lead, chans), lambda i: (jnp.minimum(i, lead - 1), 0)),
            pl.BlockSpec((chans, block), lambda i: (0, jnp.maximum(i - lead, 0))),
        ],
        [
            pl.BlockSpec((4, images // lead, quarter, chans), lambda i: (0, jnp.minimum(i, lead - 1), 0, 0)),
            pl.BlockSpec((pixels, block), lambda i: (0, jnp.maximum(i - lead, 0))),
            pl.BlockSpec((3, block), lambda i: (0, jnp.maximum(i - lead, 0))),
            whole((1, chans)),
        ],
        [((4, images, quarter, chans), LOW), ((pixels, mid), WIDE), ((3, mid), WIDE), ((1, chans), WIDE)],
        (2 * pixels * chans * (mid + 256), 20 << 20),
        [pltpu.VMEM((pixels, chans), LOW), pltpu.VMEM((image_rows * cols, image_rows * cols), LOW)],
    )(valid, hbm(images_in.reshape(pixels, chans)), hbm(reduce_w))
    planes = planes.reshape(pixels, chans)
    stats, halo_images = tie(jnp.concatenate([stats, sampled]), halo_images)
    stats = mesh_moments(stats, rounds)

    def turn(value, at, own):
        width = value.shape[1]
        return call(
            turn_kernel,
            1,
            [SCALARS, pl.BlockSpec((rows, width), lambda i: (at or 0, 0))],
            [whole((PARTS, width // PARTS, rows))],
            [((PARTS, width // PARTS, rows), LOW)],
            (0, 2 << 20),
        )(own, value if at is None else hbm(value))[0]

    sampled_turned = turn(planes, 0, own_two)
    stats, sampled_turned = tie(stats, sampled_turned)
    count_in, moments_one, sampled_mean = stats[0, 0], stats[1:3], stats[3:4]
    scalars = jnp.stack([count_in, count_in / 4.0, has_upper, has_lower])

    grouped, sums, base_two, first_row, edge = call(
        functools.partial(conv_kernel, (images, tall, half_cols)),
        steps,
        [
            SCALARS,
            SCALARS,
            wide_cols(pixels, block),
            wide_cols(2, block),
            wide_cols(2, block),
            whole((images * cols, chans)),
            wide_cols(chans, block),
            wide_cols(taps, block),
        ],
        [
            wide_cols(rows, block),
            wide_cols(2, block),
            wide_cols(1, block),
            wide_cols(images * half_cols, block),
            wide_cols(images * cols, block),
        ],
        [
            ((rows, mid), WIDE),
            ((2, mid), WIDE),
            ((1, mid), WIDE),
            ((images * half_cols, mid), LOW),
            ((images * cols, mid), LOW),
        ],
        (2 * rows * mid * 9 * 256, 14 << 20),
        [pltpu.VMEM((images * cols, chans), LOW)] + window_scratch(images, tall, half_cols, block),
    )(scalars, valid, hbm(reduced), moments_one, affine_one, halo_images, hbm(reduce_w), group_flat)
    sums_two = mesh_sum(sums, rounds)
    below_grouped = shifted(first_row, "ha", -1)
    sums_two, below_grouped = tie(sums_two, below_grouped)
    projected, side = call(
        functools.partial(project_kernel, quarter),
        strips,
        [SCALARS, whole((rows, chans)), wide_cols(chans, strip), whole((1, chans))],
        [wide_cols(rows, strip), wide_cols(3, strip)],
        [((rows, wide), WIDE), ((3, wide), WIDE)],
        (2 * rows * chans * wide, 10 << 20),
    )(valid, hbm(planes), proj_w, sampled_mean)

    hidden_two, expanded, sums, base_out = call(
        functools.partial(expand_kernel, quarter),
        strips,
        [
            SCALARS,
            SCALARS,
            whole((rows, mid)),
            whole((2, mid)),
            whole((1, mid)),
            whole((2, mid)),
            wide_cols(mid, strip),
            wide_cols(3, strip),
        ],
        [whole((rows, mid)), wide_cols(rows, strip), wide_cols(4, strip), wide_cols(2, strip)],
        [((rows, mid), LOW), ((rows, wide), WIDE), ((4, wide), WIDE), ((2, wide), WIDE)],
        (2 * rows * mid * wide, 12 << 20),
    )(scalars, valid, grouped, sums_two, base_two, affine_two, expand_w, side)
    stats_out = mesh_sum(sums, rounds)
    stats_out, hidden_turned = tie(stats_out, turn(hidden_two, None, own_one))

    cot = cotangent.reshape(rows, wide)
    output, sums = call(
        functools.partial(output_kernel, 16),
        strips,
        [
            SCALARS,
            SCALARS,
            wide_cols(rows, strip),
            wide_cols(rows, strip),
            wide_cols(4, strip),
            wide_cols(2, strip),
            wide_cols(4, strip),
            wide_cols(rows, strip),
        ],
        [wide_cols(rows, strip), wide_cols(3, strip)],
        [((rows, wide), LOW), ((3, wide), WIDE)],
        (20 * rows * wide, 12 << 20),
    )(scalars, valid, hbm(expanded), hbm(projected), stats_out, base_out, affine_out, cot)
    sums_out = mesh_sum(sums, rounds)

    def halves_specs(height, width):
        return [pl.BlockSpec((PARTS // 2, height // PARTS, width), lambda i: (0, 0, i))] * 2

    def halves_shapes(height, width):
        return [((PARTS // 2, height // PARTS, width), LOW)] * 2

    d_expanded, d_projected, *halves = call(
        functools.partial(weights_kernel, 16),
        strips,
        [
            SCALARS,
            SCALARS,
            wide_cols(rows, strip),
            wide_cols(rows, strip),
            wide_cols(4, strip),
            wide_cols(2, strip),
            wide_cols(4, strip),
            wide_cols(3, strip),
            wide_cols(rows, strip),
            whole((PARTS, mid // PARTS, rows)),
            whole((PARTS, chans // PARTS, rows)),
        ],
        [wide_cols(rows, strip), wide_cols(rows, strip)] + halves_specs(mid, strip) + halves_specs(chans, strip),
        [((rows, wide), LOW), ((rows, wide), LOW)] + halves_shapes(mid, wide) + halves_shapes(chans, wide),
        (4 * rows * mid * wide, 24 << 20),
    )(
        scalars,
        valid,
        hbm(expanded),
        hbm(projected),
        stats_out,
        base_out,
        affine_out,
        sums_out,
        cot,
        hidden_turned,
        sampled_turned,
    )
    expand_sum = Gradient(halves[:2], plain, plain[:3] + ([DEEP_ONE], [DEEP_TWO]))
    proj_sum = Gradient(halves[2:], swapped, swapped[:3] + ([DEEP_ONE], [DEEP_TWO]))
    pair = [expand_sum, proj_sum]
    for grad in pair:
        grad.send()

    grad_two, sums, first_row = call(
        functools.partial(back_two_kernel, 16, (images, tall, half_cols)),
        steps,
        [
            SCALARS,
            whole((rows, wide)),
            pl.BlockSpec((block, wide), lambda i: (i, 0)),
            wide_cols(rows, block),
            wide_cols(2, block),
            wide_cols(1, block),
            wide_cols(2, block),
        ],
        [wide_cols(rows, block), wide_cols(2, block), wide_cols(images * half_cols, block)],
        [((rows, mid), WIDE), ((2, mid), WIDE), ((images * half_cols, mid), LOW)],
        (2 * rows * mid * wide, 10 << 20),
    )(scalars, d_expanded, expand_w, grouped, sums_two, base_two, affine_two)
    sums = mesh_sum(sums, back_rounds[:1])
    sums, first_row = arrive(pair, sums, first_row)
    below_grad = shifted(first_row, "ha", -1)
    sums = mesh_sum(sums, back_rounds[1:2])
    side_grad = call(
        side_kernel,
        1,
        [whole((rows, wide)), whole((chans, wide))],
        [whole((rows, chans))],
        [((rows, chans), WIDE)],
        (2 * rows * chans * wide, 8 << 20),
    )(d_projected, proj_w)[0]
    planes_turned = [sampled_turned, turn(planes, 1, own_two)]
    sums, below_grad, side_grad, *planes_turned = arrive(pair, sums, below_grad, side_grad, *planes_turned)
    for grad in pair:
        grad.step()
    grads_two = mesh_sum(sums, back_rounds[2:])
    deep = pltpu.VMEM((images, tall + 1, half_cols, block), LOW)
    grads_two, side_grad = tie(grads_two, side_grad)
    grad_one, sums, parts_group = call(
        functools.partial(conv_back_kernel, (images, tall, half_cols)),
        steps,
        [
            SCALARS,
            SCALARS,
            SCALARS,
            wide_cols(rows, block),
            wide_cols(rows, block),
            wide_cols(images * half_cols, block),
            wide_cols(images * half_cols, block),
            wide_cols(2, block),
            wide_cols(1, block),
            wide_cols(2, block),
            wide_cols(2, block),
            wide_cols(pixels, block),
            wide_cols(images * cols, block),
            wide_cols(2, block),
            wide_cols(2, block),
            wide_cols(taps, block),
        ],
        [wide_cols(pixels, block), wide_cols(2, block), pl.BlockSpec((TAPS * TAPS, GW, block), lambda i: (0, 0, i))],
        [((pixels, mid), WIDE), ((2, mid), WIDE), ((TAPS * TAPS, GW, mid), LOW)],
        (4 * rows * mid * 9 * 256, 24 << 20),
        window_scratch(images, tall, half_cols, block) + [deep, deep],
    )(
        scalars,
        own_two,
        valid,
        grad_two,
        grouped,
        below_grad,
        below_grouped,
        sums_two,
        base_two,
        affine_two,
        grads_two,
        hbm(reduced),
        edge,
        moments_one,
        affine_one,
        group_flat,
    )
    parts_group = jnp.pad(jnp.transpose(parts_group, (1, 0, 2)), ((0, 0), (0, 16 - TAPS * TAPS), (0, 0)))
    (sums,) = arrive(pair, sums)
    sums = mesh_sum(sums, back_rounds[:1])
    (sums,) = arrive(pair, sums)
    for grad in pair:
        grad.step()
    grads_one = mesh_sum(sums, back_rounds[1:])
    planes_turned += [turn(planes, plane, own_two) for plane in (2, 3)]
    grads_one, parts_group, *planes_turned = arrive(pair, grads_one, parts_group, *planes_turned)
    for grad in pair:
        grad.take()
    both = join(pair)
    both.send()

    d_reduced, *halves = call(
        functools.partial(reduced_back_kernel, 16),
        steps,
        [
            SCALARS,
            SCALARS,
            wide_cols(pixels, block),
            wide_cols(pixels, block),
            wide_cols(2, block),
            wide_cols(2, block),
            wide_cols(2, block),
        ]
        + [whole((PARTS, chans // PARTS, rows))] * 4,
        [wide_cols(pixels, block)] + halves_specs(chans, block),
        [((pixels, mid), LOW)] + halves_shapes(chans, mid),
        (2 * pixels * mid * chans, 26 << 20),
    )(scalars, valid, hbm(grad_one), hbm(reduced), moments_one, affine_one, grads_one, *planes_turned)
    d_reduced, *halves = arrive([both], d_reduced, *halves)
    parts_group = [parts_group[: PARTS // 2], parts_group[PARTS // 2 :]]
    halves = [jnp.concatenate(members, axis=1) for members in zip(halves, parts_group)]
    reduce_sum = Gradient(halves, short)
    reduce_sum.send()

    def images_back(d_part, side_part):
        return call(
            functools.partial(images_back_kernel, (image_rows, cols)),
            images,
            [
                pl.BlockSpec((4, None, quarter, mid), lambda i: (0, i, 0, 0)),
                whole((chans, mid)),
                pl.BlockSpec((quarter, chans), lambda i: (i, 0)),
            ],
            [pl.BlockSpec((None, image_rows * cols, chans), lambda i: (i, 0, 0))],
            [((images, image_rows * cols, chans), LOW)],
            (2 * pixels * mid * chans, 16 << 20),
            [pltpu.VMEM((image_rows * cols, image_rows * cols), LOW)],
        )(d_part, reduce_w, side_part)[0]

    everyone = pair + [reduce_sum]
    both.step()
    arrive([reduce_sum])
    reduce_sum.step()
    both.got[0], *reduce_sum.got[:2] = tie(both.got[0], *reduce_sum.got[:2])
    both.step()
    arrive([both, reduce_sum])
    both.take()
    part_again(both, pair)
    for grad in pair:
        grad.send()
    reduce_sum.step()
    (d_reduced,) = arrive(everyone, d_reduced)
    for grad in everyone:
        grad.step()
    d_reduced = d_reduced.reshape(4, images, quarter, mid)
    grad_images = images_back(d_reduced, side_grad)
    (grad_images,) = arrive(everyone, grad_images)
    for grad in everyone:
        grad.step()
    done = []
    for grad, width in zip(pair, (mid, chans)):
        if done:
            done[0] = arrive([grad], done[0])[0]
        grad.take()
        done += grad.finish(width // PARTS)
    grad_expand, grad_proj = done
    (grad_proj,) = arrive([reduce_sum], grad_proj)
    reduce_sum.step()
    reduce_sum.take()
    grad_reduce, grad_group = reduce_sum.finish(chans // PARTS, TAPS * TAPS)
    return (
        output.reshape(cotangent.shape),
        grad_images.reshape(images_in.shape),
        grad_reduce.reshape(reduce_w.shape),
        grads_one[1],
        grads_one[0],
        grad_group.reshape(group_w.shape),
        grads_two[1],
        grads_two[0],
        grad_expand.reshape(expand_w.shape),
        sums_out[1],
        sums_out[0],
        grad_proj.reshape(proj_w.shape),
        sums_out[2],
        sums_out[0],
    )


def solution(mesh):
    split = P("ba", "ha", None, None)
    rest = (P(),) * 12
    return jax.shard_map(
        per_device,
        mesh=mesh,
        in_specs=(split,) + rest + (P("ba"), split),
        out_specs=(split, split) + rest,
        check_vma=False,
    )
```
